32 devices in a mesh: dp: 4 (over z), ctx: 4 (over y, core), tensor: 2 (over x).
Axes of the slice: x: 2, y: 2, z: 4, core: 2. Of those that a mesh axis runs over, the one named last changes fastest.
Arguments:
- hidden_in: bfloat16 [4, 1024, 2048], P('dp', 'ctx'), may hold values from -6 to 6
- attn_norm_gain: float32 [2048], replicated, may hold values from 0.5 to 1.5
- attn_norm_bias: float32 [2048], replicated, may hold values from -2 to 2
- qkv_weight: bfloat16 [2048, 6144], P(None, 'tensor'), may hold values from -0.125 to 0.125
- qkv_bias: float32 [6144], P('tensor'), may hold values from -1.2 to 1.2
- dense_weight: bfloat16 [2048, 2048], P('tensor'), may hold values from -2 to 2
- dense_bias: float32 [2048], replicated, may hold values from -3 to 3
- mlp_norm_gain: float32 [2048], replicated, may hold values from 0.5 to 1.5
- mlp_norm_bias: float32 [2048], replicated, may hold values from -2 to 2
- up_weight: bfloat16 [2048, 8192], P(None, 'tensor'), may hold values from -0.125 to 0.125
- up_bias: float32 [8192], P('tensor'), may hold values from -3 to 3
- down_weight: bfloat16 [8192, 2048], P('tensor'), may hold values from -0.0625 to 0.0625
- down_bias: float32 [2048], replicated, may hold values from -3 to 3
- out_cotangent: bfloat16 [4, 1024, 2048], P('dp', 'ctx'), may hold values from -6 to 6
- subset_ids: int32 [4, 1024], P('dp', 'ctx'), may hold values from 0 to 21
- subset_weights: float32 [22], replicated, may hold values from 0.5 to 2
Outputs:
- layer_out: bfloat16 [4, 1024, 2048], P('dp', 'ctx')
- input_grad: bfloat16 [4, 1024, 2048], P('dp', 'ctx')
- grad_attn_norm_gain: float32 [2048], replicated
- grad_attn_norm_bias: float32 [2048], replicated
- grad_qkv_weight: float32 [2048, 6144], P(('dp', 'ctx'), 'tensor')
- grad_qkv_bias: float32 [6144], P('tensor')
- grad_dense_weight: float32 [2048, 2048], P('tensor', ('dp', 'ctx'))
- grad_dense_bias: float32 [2048], replicated
- grad_mlp_norm_gain: float32 [2048], replicated
- grad_mlp_norm_bias: float32 [2048], replicated
- grad_up_weight: float32 [2048, 8192], P(('dp', 'ctx'), 'tensor')
- grad_up_bias: float32 [8192], P('tensor')
- grad_down_weight: float32 [8192, 2048], P('tensor', ('dp', 'ctx'))
- grad_down_bias: float32 [2048], replicated
The draws below stay inside these ranges and needn't reach their ends.
Inputs may be any that keep to these rules, and one draw needn't show every extreme that they name: `subset_ids`: the corpus subset of every token, one of 22.
All inputs are finite; a program needn't handle non-finite values.
Results may differ from the reference program's by a relative error of at most 0.012.
Values may be sent and summed in bfloat16 or wider, within the bound.
A program may use at most 256 MiB of HBM per device.

```python
import math
import jax
import jax.numpy as jnp
import numpy as np
from jax import lax

D = 2048
H = 8
HS = 256
FF = 8192
ROT = 64
SUBSETS = 22
LEN = 1024
SEQS = 4


def touch_ends(array, rng, smallest, top_value):
    place = [jax.random.randint(jax.random.fold_in(rng, axis), (), 0, length) for axis, length in enumerate(array.shape)]
    main_axis = array.shape.index(max(array.shape))
    next_to = place[:main_axis] + [(place[main_axis] + 1) % array.shape[main_axis]] + place[main_axis + 1:]
    return array.at[tuple(place)].set(smallest).at[tuple(next_to)].set(top_value)


def levels(key, shape, pieces, smallest, high):
    factor_of, own = 1.0, jax.random.fold_in(key, 6)
    for dim, shards_of in pieces:
        heights = jnp.exp(jax.random.uniform(jax.random.fold_in(own, dim), (shards_of,), jnp.float32, smallest / len(pieces), high / len(pieces)))
        factor_of = factor_of * jnp.repeat(heights, shape[dim] // shards_of).reshape([-1 if axis == dim else 1 for axis in range(len(shape))])
    return factor_of


def cumulative_ranks(count, lean):
    portions = [(1 << 20) // math.isqrt(grade ** lean) + 1 for grade in range(1, count + 1)]
    scale = 1 + sum(portions) // (1 << 30)
    return np.cumsum(np.array([max(1, weight // scale) for weight in portions]))


def skewed_ids(own_key, shape, count, skew):
    table = cumulative_ranks(count, skew)
    lot = jax.random.randint(jax.random.fold_in(own_key, 1), shape, 0, int(table[count - 1]))
    rank = jnp.searchsorted(jnp.asarray(table, jnp.int32), lot, side="right")
    return jax.random.permutation(jax.random.fold_in(own_key, 2), count)[rank].astype(jnp.int32)


def bell_draw(stream_key, dims, width, most, cuts=(), kind=jnp.bfloat16):
    entries = jax.random.normal(stream_key, dims, jnp.float32) * width
    if len(cuts) > 0:
        entries = levels(stream_key, dims, cuts, -0.22, 0.18) * entries
    return jnp.clip(entries, min=-most, max=most).astype(kind)


def setup_inputs(seed: int = 0) -> dict:
    key_list = jax.random.split(jax.random.key(seed), 17)
    return {
        "hidden_in": bell_draw(key_list[0], (SEQS, LEN, D), 1.0, 6.0, ((0, 4), (1, 4))),
        "attn_norm_gain": jnp.clip(1.0 + 0.1 * jax.random.normal(key_list[1], (D,), jnp.float32), 0.5, 1.5),
        "attn_norm_bias": bell_draw(key_list[2], (D,), 0.3, 2.0, (), jnp.float32),
        "qkv_weight": bell_draw(key_list[3], (D, H * 3 * HS), D ** -0.5, 0.125, ((1, 2),)),
        "qkv_bias": bell_draw(key_list[4], (H * 3 * HS,), 0.2, 1.2, ((0, 2),), jnp.float32),
        "dense_weight": bell_draw(key_list[5], (H * HS, D), (max(H * HS // 256, 1)) ** -0.5, 2.0, ((0, 2),)),
        "dense_bias": bell_draw(key_list[6], (D,), 0.5, 3.0, (), jnp.float32),
        "mlp_norm_gain": jnp.clip(1.0 + 0.1 * jax.random.normal(key_list[7], (D,), jnp.float32), 0.5, 1.5),
        "mlp_norm_bias": bell_draw(key_list[8], (D,), 0.3, 2.0, (), jnp.float32),
        "up_weight": bell_draw(key_list[9], (D, FF), D ** -0.5, 0.125, ((1, 2),)),
        "up_bias": bell_draw(key_list[10], (FF,), 0.5, 3.0, ((0, 2),), jnp.float32),
        "down_weight": bell_draw(key_list[11], (FF, D), FF ** -0.5, 0.0625, ((0, 2),)),
        "down_bias": bell_draw(key_list[12], (D,), 0.5, 3.0, (), jnp.float32),
        "out_cotangent": bell_draw(key_list[13], (SEQS, LEN, D), 1.0, 6.0, ((0, 4), (1, 4))),
        "subset_ids": touch_ends(skewed_ids(key_list[14], (SEQS, LEN), SUBSETS, 2), jax.random.fold_in(key_list[14], 3), 0, SUBSETS - 1).astype(jnp.int32),
        "subset_weights": jnp.clip(jnp.exp(jax.random.uniform(key_list[15], (SUBSETS,), jnp.float32, math.log(0.5), math.log(2.0))), 0.5, 2.0),
    }


@jax.custom_vjp
def low(v):
    return lax.optimization_barrier(v.astype(jnp.bfloat16)).astype(jnp.float32)

@jax.custom_vjp
def low_back(v):
    return v

def low_keep(v):
    return (low(v), None)

def low_pass(kept, grad):
    return (grad,)

def back_keep(v):
    return (v, None)

def back_low(kept, grad):
    return (low(grad),)
low.defvjp(low_keep, low_pass)
low_back.defvjp(back_keep, back_low)
NORM_EPS = 1e-05

def rope_tables(positions, rot_dims):
    half_dims = rot_dims // 2
    freqs = 10000.0 ** (-(jnp.arange(half_dims, dtype=jnp.float32) * 2.0 / rot_dims))
    angles = positions.astype(jnp.float32)[:, None] * freqs[None, :]
    return (jnp.concatenate([jnp.cos(angles), jnp.cos(angles)], -1), jnp.concatenate([jnp.sin(angles), jnp.sin(angles)], -1))

def rotate(columns, cosine_table, sine_table):
    half_dims = ROT // 2
    leading = columns[..., :ROT]
    turned = jnp.concatenate([-leading[..., half_dims:], leading[..., :half_dims]], -1)
    moved = leading * cosine_table[:, None, :] + turned * sine_table[:, None, :]
    return jnp.concatenate([moved, columns[..., ROT:]], -1)

def block_layer(seq_in, params):
    attn_gain, attn_shift, qkv_mat, qkv_add, dense_mat, dense_add, mlp_gain, mlp_shift, up_mat, up_add, down_mat, down_add = params
    row_mean = lax.optimization_barrier(jnp.mean(seq_in, -1, keepdims=True))
    centered = seq_in - row_mean
    inv_std = lax.rsqrt(lax.optimization_barrier(jnp.mean(centered * centered, -1, keepdims=True)) + NORM_EPS)
    normed = centered * inv_std
    attn_in = low(normed * attn_gain + attn_shift)
    mlp_in = low(normed * mlp_gain + mlp_shift)
    qkv_all = low_back(jnp.dot(attn_in, qkv_mat, precision=lax.Precision.HIGHEST) + qkv_add)
    qkv_all = qkv_all.reshape(LEN, H, 3, HS)
    positions = jnp.arange(LEN, dtype=jnp.int32)
    cosine_table, sine_table = rope_tables(positions, ROT)
    query_rows = low(rotate(qkv_all[:, :, 0], cosine_table, sine_table))
    key_rows = low(rotate(qkv_all[:, :, 1], cosine_table, sine_table))
    value_rows = low(qkv_all[:, :, 2])
    causal = positions[None, :] <= positions[:, None]
    score_scale = HS ** (-0.5)

    def head_attention(operands):
        head_query, head_key, head_value = operands
        scores = low_back(jnp.dot(head_query, head_key.T, precision=lax.Precision.HIGHEST) * score_scale)
        scores = jnp.where(causal, scores, -1e+30)
        row_max = lax.optimization_barrier(jnp.max(scores, -1, keepdims=True))
        expd = jnp.exp(scores - row_max)
        prob = low(expd / lax.optimization_barrier(jnp.sum(expd, -1, keepdims=True)))
        return jnp.dot(prob, head_value, precision=lax.Precision.HIGHEST)
    attended = lax.map(jax.checkpoint(head_attention), (jnp.swapaxes(query_rows, 0, 1), jnp.swapaxes(key_rows, 0, 1), jnp.swapaxes(value_rows, 0, 1)))
    attn_out = low(low_back(jnp.swapaxes(attended, 0, 1))).reshape(LEN, H * HS)
    up_pre = low_back(jnp.dot(mlp_in, up_mat, precision=lax.Precision.HIGHEST) + up_add)
    activated = low(jax.nn.gelu(up_pre, approximate=False))
    branch = low_back(jnp.dot(attn_out, dense_mat, precision=lax.Precision.HIGHEST) + jnp.dot(activated, down_mat, precision=lax.Precision.HIGHEST))
    return seq_in + branch + dense_add + down_add

def reference(hidden_in, attn_norm_gain, attn_norm_bias, qkv_weight, qkv_bias, dense_weight, dense_bias, mlp_norm_gain, mlp_norm_bias, up_weight, up_bias, down_weight, down_bias, out_cotangent, subset_ids, subset_weights):
    params = tuple((item.astype(jnp.float32) for item in (attn_norm_gain, attn_norm_bias, qkv_weight, qkv_bias, dense_weight, dense_bias, mlp_norm_gain, mlp_norm_bias, up_weight, up_bias, down_weight, down_bias)))
    inputs = hidden_in.astype(jnp.float32)
    layer_fn = jax.checkpoint(block_layer)

    def forward(all_inputs, all_params):

        def scan_step(scan_carry, seq_in):
            return (scan_carry, layer_fn(seq_in, all_params))
        _, outputs = lax.scan(scan_step, jnp.zeros((), jnp.float32), all_inputs)
        return outputs
    layer_out, pullback = jax.vjp(forward, inputs, params)
    row_weight = subset_weights.astype(jnp.float32)[subset_ids]
    grad_out = out_cotangent.astype(jnp.float32) * row_weight[..., None]
    input_grad, grads = pullback(grad_out)
    return (layer_out.astype(jnp.bfloat16), input_grad.astype(jnp.bfloat16), grads[0], grads[1], grads[2], grads[3], grads[4], grads[5], grads[6], grads[7], grads[8], grads[9], grads[10], grads[11])
```

```python
import math

import jax
import jax.numpy as jnp
from jax import lax
from jax.sharding import PartitionSpec as P

HS = 256
ROT = 64


NORM_EPS = 1e-05


def rope_tables(positions, rot_dims):
    half_dims = rot_dims // 2
    freqs = 10000.0 ** (-(jnp.arange(half_dims, dtype=jnp.float32) * 2.0 / rot_dims))
    angles = positions.astype(jnp.float32)[:, None] * freqs[None, :]
    return (
        jnp.concatenate([jnp.cos(angles), jnp.cos(angles)], -1),
        jnp.concatenate([jnp.sin(angles), jnp.sin(angles)], -1),
    )


def rotate(columns, cosine_table, sine_table):
    half_dims = ROT // 2
    leading = columns[..., :ROT]
    turned = jnp.concatenate([-leading[..., half_dims:], leading[..., :half_dims]], -1)
    moved = leading * cosine_table[:, None, :] + turned * sine_table[:, None, :]
    return jnp.concatenate([moved, columns[..., ROT:]], -1)


def rotate_back(gradient, cosine_table, sine_table):
    half_dims = ROT // 2
    leading = gradient[..., :ROT]
    scaled = leading * sine_table[:, None, :]
    turned = jnp.concatenate([scaled[..., half_dims:], -scaled[..., :half_dims]], -1)
    moved = leading * cosine_table[:, None, :] + turned
    return jnp.concatenate([moved, gradient[..., ROT:]], -1)


def swap(array, axis, bit):
    pairs = [(place, place ^ bit) for place in range(lax.axis_size(axis))]
    return lax.ppermute(array, axis, pairs)


def bits_down(axis):
    size = lax.axis_size(axis)
    return [1 << level for level in reversed(range(size.bit_length() - 1))]


def relative_blocks(array, axis, dim):
    place = lax.axis_index(axis)
    for bit in bits_down(axis):
        size = array.shape[dim]
        halves = array.reshape(
            array.shape[:dim] + (size // (2 * bit), 2, bit) + array.shape[dim + 1 :]
        )
        flipped = jnp.flip(halves, dim + 1)
        array = jnp.where((place & bit) != 0, flipped, halves).reshape(array.shape)
    return array


def gather_rows(rows, axis):
    for bit in bits_down(axis):
        rows = jnp.concatenate([rows, swap(rows, axis, bit)], 0)
    return rows


def exchange_rows(rows, axis):
    for bit in bits_down(axis):
        rows = jnp.concatenate([rows[:, :bit], swap(rows[:, bit:], axis, bit)], 0)
    return rows[:, 0]


def block_order(size):
    order = [0]
    bit = size // 2
    while bit:
        order = order + [entry ^ bit for entry in order]
        bit //= 2
    return order


def tensor_sum(part):
    if lax.axis_size("tensor") == 2:
        low = part.astype(jnp.bfloat16)
        return low.astype(jnp.float32) + swap(low, "tensor", 1).astype(jnp.float32)
    return lax.psum(part, "tensor")


def reduce_line(left, right, spec, dim):
    size = lax.axis_size("dp")
    width = left.shape[1] // size
    arrived = None
    bits = [1 << level for level in range(size.bit_length() - 1)]
    count = size
    total = None
    for bit in bits:
        count //= 2
        if total is None:
            send = jnp.einsum(
                spec, left[:, count * width :], right, preferred_element_type=jnp.float32
            )
            keep = jnp.einsum(
                spec, left[:, : count * width], right, preferred_element_type=jnp.float32
            )
        else:
            keep = lax.slice_in_dim(total, 0, count * width, axis=dim)
            send = lax.slice_in_dim(total, count * width, 2 * count * width, axis=dim)
        arrived = swap(send.astype(jnp.bfloat16), "dp", bit)
        total = keep + arrived.astype(jnp.float32)
    return total


def reduce_blocks(total, axis, dim, bits=None):
    size = lax.axis_size(axis)
    for bit in [1 << level for level in range(size.bit_length() - 1)]:
        half = total.shape[dim] // 2
        keep = lax.slice_in_dim(total, 0, half, axis=dim)
        send = lax.slice_in_dim(total, half, 2 * half, axis=dim)
        arrived = swap(send.astype(jnp.bfloat16), axis, bit)
        total = keep + arrived.astype(jnp.float32)
    return total


def spread_columns(rows):
    dp_size, ctx_size = lax.axis_size("dp"), lax.axis_size("ctx")
    width = rows.shape[1] // (dp_size * ctx_size)
    blocks = rows.reshape(rows.shape[0], dp_size, ctx_size, width)
    blocks = relative_blocks(relative_blocks(blocks, "dp", 1), "ctx", 2)
    blocks = jnp.stack([blocks[:, entry] for entry in block_order(dp_size)], 2)
    return blocks.reshape(rows.shape[0], ctx_size, dp_size * width)


def local(
    hidden_in,
    attn_norm_gain,
    attn_norm_bias,
    qkv_weight,
    qkv_bias,
    dense_weight,
    dense_bias,
    mlp_norm_gain,
    mlp_norm_bias,
    up_weight,
    up_bias,
    down_weight,
    down_bias,
    out_cotangent,
    subset_ids,
    subset_weights,
):
    seq_count, block_len, model_width = hidden_in.shape
    row_count = seq_count * block_len
    head_count = qkv_weight.shape[1] // (3 * HS)
    ctx_size = lax.axis_size("ctx")
    length = block_len * ctx_size
    score_scale = 1.0 / math.sqrt(HS)
    low_type = jnp.bfloat16
    hidden_rows = hidden_in.reshape(row_count, model_width)
    inputs = hidden_rows.astype(jnp.float32)
    row_mean = jnp.mean(inputs, -1, keepdims=True)
    centered = inputs - row_mean
    inv_std = lax.rsqrt(jnp.mean(centered * centered, -1, keepdims=True) + NORM_EPS)
    normed = centered * inv_std
    attn_in = (normed * attn_norm_gain + attn_norm_bias).astype(low_type)
    mlp_in = (normed * mlp_norm_gain + mlp_norm_bias).astype(low_type)

    subset_count = subset_weights.shape[0]
    matches = subset_ids[..., None] == jnp.arange(subset_count, dtype=jnp.int32)
    row_weight = jnp.sum(jnp.where(matches, subset_weights, 0.0), -1).reshape(row_count, 1)
    grad_out = out_cotangent.reshape(row_count, model_width).astype(jnp.float32) * row_weight
    grad_low = grad_out.astype(low_type)
    grad_out_bias = jnp.sum(grad_out, 0)

    low_part = exchange_rows(spread_columns(grad_low), "ctx")
    hidden_part = exchange_rows(spread_columns(hidden_rows), "ctx").astype(jnp.float32)
    stats = gather_rows(jnp.stack([row_mean[:, 0], inv_std[:, 0]])[None], "ctx")
    mean_all = stats[:, 0].reshape(ctx_size * row_count, 1)
    std_all = stats[:, 1].reshape(ctx_size * row_count, 1)
    normed_part = (hidden_part - mean_all) * std_all

    def own_columns(vector):
        return spread_columns(vector[None])[:, 0]

    mlp_part = (
        normed_part * own_columns(mlp_norm_gain) + own_columns(mlp_norm_bias)
    ).astype(low_type)
    attn_part = (
        normed_part * own_columns(attn_norm_gain) + own_columns(attn_norm_bias)
    ).astype(low_type)

    hidden_units = up_weight.shape[1]
    pieces = max(1, hidden_units // 1024)
    span = hidden_units // pieces
    down_grads, up_grads, up_bias_parts = [], [], []
    branch_part, grad_mlp_in = None, None
    for piece in range(pieces):
        cols = slice(piece * span, (piece + 1) * span)
        up_pre = (
            jnp.dot(mlp_in, up_weight[:, cols], preferred_element_type=jnp.float32) + up_bias[cols]
        )
        activated = jax.nn.gelu(up_pre, approximate=False).astype(low_type)
        activated_all = gather_rows(activated, "ctx")
        down_grads.append(reduce_line(low_part, activated_all, "rd,rf->fd", 1))
        grad_act = jnp.einsum(
            "rd,fd->rf", grad_low, down_weight[cols], preferred_element_type=jnp.float32
        )
        gelu_back = jax.vjp(lambda pre_act: jax.nn.gelu(pre_act, approximate=False), up_pre)[1]
        grad_pre = gelu_back(grad_act)[0].astype(low_type)
        grad_pre_all = gather_rows(grad_pre, "ctx")
        up_grads.append(reduce_line(mlp_part, grad_pre_all, "rd,rf->df", 0))
        up_bias_parts.append(jnp.sum(grad_pre.astype(jnp.float32), 0))
        more = jnp.dot(activated, down_weight[cols], preferred_element_type=jnp.float32)
        branch_part = more if branch_part is None else branch_part + more
        more = jnp.einsum(
            "rf,df->rd", grad_pre, up_weight[:, cols], preferred_element_type=jnp.float32
        )
        grad_mlp_in = more if grad_mlp_in is None else grad_mlp_in + more

    qkv_all = jnp.dot(attn_in, qkv_weight, preferred_element_type=jnp.float32) + qkv_bias
    qkv_all = qkv_all.reshape(seq_count, block_len, head_count, 3, HS)
    place = lax.axis_index("ctx")
    steps = jnp.arange(block_len, dtype=jnp.int32)
    positions = place * block_len + steps
    cosine_table, sine_table = rope_tables(positions, ROT)
    query_rows = rotate(qkv_all[:, :, :, 0], cosine_table, sine_table).astype(low_type)
    key_rows = rotate(qkv_all[:, :, :, 1], cosine_table, sine_table).astype(low_type)
    value_rows = qkv_all[:, :, :, 2].astype(low_type)
    pair = jnp.stack([key_rows, value_rows], 0).reshape(2 * seq_count, block_len, head_count * HS)
    whole = gather_rows(jnp.swapaxes(pair, 0, 1), "ctx")
    whole = jnp.swapaxes(whole, 0, 1).reshape(2, seq_count, length, head_count, HS)
    key_whole, value_whole = whole[0], whole[1]
    key_positions = jnp.concatenate(
        [(place ^ entry) * block_len + steps for entry in block_order(ctx_size)]
    )
    causal = key_positions[None, :] <= positions[:, None]
    raw = jnp.einsum("sqhd,skhd->shqk", query_rows, key_whole, preferred_element_type=jnp.float32)
    scores = jnp.where(causal, raw * score_scale, -1e30)
    row_max = jnp.max(scores, -1, keepdims=True)
    expd = jnp.exp(scores - row_max)
    prob = expd / jnp.sum(expd, -1, keepdims=True)
    prob_low = prob.astype(low_type)
    attn_out = jnp.einsum(
        "shqk,skhd->sqhd", prob_low, value_whole, preferred_element_type=jnp.float32
    ).astype(low_type)
    attn_out = attn_out.reshape(row_count, head_count * HS)
    attn_out_all = gather_rows(attn_out, "ctx")
    grad_dense_weight = reduce_line(low_part, attn_out_all, "rd,rf->fd", 1)
    branch_part = branch_part + jnp.dot(
        attn_out, dense_weight, preferred_element_type=jnp.float32
    )
    layer_out = (inputs + tensor_sum(branch_part) + dense_bias + down_bias).astype(low_type)
    layer_out = layer_out.reshape(seq_count, block_len, model_width)

    grad_attn = jnp.einsum("rd,kd->rk", grad_low, dense_weight, preferred_element_type=jnp.float32)
    grad_attn = grad_attn.astype(low_type).reshape(seq_count, block_len, head_count, HS)
    grad_prob = jnp.einsum(
        "sqhd,skhd->shqk", grad_attn, value_whole, preferred_element_type=jnp.float32
    )
    delta = jnp.sum(grad_prob * prob, -1, keepdims=True)
    grad_scores = (prob * (grad_prob - delta)).astype(low_type)
    grad_query = (
        jnp.einsum("shqk,skhd->sqhd", grad_scores, key_whole, preferred_element_type=jnp.float32)
        * score_scale
    )
    grad_key_whole = (
        jnp.einsum("shqk,sqhd->kshd", grad_scores, query_rows, preferred_element_type=jnp.float32)
        * score_scale
    )
    grad_value_whole = jnp.einsum(
        "shqk,sqhd->kshd", prob_low, grad_attn, preferred_element_type=jnp.float32
    )
    grad_pair = jnp.concatenate(
        [
            grad_key_whole.reshape(length, seq_count * head_count * HS),
            grad_value_whole.reshape(length, seq_count * head_count * HS),
        ],
        1,
    )
    grad_pair = reduce_blocks(grad_pair, "ctx", 0)
    grad_pair = grad_pair.reshape(block_len, 2, seq_count, head_count, HS)
    grad_key_rows = jnp.swapaxes(grad_pair[:, 0], 0, 1)
    grad_value_rows = jnp.swapaxes(grad_pair[:, 1], 0, 1)
    grad_qkv = jnp.stack(
        [
            rotate_back(grad_query, cosine_table, sine_table),
            rotate_back(grad_key_rows, cosine_table, sine_table),
            grad_value_rows,
        ],
        3,
    )
    grad_qkv = grad_qkv.reshape(row_count, head_count * 3 * HS).astype(low_type)
    qkv_grads = []
    for head in range(head_count):
        piece = grad_qkv[:, head * 3 * HS : (head + 1) * 3 * HS]
        qkv_grads.append(reduce_line(attn_part, gather_rows(piece, "ctx"), "rd,rc->dc", 0))
    grad_qkv_bias = jnp.sum(grad_qkv.astype(jnp.float32), 0)
    grad_attn_in = jnp.einsum("rc,dc->rd", grad_qkv, qkv_weight, preferred_element_type=jnp.float32)
    norm_parts = jnp.stack(
        [
            jnp.sum(grad_attn_in * normed, 0),
            jnp.sum(grad_attn_in, 0),
            jnp.sum(grad_mlp_in * normed, 0),
            jnp.sum(grad_mlp_in, 0),
        ]
    )
    grad_normed = grad_attn_in * attn_norm_gain + grad_mlp_in * mlp_norm_gain
    input_part = inv_std * (
        grad_normed
        - jnp.mean(grad_normed, -1, keepdims=True)
        - normed * jnp.mean(grad_normed * normed, -1, keepdims=True)
    )
    input_grad = (
        (grad_out + tensor_sum(input_part))
        .astype(low_type)
        .reshape(seq_count, block_len, model_width)
    )
    norm_total = lax.psum(norm_parts, ("dp", "ctx", "tensor"))
    qkv_bias_sum, up_bias_sum, out_bias_sum = lax.psum(
        (grad_qkv_bias, jnp.concatenate(up_bias_parts), grad_out_bias), ("dp", "ctx")
    )
    return (
        layer_out,
        input_grad,
        norm_total[0],
        norm_total[1],
        jnp.concatenate(qkv_grads, 1),
        qkv_bias_sum,
        grad_dense_weight,
        out_bias_sum,
        norm_total[2],
        norm_total[3],
        jnp.concatenate(up_grads, 1),
        up_bias_sum,
        jnp.concatenate(down_grads, 0),
        out_bias_sum,
    )


def solution(mesh):
    return jax.shard_map(
        local,
        mesh=mesh,
        in_specs=(
            P("dp", "ctx", None),
            P(),
            P(),
            P(None, "tensor"),
            P("tensor"),
            P("tensor", None),
            P(),
            P(),
            P(),
            P(None, "tensor"),
            P("tensor"),
            P("tensor", None),
            P(),
            P("dp", "ctx", None),
            P("dp", "ctx"),
            P(),
        ),
        out_specs=(
            P("dp", "ctx", None),
            P("dp", "ctx", None),
            P(),
            P(),
            P(("dp", "ctx"), "tensor"),
            P("tensor"),
            P("tensor", ("dp", "ctx")),
            P(),
            P(),
            P(),
            P(("dp", "ctx"), "tensor"),
            P("tensor"),
            P("tensor", ("dp", "ctx")),
            P(),
        ),
        check_vma=False,
    )
```

```python
import functools
import math

import jax
import jax.numpy as jnp
from jax import lax
from jax.experimental import pallas as pl
from jax.experimental.pallas import tpu as pltpu
from jax.sharding import PartitionSpec as P

HS = 256
ROT = 64
LANES = 128


NORM_EPS = 1e-05


def rope_tables(positions, rot_dims):
    half_dims = rot_dims // 2
    freqs = 10000.0 ** (-(jnp.arange(half_dims, dtype=jnp.float32) * 2.0 / rot_dims))
    angles = positions.astype(jnp.float32)[:, None] * freqs[None, :]
    return (
        jnp.concatenate([jnp.cos(angles), jnp.cos(angles)], -1),
        jnp.concatenate([jnp.sin(angles), jnp.sin(angles)], -1),
    )


def rotate(columns, cosine_table, sine_table):
    half_dims = ROT // 2
    leading = columns[..., :ROT]
    turned = jnp.concatenate([-leading[..., half_dims:], leading[..., :half_dims]], -1)
    moved = leading * cosine_table[:, None, :] + turned * sine_table[:, None, :]
    return jnp.concatenate([moved, columns[..., ROT:]], -1)


def rotate_back(gradient, cosine_table, sine_table):
    half_dims = ROT // 2
    leading = gradient[..., :ROT]
    scaled = leading * sine_table[:, None, :]
    turned = jnp.concatenate([scaled[..., half_dims:], -scaled[..., :half_dims]], -1)
    moved = leading * cosine_table[:, None, :] + turned
    return jnp.concatenate([moved, gradient[..., ROT:]], -1)


def swap(array, axis, bit):
    pairs = [(place, place ^ bit) for place in range(lax.axis_size(axis))]
    return lax.ppermute(array, axis, pairs)


def bits_down(axis):
    size = lax.axis_size(axis)
    return [1 << level for level in reversed(range(size.bit_length() - 1))]


def relative_blocks(array, axis, dim):
    place = lax.axis_index(axis)
    for bit in bits_down(axis):
        size = array.shape[dim]
        halves = array.reshape(
            array.shape[:dim] + (size // (2 * bit), 2, bit) + array.shape[dim + 1 :]
        )
        flipped = jnp.flip(halves, dim + 1)
        array = jnp.where((place & bit) != 0, flipped, halves).reshape(array.shape)
    return array


def gather_rows(rows, axis):
    for bit in bits_down(axis):
        rows = jnp.concatenate([rows, swap(rows, axis, bit)], 0)
    return rows


def exchange_rows(rows, axis):
    for bit in bits_down(axis):
        rows = jnp.concatenate([rows[:, :bit], swap(rows[:, bit:], axis, bit)], 0)
    return rows[:, 0]


def block_order(size):
    order = [0]
    bit = size // 2
    while bit:
        order = order + [entry ^ bit for entry in order]
        bit //= 2
    return order


def tensor_sum(part):
    if lax.axis_size("tensor") == 2:
        low = part.astype(jnp.bfloat16)
        return low.astype(jnp.float32) + swap(low, "tensor", 1).astype(jnp.float32)
    return lax.psum(part, "tensor")


def reduce_blocks(total, axis, dim, bits=None):
    size = lax.axis_size(axis)
    for bit in [1 << level for level in range(size.bit_length() - 1)]:
        half = total.shape[dim] // 2
        keep = lax.slice_in_dim(total, 0, half, axis=dim)
        send = lax.slice_in_dim(total, half, 2 * half, axis=dim)
        arrived = swap(send.astype(jnp.bfloat16), axis, bit)
        total = keep + arrived.astype(jnp.float32)
    return total


def spread_columns(rows):
    dp_size, ctx_size = lax.axis_size("dp"), lax.axis_size("ctx")
    width = rows.shape[1] // (dp_size * ctx_size)
    blocks = rows.reshape(rows.shape[0], dp_size, ctx_size, width)
    blocks = relative_blocks(relative_blocks(blocks, "dp", 1), "ctx", 2)
    blocks = jnp.stack([blocks[:, entry] for entry in block_order(dp_size)], 2)
    return blocks.reshape(rows.shape[0], ctx_size, dp_size * width)


MESH = pl.DeviceIdType.MESH


def flip(place, bit):
    return place + bit - 2 * bit * ((place // bit) % 2)


def device_of(axis, bit):
    return {axis: flip(lax.axis_index(axis), bit)}


def send_to(source, target, send_sem, recv_sem, axis, bit):
    return pltpu.make_async_remote_copy(
        src_ref=source,
        dst_ref=target,
        send_sem=send_sem,
        recv_sem=recv_sem,
        device_id=device_of(axis, bit),
        device_id_type=MESH,
    )


def weight_kernel(
    plan,
    left_ref,
    right_ref,
    small_ref,
    out_ref,
    small_out,
    rows_all,
    first_send,
    first_recv,
    second_send,
    second_recv,
    held,
    small_held,
    small_recv,
    local_sem,
    out_sem,
    ctx_send,
    ctx_recv,
    dp_send,
    dp_recv,
    small_sems,
):
    groups, count, span, rows, shared = plan
    width = held.shape[1] // 2
    steps = (("ctx", 1), ("ctx", 2), ("dp", 1), ("dp", 2))
    tensor_bits = [1 << level for level in range(lax.axis_size("tensor").bit_length() - 1)]
    small_steps = steps + tuple(("tensor", bit) for bit in tensor_bits)

    barrier = pltpu.get_barrier_semaphore()
    for axis, bit in small_steps:
        pl.semaphore_signal(barrier, 1, device_id=device_of(axis, bit), device_id_type=MESH)
    pl.semaphore_wait(barrier, len(small_steps))

    def columns(piece):
        return pl.ds(pl.multiple_of(piece * span, span), span)

    def own(piece):
        return pltpu.make_async_copy(
            right_ref.at[:, columns(piece)], rows_all.at[piece, pl.ds(0, rows)], local_sem.at[piece]
        )

    def across(piece):
        return send_to(
            right_ref.at[:, columns(piece)],
            rows_all.at[piece, pl.ds(rows, rows)],
            ctx_send.at[piece, 0],
            ctx_recv.at[piece, 0],
            "ctx",
            2,
        )

    def beside(piece, part):
        source = (
            right_ref.at[:, columns(piece)] if part == 0 else rows_all.at[piece, pl.ds(rows, rows)]
        )
        return send_to(
            source,
            rows_all.at[piece, pl.ds((2 + part) * rows, rows)],
            ctx_send.at[piece, 1 + part],
            ctx_recv.at[piece, 1 + part],
            "ctx",
            1,
        )

    def first(piece):
        return send_to(
            first_send.at[piece],
            first_recv.at[piece],
            dp_send.at[piece, 0],
            dp_recv.at[piece, 0],
            "dp",
            1,
        )

    def second(piece):
        return send_to(
            second_send.at[piece],
            second_recv.at[piece],
            dp_send.at[piece, 1],
            dp_recv.at[piece, 1],
            "dp",
            2,
        )

    def result(piece):
        return pltpu.make_async_copy(
            held.at[piece % 4, pl.ds(0, width)], out_ref.at[:, columns(piece)], out_sem.at[piece]
        )

    def small(step):
        axis, bit = small_steps[step]
        return send_to(
            small_held.at[step],
            small_recv.at[step],
            small_sems.at[0, step],
            small_sems.at[1, step],
            axis,
            bit,
        )

    def start(piece):
        across(piece).start()
        own(piece).start()
        beside(piece, 0).start()

    small_held[0] = small_ref[...]
    small(0).start()
    start(0)
    start(1)

    def step(now, carry):
        @pl.when(now + 2 < count)
        def _():
            start(now + 2)

        @pl.when(now < count)
        def _():
            across(now).wait_recv()
            beside(now, 1).start()

        for entry in range(len(small_steps)):

            @pl.when(now == entry + 1)
            def _():
                small(entry).wait_recv()
                if small_steps[entry][0] == "tensor":
                    some = pl.ds(0, shared)
                    rest = pl.ds(shared, small_ref.shape[0] - shared)
                    small_held[entry + 1, some] = small_held[entry, some] + small_recv[entry, some]
                    small_held[entry + 1, rest] = small_held[entry, rest]
                else:
                    small_held[entry + 1] = small_held[entry] + small_recv[entry]
                if entry + 1 < len(small_steps):
                    small(entry + 1).start()

        multiply = now - 1

        @pl.when((multiply >= 0) & (multiply < count))
        def _():
            own(multiply).wait()
            beside(multiply, 0).wait_recv()
            beside(multiply, 1).wait_recv()

            @pl.when(multiply >= 4)
            def _():
                result(multiply - 4).wait()

            for group, low, high in groups:

                @pl.when((multiply >= low) & (multiply < high))
                def _():
                    first_send[multiply] = jnp.dot(
                        left_ref[group, pl.ds(2 * width, 2 * width)],
                        rows_all[multiply],
                        preferred_element_type=jnp.float32,
                    ).astype(jnp.bfloat16)
                    first(multiply).start()
                    held[multiply % 4] = jnp.dot(
                        left_ref[group, pl.ds(0, 2 * width)],
                        rows_all[multiply],
                        preferred_element_type=jnp.float32,
                    )

        add = now - 2

        @pl.when((add >= 0) & (add < count))
        def _():
            first(add).wait_recv()
            second_send[add] = (
                held[add % 4, pl.ds(width, width)]
                + first_recv[add, pl.ds(width, width)].astype(jnp.float32)
            ).astype(jnp.bfloat16)
            second(add).start()

        last = now - 3

        @pl.when((last >= 0) & (last < count))
        def _():
            second(last).wait_recv()
            held[last % 4, pl.ds(0, width)] = (
                held[last % 4, pl.ds(0, width)]
                + first_recv[last, pl.ds(0, width)].astype(jnp.float32)
                + second_recv[last].astype(jnp.float32)
            )
            result(last).start()

        return carry

    lax.fori_loop(0, max(count + 3, len(small_steps) + 1), step, 0)
    small_out[...] = small_held[len(small_steps)]
    for entry in range(len(small_steps)):
        small(entry).wait_send()

    def finish(piece, carry):
        across(piece).wait_send()
        beside(piece, 0).wait_send()
        beside(piece, 1).wait_send()
        first(piece).wait_send()
        second(piece).wait_send()

        @pl.when(piece >= max(count - 4, 0))
        def _():
            result(piece).wait()

        return carry

    lax.fori_loop(0, count, finish, 0)


def weight_gradients(lefts, rights, small, shared):
    width = lefts[0].shape[0] // lax.axis_size("dp")
    span = min(512, math.gcd(*[right.shape[1] for _, right in rights]))
    groups, at = [], 0
    for number, right in rights:
        groups.append((number, at, at + right.shape[1] // span))
        at += right.shape[1] // span
    count = at
    rows = rights[0][1].shape[0]
    tokens = rows * lax.axis_size("ctx")
    left = jnp.stack(lefts)
    right = jnp.concatenate([right for _, right in rights], 1)
    steps = sum(lax.axis_size(axis).bit_length() - 1 for axis in ("dp", "ctx", "tensor"))
    low = jnp.bfloat16
    vmem = pl.BlockSpec(memory_space=pltpu.VMEM)
    hbm = pl.BlockSpec(memory_space=pl.ANY)
    dma = pltpu.SemaphoreType.DMA
    out, small_out = pl.pallas_call(
        functools.partial(weight_kernel, (groups, count, span, rows, shared)),
        out_shape=(
            jax.ShapeDtypeStruct((width, right.shape[1]), jnp.float32),
            jax.ShapeDtypeStruct(small.shape, jnp.float32),
        ),
        in_specs=[vmem, hbm, vmem],
        out_specs=(hbm, vmem),
        scratch_shapes=[
            pltpu.VMEM((count, tokens, span), low),
            pltpu.VMEM((count, 2 * width, span), low),
            pltpu.VMEM((count, 2 * width, span), low),
            pltpu.VMEM((count, width, span), low),
            pltpu.VMEM((count, width, span), low),
            pltpu.VMEM((4, 2 * width, span), jnp.float32),
            pltpu.VMEM((steps + 1, *small.shape), jnp.float32),
            pltpu.VMEM((steps, *small.shape), jnp.float32),
            dma((count,)),
            dma((count,)),
            dma((count, 3)),
            dma((count, 3)),
            dma((count, 2)),
            dma((count, 2)),
            dma((2, steps)),
        ],
        compiler_params=pltpu.CompilerParams(
            collective_id=0, has_side_effects=True, vmem_limit_bytes=60 << 20
        ),
    )(left, right, small)
    outs = [out[:, low_at * span : high_at * span] for _, low_at, high_at in groups]
    return outs, small_out


def local(
    hidden_in,
    attn_norm_gain,
    attn_norm_bias,
    qkv_weight,
    qkv_bias,
    dense_weight,
    dense_bias,
    mlp_norm_gain,
    mlp_norm_bias,
    up_weight,
    up_bias,
    down_weight,
    down_bias,
    out_cotangent,
    subset_ids,
    subset_weights,
):
    seq_count, block_len, model_width = hidden_in.shape
    row_count = seq_count * block_len
    head_count = qkv_weight.shape[1] // (3 * HS)
    ctx_size = lax.axis_size("ctx")
    length = block_len * ctx_size
    score_scale = 1.0 / math.sqrt(HS)
    low_type = jnp.bfloat16
    hidden_rows = hidden_in.reshape(row_count, model_width)
    inputs = hidden_rows.astype(jnp.float32)
    row_mean = jnp.mean(inputs, -1, keepdims=True)
    centered = inputs - row_mean
    inv_std = lax.rsqrt(jnp.mean(centered * centered, -1, keepdims=True) + NORM_EPS)
    normed = centered * inv_std
    attn_in = (normed * attn_norm_gain + attn_norm_bias).astype(low_type)
    mlp_in = (normed * mlp_norm_gain + mlp_norm_bias).astype(low_type)

    subset_count = subset_weights.shape[0]
    matches = subset_ids[..., None] == jnp.arange(subset_count, dtype=jnp.int32)
    row_weight = jnp.sum(jnp.where(matches, subset_weights, 0.0), -1).reshape(row_count, 1)
    grad_out = out_cotangent.reshape(row_count, model_width).astype(jnp.float32) * row_weight
    grad_low = grad_out.astype(low_type)
    grad_out_bias = jnp.sum(grad_out, 0)

    low_part = exchange_rows(spread_columns(grad_low), "ctx")
    hidden_part = exchange_rows(spread_columns(hidden_rows), "ctx").astype(jnp.float32)
    stats = gather_rows(jnp.stack([row_mean[:, 0], inv_std[:, 0]])[None], "ctx")
    mean_all = stats[:, 0].reshape(ctx_size * row_count, 1)
    std_all = stats[:, 1].reshape(ctx_size * row_count, 1)
    normed_part = (hidden_part - mean_all) * std_all

    def own_columns(vector):
        return spread_columns(vector[None])[:, 0]

    mlp_part = (
        normed_part * own_columns(mlp_norm_gain) + own_columns(mlp_norm_bias)
    ).astype(low_type)
    attn_part = (
        normed_part * own_columns(attn_norm_gain) + own_columns(attn_norm_bias)
    ).astype(low_type)

    up_pre = jnp.dot(mlp_in, up_weight, preferred_element_type=jnp.float32) + up_bias
    activated = jax.nn.gelu(up_pre, approximate=False).astype(low_type)
    grad_act = jnp.einsum("rd,fd->rf", grad_low, down_weight, preferred_element_type=jnp.float32)
    gelu_back = jax.vjp(lambda pre_act: jax.nn.gelu(pre_act, approximate=False), up_pre)[1]
    grad_pre = gelu_back(grad_act)[0].astype(low_type)
    grad_up_bias = jnp.sum(grad_pre.astype(jnp.float32), 0)
    branch_part = jnp.dot(activated, down_weight, preferred_element_type=jnp.float32)
    grad_mlp_in = jnp.einsum("rf,df->rd", grad_pre, up_weight, preferred_element_type=jnp.float32)

    qkv_all = jnp.dot(attn_in, qkv_weight, preferred_element_type=jnp.float32) + qkv_bias
    qkv_all = qkv_all.reshape(seq_count, block_len, head_count, 3, HS)
    place = lax.axis_index("ctx")
    steps = jnp.arange(block_len, dtype=jnp.int32)
    positions = place * block_len + steps
    cosine_table, sine_table = rope_tables(positions, ROT)
    query_rows = rotate(qkv_all[:, :, :, 0], cosine_table, sine_table).astype(low_type)
    key_rows = rotate(qkv_all[:, :, :, 1], cosine_table, sine_table).astype(low_type)
    value_rows = qkv_all[:, :, :, 2].astype(low_type)
    pair = jnp.stack([key_rows, value_rows], 0).reshape(2 * seq_count, block_len, head_count * HS)
    whole = gather_rows(jnp.swapaxes(pair, 0, 1), "ctx")
    whole = jnp.swapaxes(whole, 0, 1).reshape(2, seq_count, length, head_count, HS)
    key_whole, value_whole = whole[0], whole[1]
    key_positions = jnp.concatenate(
        [(place ^ entry) * block_len + steps for entry in block_order(ctx_size)]
    )
    causal = key_positions[None, :] <= positions[:, None]
    raw = jnp.einsum("sqhd,skhd->shqk", query_rows, key_whole, preferred_element_type=jnp.float32)
    scores = jnp.where(causal, raw * score_scale, -1e30)
    row_max = jnp.max(scores, -1, keepdims=True)
    expd = jnp.exp(scores - row_max)
    prob = expd / jnp.sum(expd, -1, keepdims=True)
    prob_low = prob.astype(low_type)
    attn_out = jnp.einsum(
        "shqk,skhd->sqhd", prob_low, value_whole, preferred_element_type=jnp.float32
    ).astype(low_type)
    attn_out = attn_out.reshape(row_count, head_count * HS)
    branch_part = branch_part + jnp.dot(
        attn_out, dense_weight, preferred_element_type=jnp.float32
    )
    layer_out = (inputs + tensor_sum(branch_part) + dense_bias + down_bias).astype(low_type)
    layer_out = layer_out.reshape(seq_count, block_len, model_width)

    grad_attn = jnp.einsum("rd,kd->rk", grad_low, dense_weight, preferred_element_type=jnp.float32)
    grad_attn = grad_attn.astype(low_type).reshape(seq_count, block_len, head_count, HS)
    grad_prob = jnp.einsum(
        "sqhd,skhd->shqk", grad_attn, value_whole, preferred_element_type=jnp.float32
    )
    delta = jnp.sum(grad_prob * prob, -1, keepdims=True)
    grad_scores = (prob * (grad_prob - delta)).astype(low_type)
    grad_query = (
        jnp.einsum("shqk,skhd->sqhd", grad_scores, key_whole, preferred_element_type=jnp.float32)
        * score_scale
    )
    grad_key_whole = (
        jnp.einsum("shqk,sqhd->kshd", grad_scores, query_rows, preferred_element_type=jnp.float32)
        * score_scale
    )
    grad_value_whole = jnp.einsum(
        "shqk,sqhd->kshd", prob_low, grad_attn, preferred_element_type=jnp.float32
    )
    grad_pair = jnp.concatenate(
        [
            grad_key_whole.reshape(length, seq_count * head_count * HS),
            grad_value_whole.reshape(length, seq_count * head_count * HS),
        ],
        1,
    )
    grad_pair = reduce_blocks(grad_pair, "ctx", 0)
    grad_pair = grad_pair.reshape(block_len, 2, seq_count, head_count, HS)
    grad_key_rows = jnp.swapaxes(grad_pair[:, 0], 0, 1)
    grad_value_rows = jnp.swapaxes(grad_pair[:, 1], 0, 1)
    grad_qkv = jnp.stack(
        [
            rotate_back(grad_query, cosine_table, sine_table),
            rotate_back(grad_key_rows, cosine_table, sine_table),
            grad_value_rows,
        ],
        3,
    )
    grad_qkv = grad_qkv.reshape(row_count, head_count * 3 * HS).astype(low_type)
    grad_qkv_bias = jnp.sum(grad_qkv.astype(jnp.float32), 0)
    grad_attn_in = jnp.einsum("rc,dc->rd", grad_qkv, qkv_weight, preferred_element_type=jnp.float32)
    norm_parts = jnp.stack(
        [
            jnp.sum(grad_attn_in * normed, 0),
            jnp.sum(grad_attn_in, 0),
            jnp.sum(grad_mlp_in * normed, 0),
            jnp.sum(grad_mlp_in, 0),
        ]
    )
    grad_normed = grad_attn_in * attn_norm_gain + grad_mlp_in * mlp_norm_gain
    input_part = inv_std * (
        grad_normed
        - jnp.mean(grad_normed, -1, keepdims=True)
        - normed * jnp.mean(grad_normed * normed, -1, keepdims=True)
    )
    input_grad = (
        (grad_out + tensor_sum(input_part))
        .astype(low_type)
        .reshape(seq_count, block_len, model_width)
    )
    small = jnp.concatenate(
        [norm_parts.reshape(-1), grad_out_bias, grad_qkv_bias, grad_up_bias]
    ).reshape(-1, LANES)
    shared = norm_parts.size // LANES
    (down_grad, up_grad, dense_grad, qkv_grad), small = weight_gradients(
        [low_part.T, mlp_part.T, attn_part.T],
        [(0, activated), (1, grad_pre), (0, attn_out), (2, grad_qkv)],
        small,
        shared,
    )
    small = small.reshape(-1)
    norm_total = small[: norm_parts.size].reshape(norm_parts.shape)
    cuts = [norm_parts.size, grad_out_bias.size, grad_qkv_bias.size, grad_up_bias.size]
    cuts = [sum(cuts[: place + 1]) for place in range(4)]
    out_bias_sum, qkv_bias_sum, up_bias_sum = [
        small[cuts[place] : cuts[place + 1]] for place in range(3)
    ]
    return (
        layer_out,
        input_grad,
        norm_total[0],
        norm_total[1],
        qkv_grad,
        qkv_bias_sum,
        dense_grad.T,
        out_bias_sum,
        norm_total[2],
        norm_total[3],
        up_grad,
        up_bias_sum,
        down_grad.T,
        out_bias_sum,
    )


def solution(mesh):
    return jax.shard_map(
        local,
        mesh=mesh,
        in_specs=(
            P("dp", "ctx", None),
            P(),
            P(),
            P(None, "tensor"),
            P("tensor"),
            P("tensor", None),
            P(),
            P(),
            P(),
            P(None, "tensor"),
            P("tensor"),
            P("tensor", None),
            P(),
            P("dp", "ctx", None),
            P("dp", "ctx"),
            P(),
        ),
        out_specs=(
            P("dp", "ctx", None),
            P("dp", "ctx", None),
            P(),
            P(),
            P(("dp", "ctx"), "tensor"),
            P("tensor"),
            P("tensor", ("dp", "ctx")),
            P(),
            P(),
            P(),
            P(("dp", "ctx"), "tensor"),
            P("tensor"),
            P("tensor", ("dp", "ctx")),
            P(),
        ),
        check_vma=False,
    )
```

```python
import functools
import math
import types

import jax
import jax.numpy as jnp
from jax import lax
from jax.experimental import pallas as pl
from jax.experimental.pallas import tpu as pltpu
from jax.sharding import PartitionSpec as P

HS = 256
ROT = 64
LANES = 128
RING = 8
NORM_EPS = 1e-05
MESH = pl.DeviceIdType.MESH
ORDER = (0, 2, 1, 3)
LOW = jnp.bfloat16
F32 = jnp.float32


def flip(place, bits):
    bit = 1
    while bit <= bits:
        if bits & bit:
            place = place + bit - 2 * bit * ((place // bit) % 2)
        bit *= 2
    return place


def send_to(source, target, send_sem, recv_sem, axis, bits):
    return pltpu.make_async_remote_copy(
        src_ref=source,
        dst_ref=target,
        send_sem=send_sem,
        recv_sem=recv_sem,
        device_id={axis: flip(lax.axis_index(axis), bits)},
        device_id_type=MESH,
    )


def dot(left, right):
    return jnp.dot(left, right, preferred_element_type=F32)


def dot_rows(left, right):
    return lax.dot_general(left, right, (((1,), (1,)), ((), ())), preferred_element_type=F32)


def axis_bits(axis):
    return [1 << level for level in range(lax.axis_size(axis).bit_length() - 1)]


def blocks_of(total, size):
    return pl.ds(pl.multiple_of(total * size, size), size)


def layer_kernel(plan, names, *refs):
    at = types.SimpleNamespace(**dict(zip(names, refs)))
    rows, span, count, width = plan.rows, plan.span, plan.count, plan.width
    pairs, heads, late = plan.pairs, plan.heads, 2 * plan.pairs
    attn_pieces = heads * HS // span
    per_piece = span // HS
    model = at.hidden.shape[1]
    ctx, dp = lax.axis_index("ctx"), lax.axis_index("dp")
    own_rows = pl.ds(0, rows)
    tensor_bits = axis_bits("tensor")
    halving = (("ctx", 1), ("ctx", 2), ("dp", 1), ("dp", 2))
    small_steps = halving + tuple(("tensor", bit) for bit in tensor_bits)
    scale = 1.0 / math.sqrt(HS)

    def up_load(piece):
        return pltpu.make_async_copy(
            at.up_weight.at[:, blocks_of(piece, span)], at.up_held, at.load_sem.at[0]
        )

    def down_load(piece):
        return pltpu.make_async_copy(
            at.down_weight.at[blocks_of(piece, span)], at.down_held, at.load_sem.at[1]
        )

    def qkv_load(head):
        return pltpu.make_async_copy(
            at.qkv_weight.at[:, blocks_of(head, 3 * HS)], at.qkv_held, at.load_sem.at[2]
        )

    def gate_load(head):
        return pltpu.make_async_copy(
            at.dense_weight.at[blocks_of(head, HS)], at.gate_held, at.load_sem.at[3]
        )

    def dense_load(head):
        return pltpu.make_async_copy(
            at.dense_weight.at[blocks_of(head, HS)], at.dense_held, at.load_sem.at[4]
        )

    def part_copy(kind, place, block):
        source = (at.low, at.hidden)[kind]
        target = (at.low_part, at.hidden_part)[kind]
        column = block * 4 + flip(ctx, place)
        return send_to(
            source.at[:, blocks_of(column, width)],
            target.at[pl.ds(ORDER.index(place) * rows, rows), pl.ds(block * width, width)],
            at.part_send.at[kind, place - 1, block],
            at.part_recv.at[kind, place - 1, block],
            "ctx",
            place,
        )

    def stats_copy(place):
        return send_to(
            at.stats.at[own_rows],
            at.stats.at[pl.ds(ORDER.index(place) * rows, rows)],
            at.stats_send.at[place - 1],
            at.stats_recv.at[place - 1],
            "ctx",
            place,
        )

    def across(piece):
        slot = piece % RING
        return send_to(
            at.rows_all.at[slot, own_rows],
            at.rows_all.at[slot, pl.ds(rows, rows)],
            at.ctx_send.at[slot, 0],
            at.ctx_recv.at[slot, 0],
            "ctx",
            2,
        )

    def beside(piece, part):
        slot = piece % RING
        return send_to(
            at.rows_all.at[slot, pl.ds(part * rows, rows)],
            at.rows_all.at[slot, pl.ds((2 + part) * rows, rows)],
            at.ctx_send.at[slot, 1 + part],
            at.ctx_recv.at[slot, 1 + part],
            "ctx",
            1,
        )

    def first(piece):
        return send_to(
            at.first_send.at[piece % 2],
            at.first_recv.at[piece % RING],
            at.dp_send.at[piece % RING, 0],
            at.dp_recv.at[piece % RING, 0],
            "dp",
            1,
        )

    def second(piece):
        return send_to(
            at.second_send.at[piece % 2],
            at.second_recv.at[piece % RING],
            at.dp_send.at[piece % RING, 1],
            at.dp_recv.at[piece % RING, 1],
            "dp",
            2,
        )

    def results(piece):
        slot = piece % 2
        turned, plain = at.turned.at[slot], at.plain.at[slot]
        feed = piece < late
        dense = (piece >= late) & (piece < late + attn_pieces)
        return (
            (feed & (piece % 2 == 0), turned, at.down_out.at[blocks_of(piece // 2, span)]),
            (feed & (piece % 2 == 1), plain, at.up_out.at[:, blocks_of(piece // 2, span)]),
            (dense, turned, at.dense_out.at[blocks_of(piece - late, span)]),
            (
                piece >= late + attn_pieces,
                plain,
                at.qkv_out.at[:, blocks_of(piece - late - attn_pieces, span)],
            ),
        )

    def for_result(piece, act):
        for holds, source, target in results(piece):

            @pl.when(holds)
            def _():
                act(pltpu.make_async_copy(source, target, at.out_sem.at[piece % 2]))

    def kv_across(head):
        return send_to(
            at.kv.at[head, own_rows],
            at.kv.at[head, pl.ds(rows, rows)],
            at.kv_send.at[head, 0],
            at.kv_recv.at[head, 0],
            "ctx",
            2,
        )

    def kv_beside(head, part):
        return send_to(
            at.kv.at[head, pl.ds(part * rows, rows)],
            at.kv.at[head, pl.ds((2 + part) * rows, rows)],
            at.kv_send.at[head, 1 + part],
            at.kv_recv.at[head, 1 + part],
            "ctx",
            1,
        )

    def pair_beside(head):
        return send_to(
            at.pair_send,
            at.pair_recv.at[head],
            at.kv_send.at[head, 3],
            at.kv_recv.at[head, 3],
            "ctx",
            1,
        )

    def pair_across(head):
        return send_to(
            at.pair_send_low.at[head % 2],
            at.pair_recv_low.at[head],
            at.kv_send.at[head, 4],
            at.kv_recv.at[head, 4],
            "ctx",
            2,
        )

    def tensor_copy(which, level):
        return send_to(
            at.sum_send.at[level],
            at.sum_recv.at[which, level],
            at.sum_sems.at[0, which, level],
            at.sum_sems.at[1, which, level],
            "tensor",
            tensor_bits[level],
        )

    def small_copy(entry):
        axis, bit = small_steps[entry]
        return send_to(
            at.small.at[entry],
            at.small_recv.at[entry],
            at.small_sems.at[0, entry],
            at.small_sems.at[1, entry],
            axis,
            bit,
        )

    def vector(number):
        return at.vectors[pl.ds(number, 1)]

    def turn(heads_rows, back):
        start_part = heads_rows[:, :LANES]
        ahead = pltpu.roll(start_part, LANES - ROT // 2, 1) * at.angles[1]
        behind = pltpu.roll(start_part, ROT // 2, 1) * at.angles[2]
        straight = start_part * at.angles[0]
        moved = straight - ahead - behind if back else straight + ahead + behind
        return jnp.concatenate([moved, heads_rows[:, LANES:]], 1)

    def late_block(block):
        piece = attn_pieces + block // per_piece
        return at.late.at[piece, :, blocks_of(block % per_piece, HS)]

    up_load(0).start()
    down_load(0).start()
    qkv_load(0).start()
    gate_load(0).start()
    dense_load(0).start()
    barrier = pltpu.get_barrier_semaphore()
    partners = small_steps + (("ctx", 3),)
    for axis, bits in partners:
        pl.semaphore_signal(
            barrier,
            1,
            device_id={axis: flip(lax.axis_index(axis), bits)},
            device_id_type=MESH,
        )
    pl.semaphore_wait(barrier, len(partners))
    for place in (2, 3, 1):
        for block in range(4):
            part_copy(1, place, block).start()
    at.small[0] = jnp.zeros_like(at.small[0])
    step_rows = 32

    @pl.loop(0, rows // step_rows)
    def _(block):
        some = blocks_of(block, step_rows)
        inputs = at.hidden[some].astype(F32)
        mean = jnp.mean(inputs, -1, keepdims=True)
        centered = inputs - mean
        inv_std = lax.rsqrt(jnp.mean(centered * centered, -1, keepdims=True) + NORM_EPS)
        normed = centered * inv_std
        at.attn_in[some] = (normed * vector(0) + vector(1)).astype(LOW)
        at.mlp_in[some] = (normed * vector(2) + vector(3)).astype(LOW)
        lane = lax.broadcasted_iota(jnp.int32, (step_rows, LANES), 1)
        at.stats[some] = jnp.where(lane < LANES // 2, mean, inv_std)
        grad_out = at.cotangent[some].astype(F32) * at.row_weight[some]
        at.low[some] = grad_out.astype(LOW)
        at.small[0, pl.ds(2, 1), pl.ds(0, model)] += jnp.sum(grad_out, 0, keepdims=True)
        zeros = jnp.zeros((step_rows, model), F32)
        at.branch[some] = zeros
        at.grad_mlp[some] = zeros
        at.grad_attn[some] = zeros

    for place in (2, 3, 1):
        stats_copy(place).start()
        for block in range(4):
            part_copy(0, place, block).start()
    for block in range(4):
        column = blocks_of(block * 4 + ctx, width)
        at.low_part[own_rows, pl.ds(block * width, width)] = at.low[:, column]
        at.hidden_part[own_rows, pl.ds(block * width, width)] = at.hidden[:, column]

    def low_left():
        for place in (1, 2, 3):
            for block in range(4):
                part_copy(0, place, block).wait_recv()
        for entry, bits in enumerate(ORDER):
            block = at.low_part[:, blocks_of(flip(dp, bits), width)]
            at.left[0, pl.ds(entry * width, width)] = block.T

    def hidden_left():
        for place in (1, 2, 3):
            stats_copy(place).wait_recv()
            for block in range(4):
                part_copy(1, place, block).wait_recv()
        for entry, bits in enumerate(ORDER):
            place = flip(dp, bits)
            block = at.hidden_part[:, blocks_of(place, width)].astype(F32)
            normed = (block - at.stats[:, :1]) * at.stats[:, LANES // 2 : LANES // 2 + 1]
            column = blocks_of(place * 4 + ctx, width)
            to = pl.ds(entry * width, width)
            for number in range(2):
                gain = at.vectors[pl.ds(2 - 2 * number, 1), column]
                bias = at.vectors[pl.ds(3 - 2 * number, 1), column]
                at.left[1 + number, to] = (normed * gain + bias).astype(LOW).T

    def start_piece(piece):
        @pl.when(piece >= RING)
        def _():
            pl.semaphore_wait(at.free.at[0], 1)
            pl.semaphore_wait(at.free.at[1], 1)

        @pl.when(piece >= late)
        def _():
            at.rows_all[piece % RING, own_rows] = at.late[piece - late]

        across(piece).start()
        beside(piece, 0).start()

    def feed_forward(pair):
        up_load(pair).wait()
        down_load(pair).wait()
        pre = dot(at.mlp_in[...], at.up_held[...]) + at.up_bias[:, blocks_of(pair, span)]
        cumulative = 0.5 * (1.0 + lax.erf(pre * math.sqrt(0.5)))
        at.rows_all[(2 * pair) % RING, own_rows] = (pre * cumulative).astype(LOW)
        start_piece(2 * pair)
        grad_act = dot_rows(at.low[...], at.down_held[...])
        density = jnp.exp(-0.5 * pre * pre) * (1.0 / math.sqrt(2.0 * math.pi))
        grad_pre = (grad_act * (cumulative + pre * density)).astype(LOW)
        at.rows_all[(2 * pair + 1) % RING, own_rows] = grad_pre
        at.small[0, pl.ds(4, 1), blocks_of(pair, span)] = jnp.sum(
            grad_pre.astype(F32), 0, keepdims=True
        )
        start_piece(2 * pair + 1)
        at.branch[...] += dot(at.rows_all[(2 * pair) % RING, own_rows], at.down_held[...])
        at.grad_mlp[...] += dot_rows(
            at.rows_all[(2 * pair + 1) % RING, own_rows], at.up_held[...]
        )

        @pl.when(pair + 1 < pairs)
        def _():
            up_load(pair + 1).start()
            down_load(pair + 1).start()

    def project(head):
        qkv_load(head).wait()
        out = dot(at.attn_in[...], at.qkv_held[...]) + at.qkv_bias[:, blocks_of(head, 3 * HS)]
        at.kv[head, own_rows, pl.ds(0, HS)] = turn(out[:, HS : 2 * HS], False).astype(LOW)
        at.kv[head, own_rows, pl.ds(HS, HS)] = out[:, 2 * HS :].astype(LOW)
        kv_across(head).start()
        kv_beside(head, 0).start()
        at.query[head] = turn(out[:, :HS], False).astype(LOW)
        gate_load(head).wait()
        at.gate[head] = dot_rows(at.low[...], at.gate_held[...]).astype(LOW)
        qkv_load((head + 1) % heads).start()

        @pl.when(head + 1 < heads)
        def _():
            gate_load(head + 1).start()

    def kv_forward(head):
        kv_across(head).wait_recv()
        kv_beside(head, 1).start()

    def attend(head):
        kv_beside(head, 0).wait_recv()
        kv_beside(head, 1).wait_recv()
        query, gate = at.query[head], at.gate[head]
        keys, values = at.kv[head, :, :HS], at.kv[head, :, HS:]
        shape = (rows, 4 * rows)
        key_place = lax.broadcasted_iota(jnp.int32, shape, 1)
        shift = jnp.full(shape, flip(ctx, ORDER[3]) * rows - 3 * rows, jnp.int32)
        for entry in (2, 1, 0):
            here = flip(ctx, ORDER[entry]) * rows - entry * rows
            shift = jnp.where(key_place < (entry + 1) * rows, here, shift)
        query_place = lax.broadcasted_iota(jnp.int32, shape, 0) + ctx * rows
        scores = jnp.where(
            key_place + shift <= query_place, dot_rows(query, keys) * scale, -1e30
        )
        expd = jnp.exp(scores - jnp.max(scores, -1, keepdims=True))
        prob = expd * (1.0 / jnp.sum(expd, -1, keepdims=True))
        prob_low = prob.astype(LOW)
        attended = dot(prob_low, values).astype(LOW)
        at.late[head // per_piece, :, blocks_of(head % per_piece, HS)] = attended
        grad_prob = dot_rows(gate, values)
        delta = jnp.sum(grad_prob * prob, -1, keepdims=True)
        grad_scores = (prob * (grad_prob - delta)).astype(LOW)
        grad_key = dot(grad_scores.T, query) * scale
        grad_value = dot(prob_low.T, gate)
        at.pair_send[:, pl.ds(0, HS)] = grad_key[2 * rows :].astype(LOW)
        at.pair_send[:, pl.ds(HS, HS)] = grad_value[2 * rows :].astype(LOW)
        pair_beside(head).start()
        at.pair[head % 2, :, pl.ds(0, HS)] = grad_key[: 2 * rows]
        at.pair[head % 2, :, pl.ds(HS, HS)] = grad_value[: 2 * rows]
        late_block(3 * head)[...] = turn(dot(grad_scores, keys) * scale, True).astype(LOW)
        dense_load(head).wait()
        at.branch[...] += dot(attended, at.dense_held[...])

        @pl.when(head + 1 < heads)
        def _():
            dense_load(head + 1).start()

    def pair_halve(head):
        pair_beside(head).wait()
        at.pair[head % 2] += at.pair_recv[head].astype(F32)
        at.pair_send_low[head % 2] = at.pair[head % 2, pl.ds(rows, rows)].astype(LOW)
        pair_across(head).start()

    def pair_finish(head):
        pair_across(head).wait()
        total = at.pair[head % 2, own_rows] + at.pair_recv_low[head].astype(F32)
        late_block(3 * head + 1)[...] = turn(total[:, :HS], True).astype(LOW)
        late_block(3 * head + 2)[...] = total[:, HS:].astype(LOW)
        for number in range(3):
            at.small[0, pl.ds(3, 1), blocks_of(3 * head + number, HS)] = jnp.sum(
                late_block(3 * head + number)[...].astype(F32), 0, keepdims=True
            )

    def project_back(head):
        qkv_load(head).wait()
        at.grad_attn[...] += (
            dot_rows(late_block(3 * head)[...], at.qkv_held[:, :HS])
            + dot_rows(late_block(3 * head + 1)[...], at.qkv_held[:, HS : 2 * HS])
            + dot_rows(late_block(3 * head + 2)[...], at.qkv_held[:, 2 * HS :])
        )

        @pl.when(head + 1 < heads)
        def _():
            qkv_load(head + 1).start()

    def branch_send():
        at.sum_send[0] = at.branch[...].astype(LOW)
        tensor_copy(0, 0).start()

    def tensor_step(which, level):
        tensor_copy(which, level).wait()
        if level + 1 < len(tensor_bits):
            at.sum_send[level + 1] = (
                at.sum_send[level].astype(F32) + at.sum_recv[which, level].astype(F32)
            ).astype(LOW)
            tensor_copy(which, level + 1).start()
            return

        @pl.loop(0, rows // step_rows)
        def _(block):
            some = blocks_of(block, step_rows)
            total = at.sum_send[level, some].astype(F32) + at.sum_recv[which, level, some].astype(
                F32
            )
            if which == 0:
                total = at.hidden[some].astype(F32) + total + vector(4) + vector(5)
                at.layer_out[some] = total.astype(LOW)
            else:
                grad_out = at.cotangent[some].astype(F32) * at.row_weight[some]
                at.input_grad[some] = (grad_out + total).astype(LOW)

    def norm_back():
        @pl.loop(0, rows // step_rows)
        def _(block):
            some = blocks_of(block, step_rows)
            stats = at.stats[some]
            inv_std = stats[:, LANES // 2 : LANES // 2 + 1]
            normed = (at.hidden[some].astype(F32) - stats[:, :1]) * inv_std
            grad_attn, grad_mlp = at.grad_attn[some], at.grad_mlp[some]
            for row, grad in enumerate((grad_attn, grad_mlp)):
                at.small[0, pl.ds(row, 1), pl.ds(0, model)] += jnp.sum(
                    grad * normed, 0, keepdims=True
                )
                at.small[0, pl.ds(row, 1), pl.ds(model, model)] += jnp.sum(grad, 0, keepdims=True)
            grad = grad_attn * vector(0) + grad_mlp * vector(2)
            part = inv_std * (
                grad
                - jnp.mean(grad, -1, keepdims=True)
                - normed * jnp.mean(grad * normed, -1, keepdims=True)
            )
            at.sum_send[0, some] = part.astype(LOW)

        tensor_copy(1, 0).start()
        small_copy(0).start()

    def small_step(entry):
        small_copy(entry).wait()
        if small_steps[entry][0] == "tensor":
            both, rest = pl.ds(0, 2), pl.ds(2, at.small.shape[1] - 2)
            at.small[entry + 1, both] = at.small[entry, both] + at.small_recv[entry, both]
            at.small[entry + 1, rest] = at.small[entry, rest]
        else:
            at.small[entry + 1] = at.small[entry] + at.small_recv[entry]
        if entry + 1 < len(small_steps):
            small_copy(entry + 1).start()
        else:
            at.small_out[...] = at.small[entry + 1]

    attend_at = 5
    last_attend = attend_at + 2 * (heads - 1)
    last_feed = 2 * (pairs - 1) - 2
    branch_at = max(last_attend, last_feed) + 1
    back_at = last_attend + 5
    assert branch_at + 3 * len(tensor_bits) <= back_at or heads == 1
    back_at = max(back_at, branch_at + 3 * len(tensor_bits) + 1)
    total_steps = max(
        count + 3, back_at + 1 + len(small_steps), back_at + 3 * len(tensor_bits) + 1
    )

    def step(turn_number, carry):
        now = turn_number - 2

        def job(start, stride, times, act):
            index = now - start

            @pl.when((index >= 0) & (index < stride * times) & (index % stride == 0))
            def _():
                act(index // stride)

        @pl.when((now >= 0) & (now < count))
        def _():
            across(now).wait_recv()
            beside(now, 1).start()

        multiply = now - 1

        @pl.when((multiply >= 0) & (multiply < count))
        def _():
            beside(multiply, 0).wait_recv()
            beside(multiply, 1).wait_recv()

            @pl.when(multiply >= RING)
            def _():
                pl.semaphore_wait(at.free.at[2], 1)

            @pl.when(multiply >= 2)
            def _():
                first(multiply - 2).wait_send()

            feed = multiply < late
            group = jnp.where(
                feed, multiply % 2, jnp.where(multiply < late + attn_pieces, 0, 2)
            )
            at.first_send[multiply % 2] = dot(
                at.left[group, pl.ds(2 * width, 2 * width)], at.rows_all[multiply % RING]
            ).astype(LOW)
            first(multiply).start()
            at.held[multiply % 3] = dot(
                at.left[group, pl.ds(0, 2 * width)], at.rows_all[multiply % RING]
            )

        add = now - 2

        @pl.when((add >= 0) & (add < count))
        def _():
            first(add).wait_recv()

            @pl.when(add >= RING)
            def _():
                pl.semaphore_wait(at.free.at[3], 1)

            @pl.when(add >= 2)
            def _():
                second(add - 2).wait_send()

            lower = pl.ds(width, width)
            at.second_send[add % 2] = (
                at.held[add % 3, lower] + at.first_recv[add % RING, lower].astype(F32)
            ).astype(LOW)
            second(add).start()
            across(add).wait_send()
            beside(add, 0).wait_send()
            beside(add, 1).wait_send()

            @pl.when(add < count - RING)
            def _():
                for number, bit in ((0, 2), (1, 1)):
                    pl.semaphore_signal(
                        at.free.at[number],
                        1,
                        device_id={"ctx": flip(ctx, bit)},
                        device_id_type=MESH,
                    )

        last = now - 3

        @pl.when((last >= 0) & (last < count))
        def _():
            second(last).wait_recv()

            @pl.when(last >= 2)
            def _():
                for_result(last - 2, lambda copy: copy.wait())

            upper = pl.ds(0, width)
            total = (
                at.held[last % 3, upper]
                + at.first_recv[last % RING, upper].astype(F32)
                + at.second_recv[last % RING].astype(F32)
            )
            flat = ((last < late) & (last % 2 == 1)) | (last >= late + attn_pieces)

            @pl.when(flat)
            def _():
                at.plain[last % 2] = total

            @pl.when(jnp.logical_not(flat))
            def _():
                at.turned[last % 2] = total.T

            for_result(last, lambda copy: copy.start())

            @pl.when(last < count - RING)
            def _():
                for number, bit in ((2, 1), (3, 2)):
                    pl.semaphore_signal(
                        at.free.at[number],
                        1,
                        device_id={"dp": flip(dp, bit)},
                        device_id_type=MESH,
                    )

        job(0, 1, 1, lambda _: low_left())
        job(1, 1, 1, lambda _: hidden_left())
        job(-2, 2, pairs, feed_forward)
        job(-1, 2, heads, project)
        job(1, 2, heads, kv_forward)
        job(attend_at + 3, 2, heads, pair_finish)
        job(attend_at + 1, 2, heads, pair_halve)
        job(attend_at, 2, heads, attend)
        job(attend_at + 4, 2, heads, project_back)
        job(branch_at, 1, 1, lambda _: branch_send())
        for level in range(len(tensor_bits)):
            job(branch_at + 3 * (level + 1), 1, 1, lambda _: tensor_step(0, level))
        job(back_at, 1, 1, lambda _: norm_back())
        for level in range(len(tensor_bits)):
            job(back_at + 3 * (level + 1), 1, 1, lambda _: tensor_step(1, level))
        for entry in range(len(small_steps)):
            job(back_at + 1 + entry, 1, 1, lambda _: small_step(entry))

        @pl.when((now + 2 >= late) & (now + 2 < count))
        def _():
            start_piece(now + 2)

        return carry

    lax.fori_loop(0, total_steps + 2, step, 0)

    for place in (1, 2, 3):
        stats_copy(place).wait_send()
        for kind in range(2):
            for block in range(4):
                part_copy(kind, place, block).wait_send()

    @pl.loop(0, heads)
    def _(head):
        kv_across(head).wait_send()
        kv_beside(head, 0).wait_send()
        kv_beside(head, 1).wait_send()

    @pl.loop(count - 2, count)
    def _(piece):
        first(piece).wait_send()
        second(piece).wait_send()
        for_result(piece, lambda copy: copy.wait())


def local(
    hidden_in,
    attn_norm_gain,
    attn_norm_bias,
    qkv_weight,
    qkv_bias,
    dense_weight,
    dense_bias,
    mlp_norm_gain,
    mlp_norm_bias,
    up_weight,
    up_bias,
    down_weight,
    down_bias,
    out_cotangent,
    subset_ids,
    subset_weights,
):
    seq_count, rows, model = hidden_in.shape
    heads = qkv_weight.shape[1] // (3 * HS)
    units = up_weight.shape[1]
    width = model // (lax.axis_size("dp") * lax.axis_size("ctx"))
    span = min(512, math.gcd(units, heads * HS, heads * 3 * HS))
    pairs = units // span
    late_count = heads * 4 * HS // span
    plan = types.SimpleNamespace(
        rows=rows, span=span, width=width, pairs=pairs, heads=heads, count=2 * pairs + late_count
    )
    tokens = rows * lax.axis_size("ctx")

    subset_count = subset_weights.shape[0]
    matches = subset_ids[..., None] == jnp.arange(subset_count, dtype=jnp.int32)
    row_weight = jnp.sum(jnp.where(matches, subset_weights, 0.0), -1).reshape(rows, 1)
    positions = lax.axis_index("ctx") * rows + jnp.arange(rows, dtype=jnp.int32)
    half = ROT // 2
    freqs = 10000.0 ** (-(jnp.arange(half, dtype=F32) * 2.0 / ROT))
    table = positions.astype(F32)[:, None] * freqs[None, :]
    cosine, sine = jnp.cos(table), jnp.sin(table)
    none, rest = jnp.zeros_like(sine), jnp.zeros((rows, LANES - ROT), F32)
    angles = jnp.stack(
        [
            jnp.concatenate([cosine, cosine, rest + 1.0], 1),
            jnp.concatenate([-sine, none, rest], 1),
            jnp.concatenate([none, sine, rest], 1),
        ]
    )
    vectors = jnp.stack(
        [attn_norm_gain, attn_norm_bias, mlp_norm_gain, mlp_norm_bias, dense_bias, down_bias]
    )

    bits = lax.axis_size("tensor").bit_length() - 1
    steps = 4 + bits
    small_width = max(2 * model, units, heads * 3 * HS)
    dma = pltpu.SemaphoreType.DMA
    vmem = pl.BlockSpec(memory_space=pltpu.VMEM)
    hbm = pl.BlockSpec(memory_space=pl.ANY)
    inputs = {
        "hidden": (hidden_in.reshape(rows, model), vmem),
        "cotangent": (out_cotangent.reshape(rows, model), vmem),
        "row_weight": (row_weight, vmem),
        "angles": (angles, vmem),
        "vectors": (vectors, vmem),
        "qkv_bias": (qkv_bias[None], vmem),
        "up_bias": (up_bias[None], vmem),
        "qkv_weight": (qkv_weight, hbm),
        "dense_weight": (dense_weight, hbm),
        "up_weight": (up_weight, hbm),
        "down_weight": (down_weight, hbm),
    }
    outputs = {
        "layer_out": ((rows, model), LOW, vmem),
        "input_grad": ((rows, model), LOW, vmem),
        "small_out": ((8, small_width), F32, vmem),
        "down_out": ((units, width), F32, hbm),
        "up_out": ((width, units), F32, hbm),
        "dense_out": ((heads * HS, width), F32, hbm),
        "qkv_out": ((width, heads * 3 * HS), F32, hbm),
    }
    scratch = {
        "rows_all": pltpu.VMEM((RING, tokens, span), LOW),
        "first_send": pltpu.VMEM((2, 2 * width, span), LOW),
        "first_recv": pltpu.VMEM((RING, 2 * width, span), LOW),
        "second_send": pltpu.VMEM((2, width, span), LOW),
        "second_recv": pltpu.VMEM((RING, width, span), LOW),
        "held": pltpu.VMEM((3, 2 * width, span), F32),
        "plain": pltpu.VMEM((2, width, span), F32),
        "turned": pltpu.VMEM((2, span, width), F32),
        "left": pltpu.VMEM((3, 4 * width, tokens), LOW),
        "low_part": pltpu.VMEM((tokens, 4 * width), LOW),
        "hidden_part": pltpu.VMEM((tokens, 4 * width), LOW),
        "stats": pltpu.VMEM((tokens, LANES), F32),
        "attn_in": pltpu.VMEM((rows, model), LOW),
        "mlp_in": pltpu.VMEM((rows, model), LOW),
        "low": pltpu.VMEM((rows, model), LOW),
        "up_held": pltpu.VMEM((model, span), LOW),
        "down_held": pltpu.VMEM((span, model), LOW),
        "qkv_held": pltpu.VMEM((model, 3 * HS), LOW),
        "gate_held": pltpu.VMEM((HS, model), LOW),
        "dense_held": pltpu.VMEM((HS, model), LOW),
        "query": pltpu.VMEM((heads, rows, HS), LOW),
        "gate": pltpu.VMEM((heads, rows, HS), LOW),
        "kv": pltpu.VMEM((heads, tokens, 2 * HS), LOW),
        "pair": pltpu.VMEM((2, 2 * rows, 2 * HS), F32),
        "pair_send": pltpu.VMEM((2 * rows, 2 * HS), LOW),
        "pair_recv": pltpu.VMEM((heads, 2 * rows, 2 * HS), LOW),
        "pair_send_low": pltpu.VMEM((2, rows, 2 * HS), LOW),
        "pair_recv_low": pltpu.VMEM((heads, rows, 2 * HS), LOW),
        "late": pltpu.VMEM((late_count, rows, span), LOW),
        "branch": pltpu.VMEM((rows, model), F32),
        "grad_mlp": pltpu.VMEM((rows, model), F32),
        "grad_attn": pltpu.VMEM((rows, model), F32),
        "sum_send": pltpu.VMEM((bits, rows, model), LOW),
        "sum_recv": pltpu.VMEM((2, bits, rows, model), LOW),
        "small": pltpu.VMEM((steps + 1, 8, small_width), F32),
        "small_recv": pltpu.VMEM((steps, 8, small_width), F32),
        "load_sem": dma((5,)),
        "part_send": dma((2, 3, 4)),
        "part_recv": dma((2, 3, 4)),
        "stats_send": dma((3,)),
        "stats_recv": dma((3,)),
        "ctx_send": dma((RING, 3)),
        "ctx_recv": dma((RING, 3)),
        "dp_send": dma((RING, 2)),
        "dp_recv": dma((RING, 2)),
        "out_sem": dma((2,)),
        "kv_send": dma((heads, 5)),
        "kv_recv": dma((heads, 5)),
        "sum_sems": dma((2, 2, bits)),
        "small_sems": dma((2, steps)),
        "free": pltpu.SemaphoreType.REGULAR((4,)),
    }
    names = [*inputs, *outputs, *scratch]
    results = pl.pallas_call(
        functools.partial(layer_kernel, plan, names),
        out_shape=[jax.ShapeDtypeStruct(shape, kind) for shape, kind, _ in outputs.values()],
        in_specs=[spec for _, spec in inputs.values()],
        out_specs=[spec for _, _, spec in outputs.values()],
        scratch_shapes=list(scratch.values()),
        compiler_params=pltpu.CompilerParams(
            collective_id=0, has_side_effects=True, vmem_limit_bytes=63 << 20
        ),
        name="layer",
    )(*[array for array, _ in inputs.values()])
    layer_out, input_grad, small, down_grad, up_grad, dense_grad, qkv_grad = results
    shape = (seq_count, rows, model)
    out_bias_sum = small[2, :model]
    return (
        layer_out.reshape(shape),
        input_grad.reshape(shape),
        small[0, :model],
        small[0, model : 2 * model],
        qkv_grad,
        small[3, : heads * 3 * HS],
        dense_grad,
        out_bias_sum,
        small[1, :model],
        small[1, model : 2 * model],
        up_grad,
        small[4, :units],
        down_grad,
        out_bias_sum,
    )


def solution(mesh):
    return jax.shard_map(
        local,
        mesh=mesh,
        in_specs=(
            P("dp", "ctx", None),
            P(),
            P(),
            P(None, "tensor"),
            P("tensor"),
            P("tensor", None),
            P(),
            P(),
            P(),
            P(None, "tensor"),
            P("tensor"),
            P("tensor", None),
            P(),
            P("dp", "ctx", None),
            P("dp", "ctx"),
            P(),
        ),
        out_specs=(
            P("dp", "ctx", None),
            P("dp", "ctx", None),
            P(),
            P(),
            P(("dp", "ctx"), "tensor"),
            P("tensor"),
            P("tensor", ("dp", "ctx")),
            P(),
            P(),
            P(),
            P(("dp", "ctx"), "tensor"),
            P("tensor"),
            P("tensor", ("dp", "ctx")),
            P(),
        ),
        check_vma=False,
    )
```

```python
import functools
import math
import types

import jax
import jax.numpy as jnp
from jax import lax
from jax.experimental import pallas as pl
from jax.experimental.pallas import tpu as pltpu
from jax.sharding import PartitionSpec as P

HS = 256
ROT = 64
LANES = 128
RING = 8
NORM_EPS = 1e-05
MESH = pl.DeviceIdType.MESH
ORDER = (0, 2, 1, 3)
LOW = jnp.bfloat16
F32 = jnp.float32


def flip(place, bits):
    bit = 1
    while bit <= bits:
        if bits & bit:
            place = place + bit - 2 * bit * ((place // bit) % 2)
        bit *= 2
    return place


def send_to(source, target, send_sem, recv_sem, axis, bits):
    return pltpu.make_async_remote_copy(
        src_ref=source,
        dst_ref=target,
        send_sem=send_sem,
        recv_sem=recv_sem,
        device_id={axis: flip(lax.axis_index(axis), bits)},
        device_id_type=MESH,
    )


def dot(left, right):
    return jnp.dot(left, right, preferred_element_type=F32)


def dot_rows(left, right):
    return lax.dot_general(left, right, (((1,), (1,)), ((), ())), preferred_element_type=F32)


def axis_bits(axis):
    return [1 << level for level in range(lax.axis_size(axis).bit_length() - 1)]


def blocks_of(total, size):
    return pl.ds(pl.multiple_of(total * size, size), size)


def layer_kernel(plan, names, *refs):
    at = types.SimpleNamespace(**dict(zip(names, refs)))
    rows, span, count, width = plan.rows, plan.span, plan.count, plan.width
    pairs, heads, late = plan.pairs, plan.heads, 2 * plan.pairs
    attn_pieces = heads * HS // span
    per_piece = span // HS
    model = at.hidden.shape[1]
    ctx, dp = lax.axis_index("ctx"), lax.axis_index("dp")
    own_rows = pl.ds(0, rows)
    tensor_bits = axis_bits("tensor")
    halving = (("ctx", 1), ("ctx", 2), ("dp", 1), ("dp", 2))
    small_steps = halving + tuple(("tensor", bit) for bit in tensor_bits)
    scale = 1.0 / math.sqrt(HS)

    def up_load(piece):
        return pltpu.make_async_copy(
            at.up_weight.at[:, blocks_of(piece, span)], at.up_held, at.load_sem.at[0]
        )

    def down_load(piece):
        return pltpu.make_async_copy(
            at.down_weight.at[blocks_of(piece, span)], at.down_held, at.load_sem.at[1]
        )

    def qkv_load(head):
        return pltpu.make_async_copy(
            at.qkv_weight.at[:, blocks_of(head, 3 * HS)], at.qkv_held, at.load_sem.at[2]
        )

    def gate_load(head):
        return pltpu.make_async_copy(
            at.dense_weight.at[blocks_of(head, HS)], at.gate_held, at.load_sem.at[3]
        )

    def dense_load(head):
        return pltpu.make_async_copy(
            at.dense_weight.at[blocks_of(head, HS)], at.dense_held, at.load_sem.at[4]
        )

    def part_copy(kind, place, block):
        source = (at.low, at.hidden)[kind]
        target = (at.low_part, at.hidden_part)[kind]
        column = block * 4 + flip(ctx, place)
        return send_to(
            source.at[:, blocks_of(column, width)],
            target.at[pl.ds(ORDER.index(place) * rows, rows), pl.ds(block * width, width)],
            at.part_send.at[kind, place - 1, block],
            at.part_recv.at[kind, place - 1, block],
            "ctx",
            place,
        )

    def stats_copy(place):
        return send_to(
            at.stats_line.at[0],
            at.stats_line.at[ORDER.index(place)],
            at.stats_send.at[place - 1],
            at.stats_recv.at[place - 1],
            "ctx",
            place,
        )

    def across(piece):
        slot = piece % RING
        return send_to(
            at.rows_all.at[slot, own_rows],
            at.rows_all.at[slot, pl.ds(rows, rows)],
            at.ctx_send.at[slot, 0],
            at.ctx_recv.at[slot, 0],
            "ctx",
            2,
        )

    def beside(piece, part):
        slot = piece % RING
        return send_to(
            at.rows_all.at[slot, pl.ds(part * rows, rows)],
            at.rows_all.at[slot, pl.ds((2 + part) * rows, rows)],
            at.ctx_send.at[slot, 1 + part],
            at.ctx_recv.at[slot, 1 + part],
            "ctx",
            1,
        )

    def first(piece):
        return send_to(
            at.first_send.at[piece % 3],
            at.first_recv.at[piece % RING],
            at.dp_send.at[piece % RING, 0],
            at.dp_recv.at[piece % RING, 0],
            "dp",
            1,
        )

    def second(piece):
        return send_to(
            at.second_send.at[piece % 3],
            at.second_recv.at[piece % RING],
            at.dp_send.at[piece % RING, 1],
            at.dp_recv.at[piece % RING, 1],
            "dp",
            2,
        )

    def is_given(piece):
        return (piece < 4) | ((piece >= 8) & (piece % 4 < 2))

    def results(piece):
        slot = piece % 2
        turned, plain = at.turned.at[slot], at.plain.at[slot]
        feed = piece < late
        pair = jnp.where(piece < 8, piece % 4, piece // 4 * 2 + piece % 2)
        gives = is_given(piece)
        dense = (piece >= late) & (piece < late + attn_pieces)
        return (
            (feed & gives, turned, at.down_out.at[blocks_of(pair, span)]),
            (feed & jnp.logical_not(gives), plain, at.up_out.at[:, blocks_of(pair, span)]),
            (dense, turned, at.dense_out.at[blocks_of(piece - late, span)]),
            (
                piece >= late + attn_pieces,
                plain,
                at.qkv_out.at[:, blocks_of(piece - late - attn_pieces, span)],
            ),
        )

    def for_result(piece, act):
        for holds, source, target in results(piece):

            @pl.when(holds)
            def _():
                act(pltpu.make_async_copy(source, target, at.out_sem.at[piece % 2]))

    def kv_across(head):
        return send_to(
            at.kv.at[head, own_rows],
            at.kv.at[head, pl.ds(rows, rows)],
            at.kv_send.at[head, 0],
            at.kv_recv.at[head, 0],
            "ctx",
            2,
        )

    def kv_beside(head, part):
        return send_to(
            at.kv.at[head, pl.ds(part * rows, rows)],
            at.kv.at[head, pl.ds((2 + part) * rows, rows)],
            at.kv_send.at[head, 1 + part],
            at.kv_recv.at[head, 1 + part],
            "ctx",
            1,
        )

    def pair_beside(head):
        return send_to(
            at.pair_send,
            at.pair_recv.at[head],
            at.kv_send.at[head, 3],
            at.kv_recv.at[head, 3],
            "ctx",
            1,
        )

    def pair_across(head):
        return send_to(
            at.pair_send_low,
            at.pair_recv_low.at[head],
            at.kv_send.at[head, 4],
            at.kv_recv.at[head, 4],
            "ctx",
            2,
        )

    def tensor_copy(which, level):
        return send_to(
            at.sum_send.at[level],
            at.sum_recv.at[which, level],
            at.sum_sems.at[0, which, level],
            at.sum_sems.at[1, which, level],
            "tensor",
            tensor_bits[level],
        )

    def small_copy(entry):
        axis, bit = small_steps[entry]
        return send_to(
            at.small.at[entry],
            at.small_recv.at[entry],
            at.small_sems.at[0, entry],
            at.small_sems.at[1, entry],
            axis,
            bit,
        )

    def turn(heads_rows, back):
        start_part = heads_rows[:, :LANES]
        ahead = pltpu.roll(start_part, LANES - ROT // 2, 1) * at.sine_ahead[...]
        behind = pltpu.roll(start_part, ROT // 2, 1) * at.sine_behind[...]
        straight = start_part * at.cosine[...]
        moved = straight - ahead - behind if back else straight + ahead + behind
        return jnp.concatenate([moved, heads_rows[:, LANES:]], 1)

    def late_block(block):
        piece = attn_pieces + block // per_piece
        return at.late.at[piece, :, blocks_of(block % per_piece, HS)]

    up_load(0).start()
    down_load(0).start()
    qkv_load(0).start()
    gate_load(0).start()
    dense_load(0).start()
    barrier = pltpu.get_barrier_semaphore()
    partners = small_steps + (("ctx", 3),)
    for axis, bits in partners:
        pl.semaphore_signal(
            barrier,
            1,
            device_id={axis: flip(lax.axis_index(axis), bits)},
            device_id_type=MESH,
        )
    pl.semaphore_wait(barrier, len(partners))
    step_rows = 32
    at.small[0] = jnp.zeros_like(at.small[0])
    ids = at.subset_ids[...]
    weight_line = jnp.zeros(ids.shape, F32)
    for number in range(at.subset_weights.shape[0]):
        weight_line = jnp.where(ids == number, at.subset_weights[number], weight_line)
    at.row_weight[...] = jnp.broadcast_to(weight_line, (LANES, rows)).T

    def grad_of(some):
        return at.cotangent[some].astype(F32) * at.row_weight[some, pl.ds(0, 1)]

    @pl.loop(0, rows // step_rows)
    def _(block):
        some = blocks_of(block, step_rows)
        at.low[some] = grad_of(some).astype(LOW)

    for place in (2, 3, 1):
        for block in range(4):
            part_copy(0, place, block).start()

    @pl.loop(0, rows // step_rows)
    def _(block):
        some = blocks_of(block, step_rows)
        inputs = at.hidden[some].astype(F32)
        mean = jnp.mean(inputs, -1, keepdims=True)
        centered = inputs - mean
        inv_std = lax.rsqrt(jnp.mean(centered * centered, -1, keepdims=True) + NORM_EPS)
        normed = centered * inv_std
        at.attn_in[some] = (normed * at.attn_gain[...] + at.attn_bias[...]).astype(LOW)
        at.mlp_in[some] = (normed * at.mlp_gain[...] + at.mlp_bias[...]).astype(LOW)
        lane = lax.broadcasted_iota(jnp.int32, (step_rows, LANES), 1)
        at.stats[some] = jnp.where(lane < LANES // 2, mean, inv_std)

    def send_hidden():
        line = at.stats[own_rows].T
        at.stats_line[0, pl.ds(0, 8)] = line[:8]
        at.stats_line[0, pl.ds(8, 8)] = line[LANES // 2 : LANES // 2 + 8]
        for place in (2, 3, 1):
            stats_copy(place).start()
            for block in range(4):
                part_copy(1, place, block).start()
        for block in range(4):
            column = blocks_of(block * 4 + ctx, width)
            at.hidden_part[own_rows, pl.ds(block * width, width)] = at.hidden[:, column]

    def low_left():
        for block in range(4):
            column = blocks_of(block * 4 + ctx, width)
            at.low_part[own_rows, pl.ds(block * width, width)] = at.low[:, column]
        for place in (1, 2, 3):
            for block in range(4):
                part_copy(0, place, block).wait_recv()
        for entry, bits in enumerate(ORDER):
            block = at.low_part[:, blocks_of(flip(dp, bits), width)]
            at.left[0, pl.ds(entry * width, width)] = block.T

    def hidden_left():
        for place in (1, 2, 3):
            stats_copy(place).wait_recv()
            for block in range(4):
                part_copy(1, place, block).wait_recv()
        for slot in range(1, 4):
            half = lax.broadcasted_iota(jnp.int32, (LANES, rows), 0) < LANES // 2
            line = jnp.where(half, at.stats_line[slot, :1], at.stats_line[slot, 8:9])
            at.stats[pl.ds(slot * rows, rows)] = line.T
        for entry, bits in enumerate(ORDER):
            place = flip(dp, bits)
            block = at.hidden_part[:, blocks_of(place, width)].astype(F32)
            normed = (block - at.stats[:, :1]) * at.stats[:, LANES // 2 : LANES // 2 + 1]
            column = blocks_of(place * 4 + ctx, width)
            to = pl.ds(entry * width, width)
            sides = ((at.mlp_gain, at.mlp_bias), (at.attn_gain, at.attn_bias))
            for number, (gain, bias) in enumerate(sides):
                at.left[1 + number, to] = (normed * gain[:, column] + bias[:, column]).astype(LOW).T

    def start_piece(piece):
        @pl.when(piece >= RING)
        def _():
            pl.semaphore_wait(at.free.at[0], 1)
            pl.semaphore_wait(at.free.at[1], 1)

        @pl.when(piece >= late)
        def _():
            at.rows_all[piece % RING, own_rows] = at.late[piece - late]

        across(piece).start()
        beside(piece, 0).start()

    def feed_forward(pair):
        up_load(pair).wait()
        down_load(pair).wait()
        pre = dot(at.mlp_in[...], at.up_held[...]) + at.up_bias[:, blocks_of(pair, span)]
        cumulative = 0.5 * (1.0 + lax.erf(pre * math.sqrt(0.5)))
        feed_piece = jnp.where(pair < 4, pair, pair // 2 * 4 + pair % 2)
        grad_piece = feed_piece + jnp.where(pair < 4, 4, 2)
        at.rows_all[feed_piece % RING, own_rows] = (pre * cumulative).astype(LOW)
        start_piece(feed_piece)
        grad_act = dot_rows(at.low[...], at.down_held[...])
        density = jnp.exp(-0.5 * pre * pre) * (1.0 / math.sqrt(2.0 * math.pi))
        grad_pre = (grad_act * (cumulative + pre * density)).astype(LOW)
        at.rows_all[grad_piece % RING, own_rows] = grad_pre
        at.small[0, pl.ds(4, 1), blocks_of(pair, span)] = jnp.sum(
            grad_pre.astype(F32), 0, keepdims=True
        )
        @pl.when(pair == 3)
        def _():
            send_hidden()

        @pl.when(pair == 0)
        def _():
            for held in (at.branch, at.grad_mlp, at.grad_attn):
                held[...] = jnp.zeros_like(held)

        at.branch[...] += dot(at.rows_all[feed_piece % RING, own_rows], at.down_held[...])
        at.grad_mlp[...] += dot_rows(at.rows_all[grad_piece % RING, own_rows], at.up_held[...])

        @pl.when(pair + 1 < pairs)
        def _():
            up_load(pair + 1).start()
            down_load(pair + 1).start()

    def project(head):
        qkv_load(head).wait()
        out = dot(at.attn_in[...], at.qkv_held[...]) + at.qkv_bias[:, blocks_of(head, 3 * HS)]
        at.kv[head, own_rows, pl.ds(0, HS)] = turn(out[:, HS : 2 * HS], False).astype(LOW)
        at.kv[head, own_rows, pl.ds(HS, HS)] = out[:, 2 * HS :].astype(LOW)

        @pl.when(ctx < 2)
        def _():
            kv_across(head).start()

        kv_beside(head, 0).start()
        at.query[head] = turn(out[:, :HS], False).astype(LOW)
        gate_load(head).wait()
        at.gate[head] = dot_rows(at.low[...], at.gate_held[...]).astype(LOW)
        qkv_load((head + 1) % heads).start()

        @pl.when(head + 1 < heads)
        def _():
            gate_load(head + 1).start()

    def kv_forward(head):
        @pl.when(ctx >= 2)
        def _():
            kv_across(head).wait_recv()
            kv_beside(head, 1).start()

        @pl.when(ctx < 2)
        def _():
            for slot in (1, 3):
                at.kv[head, pl.ds(slot * rows, rows)] = jnp.zeros((rows, 2 * HS), LOW)

    def attend(head):
        kv_beside(head, 0).wait_recv()

        @pl.when(ctx >= 2)
        def _():
            kv_beside(head, 1).wait_recv()

        query, gate = at.query[head], at.gate[head]
        keys, values = at.kv[head, :, :HS], at.kv[head, :, HS:]
        shape = (rows, 4 * rows)
        key_place = lax.broadcasted_iota(jnp.int32, shape, 1)
        shift = jnp.full(shape, flip(ctx, ORDER[3]) * rows - 3 * rows, jnp.int32)
        for entry in (2, 1, 0):
            here = flip(ctx, ORDER[entry]) * rows - entry * rows
            shift = jnp.where(key_place < (entry + 1) * rows, here, shift)
        query_place = lax.broadcasted_iota(jnp.int32, shape, 0) + ctx * rows
        scores = jnp.where(
            key_place + shift <= query_place, dot_rows(query, keys) * scale, -1e30
        )
        expd = jnp.exp(scores - jnp.max(scores, -1, keepdims=True))
        prob = expd * (1.0 / jnp.sum(expd, -1, keepdims=True))
        prob_low = prob.astype(LOW)
        attended = dot(prob_low, values).astype(LOW)
        at.late[head // per_piece, :, blocks_of(head % per_piece, HS)] = attended
        grad_prob = dot_rows(gate, values)
        delta = jnp.sum(grad_prob * prob, -1, keepdims=True)
        grad_scores = (prob * (grad_prob - delta)).astype(LOW)
        grad_key = dot(grad_scores.T, query) * scale
        grad_value = dot(prob_low.T, gate)
        at.pair_send[:, pl.ds(0, HS)] = grad_key[2 * rows :].astype(LOW)
        at.pair_send[:, pl.ds(HS, HS)] = grad_value[2 * rows :].astype(LOW)
        pair_beside(head).start()
        at.pair[:, pl.ds(0, HS)] = grad_key[: 2 * rows]
        at.pair[:, pl.ds(HS, HS)] = grad_value[: 2 * rows]
        late_block(3 * head)[...] = turn(dot(grad_scores, keys) * scale, True).astype(LOW)
        dense_load(head).wait()
        at.branch[...] += dot(attended, at.dense_held[...])

        @pl.when(head + 1 < heads)
        def _():
            dense_load(head + 1).start()

    def pair_halve(head):
        pair_beside(head).wait()

        @pl.when(ctx >= 2)
        def _():
            other = pl.ds(rows, rows)
            at.pair_send_low[...] = (
                at.pair[other] + at.pair_recv[head, other].astype(F32)
            ).astype(LOW)
            pair_across(head).start()

        at.pair_own[...] = at.pair[own_rows] + at.pair_recv[head, own_rows].astype(F32)

    def pair_finish(head):
        @pl.when(ctx < 2)
        def _():
            pair_across(head).wait_recv()
            at.pair_own[...] += at.pair_recv_low[head].astype(F32)

        @pl.when(ctx >= 2)
        def _():
            pair_across(head).wait_send()

        total = at.pair_own[...]
        late_block(3 * head + 1)[...] = turn(total[:, :HS], True).astype(LOW)
        late_block(3 * head + 2)[...] = total[:, HS:].astype(LOW)
        for number in range(3):
            at.small[0, pl.ds(3, 1), blocks_of(3 * head + number, HS)] = jnp.sum(
                late_block(3 * head + number)[...].astype(F32), 0, keepdims=True
            )

    def project_back(head):
        qkv_load(head).wait()
        at.grad_attn[...] += (
            dot_rows(late_block(3 * head)[...], at.qkv_held[:, :HS])
            + dot_rows(late_block(3 * head + 1)[...], at.qkv_held[:, HS : 2 * HS])
            + dot_rows(late_block(3 * head + 2)[...], at.qkv_held[:, 2 * HS :])
        )

        @pl.when(head + 1 < heads)
        def _():
            qkv_load(head + 1).start()

    def branch_send():
        at.sum_send[0] = at.branch[...].astype(LOW)
        tensor_copy(0, 0).start()

    def tensor_step(which, level):
        tensor_copy(which, level).wait()
        if level + 1 < len(tensor_bits):
            at.sum_send[level + 1] = (
                at.sum_send[level].astype(F32) + at.sum_recv[which, level].astype(F32)
            ).astype(LOW)
            tensor_copy(which, level + 1).start()
            return

        @pl.loop(0, rows // step_rows)
        def _(block):
            some = blocks_of(block, step_rows)
            total = at.sum_send[level, some].astype(F32) + at.sum_recv[which, level, some].astype(
                F32
            )
            if which == 0:
                total = (
                    at.hidden[some].astype(F32) + total + at.dense_bias[...] + at.down_bias[...]
                )
                at.mlp_in[some] = total.astype(LOW)
            else:
                at.attn_in[some] = (grad_of(some) + total).astype(LOW)

        row_result(which).start()

    def row_result(which):
        source = (at.mlp_in, at.attn_in)[which]
        target = (at.layer_out, at.input_grad)[which]
        return pltpu.make_async_copy(source, target, at.row_sem.at[which])

    def norm_back():
        @pl.loop(0, rows // step_rows)
        def _(block):
            some = blocks_of(block, step_rows)
            stats = at.stats[some]
            inv_std = stats[:, LANES // 2 : LANES // 2 + 1]
            normed = (at.hidden[some].astype(F32) - stats[:, :1]) * inv_std
            grad_attn, grad_mlp = at.grad_attn[some], at.grad_mlp[some]
            at.small[0, pl.ds(2, 1), pl.ds(0, model)] += jnp.sum(grad_of(some), 0, keepdims=True)
            for row, grad in enumerate((grad_attn, grad_mlp)):
                at.small[0, pl.ds(row, 1), pl.ds(0, model)] += jnp.sum(
                    grad * normed, 0, keepdims=True
                )
                at.small[0, pl.ds(row, 1), pl.ds(model, model)] += jnp.sum(grad, 0, keepdims=True)
            grad = grad_attn * at.attn_gain[...] + grad_mlp * at.mlp_gain[...]
            part = inv_std * (
                grad
                - jnp.mean(grad, -1, keepdims=True)
                - normed * jnp.mean(grad * normed, -1, keepdims=True)
            )
            at.sum_send[0, some] = part.astype(LOW)

        tensor_copy(1, 0).start()
        small_copy(0).start()

    def small_step(entry):
        small_copy(entry).wait()
        if small_steps[entry][0] == "tensor":
            both, rest = pl.ds(0, 2), pl.ds(2, at.small.shape[1] - 2)
            at.small[entry + 1, both] = at.small[entry, both] + at.small_recv[entry, both]
            at.small[entry + 1, rest] = at.small[entry, rest]
        else:
            at.small[entry + 1] = at.small[entry] + at.small_recv[entry]
        if entry + 1 < len(small_steps):
            small_copy(entry + 1).start()
        else:
            at.small_out[...] = at.small[entry + 1]

    lead, grad_lead = 3, 4
    assert pairs % 2 == 0 and pairs >= 4

    def places(*lags):
        return [
            [2 + 2 * head + sum(lags[:stage]) for stage in range(5)] for head in range(heads)
        ]

    def in_time(jobs):
        for piece in range(attn_pieces):
            if jobs[(piece + 1) * per_piece - 1][2] > late + piece - lead:
                return False
        for block in range(3 * heads):
            if jobs[block // 3][4] > late + attn_pieces + block // per_piece - lead:
                return False
        return True

    jobs = next(pace for pace in (places(4, 2, 2, 2), places(1, 1, 1, 1)) if in_time(pace))
    project_at, forward_at, attend_at, halve_at, finish_at = jobs[0]
    feed_end = max(2 * (pairs - 1) - 5, 1)
    branch_at = max(attend_at + 2 * (heads - 1), feed_end) + 1
    back_at = max(finish_at + 2 * (heads - 1) + 2, branch_at + 3 * len(tensor_bits) + 1)
    total_steps = max(
        count + 5, back_at + 1 + len(small_steps), back_at + 3 * len(tensor_bits) + 1
    )

    def step(turn_number, carry):
        now = turn_number - 2

        def job(start, stride, times, act):
            index = now - start

            @pl.when((index >= 0) & (index < stride * times) & (index % stride == 0))
            def _():
                act(index // stride)

        multiply = now - 1

        @pl.when((multiply >= 0) & (multiply < count))
        def _():
            beside(multiply, 0).wait_recv()
            beside(multiply, 1).wait_recv()

            @pl.when(multiply >= RING)
            def _():
                pl.semaphore_wait(at.free.at[2], 1)

            @pl.when(multiply >= 3)
            def _():
                first(multiply - 3).wait_send()

            feed = multiply < late
            group = jnp.where(
                feed,
                jnp.where(is_given(multiply), 0, 1),
                jnp.where(multiply < late + attn_pieces, 0, 2),
            )
            at.first_send[multiply % 3] = dot(
                at.left[group, pl.ds(2 * width, 2 * width)], at.rows_all[multiply % RING]
            ).astype(LOW)
            first(multiply).start()
            at.held[multiply % 5] = dot(
                at.left[group, pl.ds(0, 2 * width)], at.rows_all[multiply % RING]
            )

        add = now - 3

        @pl.when((add >= 0) & (add < count))
        def _():
            first(add).wait_recv()

            @pl.when(add >= RING)
            def _():
                pl.semaphore_wait(at.free.at[3], 1)

            @pl.when(add >= 3)
            def _():
                second(add - 3).wait_send()

            lower = pl.ds(width, width)
            at.second_send[add % 3] = (
                at.held[add % 5, lower] + at.first_recv[add % RING, lower].astype(F32)
            ).astype(LOW)
            second(add).start()

        last = now - 5

        @pl.when((last >= 0) & (last < count))
        def _():
            second(last).wait_recv()

            @pl.when(last >= 2)
            def _():
                for_result(last - 2, lambda copy: copy.wait())

            upper = pl.ds(0, width)
            total = (
                at.held[last % 5, upper]
                + at.first_recv[last % RING, upper].astype(F32)
                + at.second_recv[last % RING].astype(F32)
            )
            flat = ((last < late) & jnp.logical_not(is_given(last))) | (last >= late + attn_pieces)

            @pl.when(flat)
            def _():
                at.plain[last % 2] = total

            @pl.when(jnp.logical_not(flat))
            def _():
                at.turned[last % 2] = total.T

            for_result(last, lambda copy: copy.start())

            @pl.when(last < count - RING)
            def _():
                for number, bit in ((2, 1), (3, 2)):
                    pl.semaphore_signal(
                        at.free.at[number],
                        1,
                        device_id={"dp": flip(dp, bit)},
                        device_id_type=MESH,
                    )

        @pl.when((now >= 0) & (now < count))
        def _():
            across(now).wait_recv()
            beside(now, 1).start()

        sent = now - 1

        @pl.when((sent >= 0) & (sent < count))
        def _():
            across(sent).wait_send()
            beside(sent, 0).wait_send()
            beside(sent, 1).wait_send()

            @pl.when(sent < count - RING)
            def _():
                for number, bit in ((0, 2), (1, 1)):
                    pl.semaphore_signal(
                        at.free.at[number],
                        1,
                        device_id={"ctx": flip(ctx, bit)},
                        device_id_type=MESH,
                    )

        job(4, 1, 1, lambda _: hidden_left())

        @pl.when(now == 2)
        def _():
            for piece in range(4, 8):
                start_piece(piece)

        grads = now + grad_lead

        @pl.when((grads >= 8) & (grads < late) & (grads % 4 >= 2))
        def _():
            start_piece(grads)

        @pl.when((now < 2) | ((now % 2 == 1) & (now < 2 * pairs - 5)))
        def _():
            feed_forward(jnp.where(now < 2, now + 2, (now + 5) // 2))

        job(-1, 1, 1, lambda _: low_left())
        job(project_at, 2, heads, project)
        job(forward_at, 2, heads, kv_forward)
        job(finish_at, 2, heads, pair_finish)
        job(halve_at, 2, heads, pair_halve)
        job(attend_at, 2, heads, attend)
        job(finish_at + 1, 2, heads, project_back)
        job(branch_at, 1, 1, lambda _: branch_send())
        for level in range(len(tensor_bits)):
            job(branch_at + 3 * (level + 1), 1, 1, lambda _: tensor_step(0, level))
        job(back_at, 1, 1, lambda _: norm_back())
        for level in range(len(tensor_bits)):
            job(back_at + 3 * (level + 1), 1, 1, lambda _: tensor_step(1, level))
        for entry in range(len(small_steps)):
            job(back_at + 1 + entry, 1, 1, lambda _: small_step(entry))

        @pl.when((now + lead >= late) & (now + lead < count))
        def _():
            start_piece(now + lead)

        return carry

    lax.fori_loop(0, total_steps + 2, step, 0)

    for place in (1, 2, 3):
        stats_copy(place).wait_send()
        for kind in range(2):
            for block in range(4):
                part_copy(kind, place, block).wait_send()

    @pl.loop(0, heads)
    def _(head):
        kv_beside(head, 0).wait_send()

        @pl.when(ctx < 2)
        def _():
            kv_across(head).wait_send()

        @pl.when(ctx >= 2)
        def _():
            kv_beside(head, 1).wait_send()

    @pl.loop(count - 3, count)
    def _(piece):
        first(piece).wait_send()
        second(piece).wait_send()

        @pl.when(piece >= count - 2)
        def _():
            for_result(piece, lambda copy: copy.wait())

    row_result(0).wait()
    row_result(1).wait()


def hand_on(cuts, *refs):
    whole = 6
    sources, small = refs[:whole], refs[whole]
    targets, refs = refs[whole + 1 : 2 * whole + 1], refs[2 * whole + 1 :]
    pieces, refs = refs[: len(cuts)], refs[len(cuts) :]
    held, sem = refs[:whole], refs[whole]

    def halves(ref):
        size = ref.shape[0] // 2
        return [ref.at[pl.ds(half * size, size)] for half in range(2)]

    copies = []
    for number in range(whole):
        parts = zip(halves(sources[number]), halves(held[number]), halves(targets[number]))
        for half, (source, middle, target) in enumerate(parts):
            copies.append(
                (
                    pltpu.make_async_copy(source, middle, sem.at[0, number, half]),
                    pltpu.make_async_copy(middle, target, sem.at[1, number, half]),
                )
            )
    for fetch, _ in copies:
        fetch.start()
    for piece, (row, low, high) in zip(pieces, cuts):
        piece[...] = small[row : row + 1, low:high]
    for fetch, put in copies:
        fetch.wait()
        put.start()
    for _, put in copies:
        put.wait()


def local(
    hidden_in,
    attn_norm_gain,
    attn_norm_bias,
    qkv_weight,
    qkv_bias,
    dense_weight,
    dense_bias,
    mlp_norm_gain,
    mlp_norm_bias,
    up_weight,
    up_bias,
    down_weight,
    down_bias,
    out_cotangent,
    subset_ids,
    subset_weights,
):
    seq_count, rows, model = hidden_in.shape
    heads = qkv_weight.shape[1] // (3 * HS)
    units = up_weight.shape[1]
    width = model // (lax.axis_size("dp") * lax.axis_size("ctx"))
    span = min(512, math.gcd(units, heads * HS, heads * 3 * HS))
    pairs = units // span
    late_count = heads * 4 * HS // span
    plan = types.SimpleNamespace(
        rows=rows, span=span, width=width, pairs=pairs, heads=heads, count=2 * pairs + late_count
    )
    tokens = rows * lax.axis_size("ctx")

    half = ROT // 2
    lane = jnp.arange(LANES, dtype=jnp.int32)[None, :]
    positions = lax.axis_index("ctx") * rows + jnp.arange(rows, dtype=jnp.int32)
    freqs = 10000.0 ** (-((lane % half).astype(F32) * 2.0 / ROT))
    table = positions.astype(F32)[:, None] * freqs
    sine = jnp.sin(table)
    cosine = jnp.where(lane < ROT, jnp.cos(table), 1.0)
    sine_ahead = jnp.where(lane < half, -sine, 0.0)
    sine_behind = jnp.where((lane >= half) & (lane < ROT), sine, 0.0)

    bits = lax.axis_size("tensor").bit_length() - 1
    steps = 4 + bits
    small_width = max(2 * model, units, heads * 3 * HS)
    dma = pltpu.SemaphoreType.DMA
    vmem = pl.BlockSpec(memory_space=pltpu.VMEM)
    hbm = pl.BlockSpec(memory_space=pl.ANY)
    inputs = {
        "hidden": (hidden_in.reshape(rows, model), vmem),
        "cotangent": (out_cotangent.reshape(rows, model), vmem),
        "subset_ids": (subset_ids, vmem),
        "subset_weights": (subset_weights, pl.BlockSpec(memory_space=pltpu.SMEM)),
        "cosine": (cosine, vmem),
        "sine_ahead": (sine_ahead, vmem),
        "sine_behind": (sine_behind, vmem),
        "attn_gain": (attn_norm_gain[None], vmem),
        "attn_bias": (attn_norm_bias[None], vmem),
        "mlp_gain": (mlp_norm_gain[None], vmem),
        "mlp_bias": (mlp_norm_bias[None], vmem),
        "dense_bias": (dense_bias[None], vmem),
        "down_bias": (down_bias[None], vmem),
        "qkv_bias": (qkv_bias[None], vmem),
        "up_bias": (up_bias[None], vmem),
        "qkv_weight": (qkv_weight, hbm),
        "dense_weight": (dense_weight, hbm),
        "up_weight": (up_weight, hbm),
        "down_weight": (down_weight, hbm),
    }
    outputs = {
        "layer_out": ((rows, model), LOW, hbm),
        "input_grad": ((rows, model), LOW, hbm),
        "small_out": ((8, small_width), F32, vmem),
        "down_out": ((units, width), F32, hbm),
        "up_out": ((width, units), F32, hbm),
        "dense_out": ((heads * HS, width), F32, hbm),
        "qkv_out": ((width, heads * 3 * HS), F32, hbm),
    }
    scratch = {
        "rows_all": pltpu.VMEM((RING, tokens, span), LOW),
        "first_send": pltpu.VMEM((3, 2 * width, span), LOW),
        "first_recv": pltpu.VMEM((RING, 2 * width, span), LOW),
        "second_send": pltpu.VMEM((3, width, span), LOW),
        "second_recv": pltpu.VMEM((RING, width, span), LOW),
        "held": pltpu.VMEM((5, 2 * width, span), F32),
        "plain": pltpu.VMEM((2, width, span), F32),
        "turned": pltpu.VMEM((2, span, width), F32),
        "left": pltpu.VMEM((3, 4 * width, tokens), LOW),
        "low_part": pltpu.VMEM((tokens, 4 * width), LOW),
        "hidden_part": pltpu.VMEM((tokens, 4 * width), LOW),
        "stats": pltpu.VMEM((tokens, LANES), F32),
        "stats_line": pltpu.VMEM((4, 16, rows), F32),
        "row_weight": pltpu.VMEM((rows, LANES), F32),
        "attn_in": pltpu.VMEM((rows, model), LOW),
        "mlp_in": pltpu.VMEM((rows, model), LOW),
        "low": pltpu.VMEM((rows, model), LOW),
        "up_held": pltpu.VMEM((model, span), LOW),
        "down_held": pltpu.VMEM((span, model), LOW),
        "qkv_held": pltpu.VMEM((model, 3 * HS), LOW),
        "gate_held": pltpu.VMEM((HS, model), LOW),
        "dense_held": pltpu.VMEM((HS, model), LOW),
        "query": pltpu.VMEM((heads, rows, HS), LOW),
        "gate": pltpu.VMEM((heads, rows, HS), LOW),
        "kv": pltpu.VMEM((heads, tokens, 2 * HS), LOW),
        "pair": pltpu.VMEM((2 * rows, 2 * HS), F32),
        "pair_own": pltpu.VMEM((rows, 2 * HS), F32),
        "pair_send": pltpu.VMEM((2 * rows, 2 * HS), LOW),
        "pair_recv": pltpu.VMEM((heads, 2 * rows, 2 * HS), LOW),
        "pair_send_low": pltpu.VMEM((rows, 2 * HS), LOW),
        "pair_recv_low": pltpu.VMEM((heads, rows, 2 * HS), LOW),
        "late": pltpu.VMEM((late_count, rows, span), LOW),
        "branch": pltpu.VMEM((rows, model), F32),
        "grad_mlp": pltpu.VMEM((rows, model), F32),
        "grad_attn": pltpu.VMEM((rows, model), F32),
        "sum_send": pltpu.VMEM((bits, rows, model), LOW),
        "sum_recv": pltpu.VMEM((2, bits, rows, model), LOW),
        "small": pltpu.VMEM((steps + 1, 8, small_width), F32),
        "small_recv": pltpu.VMEM((steps, 8, small_width), F32),
        "load_sem": dma((5,)),
        "part_send": dma((2, 3, 4)),
        "part_recv": dma((2, 3, 4)),
        "stats_send": dma((3,)),
        "stats_recv": dma((3,)),
        "ctx_send": dma((RING, 3)),
        "ctx_recv": dma((RING, 3)),
        "dp_send": dma((RING, 2)),
        "dp_recv": dma((RING, 2)),
        "out_sem": dma((2,)),
        "row_sem": dma((2,)),
        "kv_send": dma((heads, 5)),
        "kv_recv": dma((heads, 5)),
        "sum_sems": dma((2, 2, bits)),
        "small_sems": dma((2, steps)),
        "free": pltpu.SemaphoreType.REGULAR((4,)),
    }
    names = [*inputs, *outputs, *scratch]
    results = pl.pallas_call(
        functools.partial(layer_kernel, plan, names),
        out_shape=[jax.ShapeDtypeStruct(shape, kind) for shape, kind, _ in outputs.values()],
        in_specs=[spec for _, spec in inputs.values()],
        out_specs=[spec for _, _, spec in outputs.values()],
        scratch_shapes=list(scratch.values()),
        compiler_params=pltpu.CompilerParams(
            collective_id=0, has_side_effects=True, vmem_limit_bytes=63 << 20
        ),
        name="layer",
    )(*[array for array, _ in inputs.values()])
    cuts = [
        (0, 0, model),
        (0, model, 2 * model),
        (1, 0, model),
        (1, model, 2 * model),
        (2, 0, model),
        (2, 0, model),
        (3, 0, heads * 3 * HS),
        (4, 0, units),
    ]
    layer_out, input_grad, small, down_grad, up_grad, dense_grad, qkv_grad = results
    large = [layer_out, input_grad, down_grad, up_grad, dense_grad, qkv_grad]
    shapes = [jax.ShapeDtypeStruct(array.shape, array.dtype) for array in large]
    shapes += [jax.ShapeDtypeStruct((1, high - low), F32) for _, low, high in cuts]
    done = pl.pallas_call(
        functools.partial(hand_on, cuts),
        out_shape=shapes,
        in_specs=[hbm] * len(large) + [vmem],
        out_specs=[hbm] * len(large) + [vmem] * len(cuts),
        scratch_shapes=[pltpu.VMEM(array.shape, array.dtype) for array in large]
        + [dma((2, len(large), 2))],
        compiler_params=pltpu.CompilerParams(vmem_limit_bytes=60 << 20),
        name="hand_on",
    )(*large, small)
    layer_out, input_grad, down_grad, up_grad, dense_grad, qkv_grad = done[:6]
    vectors = [vector.reshape(-1) for vector in done[6:]]
    attn_gain, attn_bias, mlp_gain, mlp_bias, dense_sum, down_sum, qkv_sum, up_sum = vectors
    shape = (seq_count, rows, model)
    return (
        layer_out.reshape(shape),
        input_grad.reshape(shape),
        attn_gain,
        attn_bias,
        qkv_grad,
        qkv_sum,
        dense_grad,
        dense_sum,
        mlp_gain,
        mlp_bias,
        up_grad,
        up_sum,
        down_grad,
        down_sum,
    )


def solution(mesh):
    return jax.shard_map(
        local,
        mesh=mesh,
        in_specs=(
            P("dp", "ctx", None),
            P(),
            P(),
            P(None, "tensor"),
            P("tensor"),
            P("tensor", None),
            P(),
            P(),
            P(),
            P(None, "tensor"),
            P("tensor"),
            P("tensor", None),
            P(),
            P("dp", "ctx", None),
            P("dp", "ctx"),
            P(),
        ),
        out_specs=(
            P("dp", "ctx", None),
            P("dp", "ctx", None),
            P(),
            P(),
            P(("dp", "ctx"), "tensor"),
            P("tensor"),
            P("tensor", ("dp", "ctx")),
            P(),
            P(),
            P(),
            P(("dp", "ctx"), "tensor"),
            P("tensor"),
            P("tensor", ("dp", "ctx")),
            P(),
        ),
        check_vma=False,
    )
```

```python
import functools
import math
import types

import jax
import jax.numpy as jnp
from jax import lax
from jax.experimental import pallas as pl
from jax.experimental.pallas import tpu as pltpu
from jax.sharding import PartitionSpec as P

HS = 256
ROT = 64
LANES = 128
RING = 8
NORM_EPS = 1e-05
MESH = pl.DeviceIdType.MESH
ORDER = (0, 2, 1, 3)
LOW = jnp.bfloat16
F32 = jnp.float32


def flip(place, bits):
    bit = 1
    while bit <= bits:
        if bits & bit:
            place = place + bit - 2 * bit * ((place // bit) % 2)
        bit *= 2
    return place


def send_to(source, target, send_sem, recv_sem, axis, bits):
    return pltpu.make_async_remote_copy(
        src_ref=source,
        dst_ref=target,
        send_sem=send_sem,
        recv_sem=recv_sem,
        device_id={axis: flip(lax.axis_index(axis), bits)},
        device_id_type=MESH,
    )


def dot(left, right):
    return jnp.dot(left, right, preferred_element_type=F32)


def dot_rows(left, right):
    return lax.dot_general(left, right, (((1,), (1,)), ((), ())), preferred_element_type=F32)


def axis_bits(axis):
    return [1 << level for level in range(lax.axis_size(axis).bit_length() - 1)]


def blocks_of(total, size):
    return pl.ds(pl.multiple_of(total * size, size), size)


def layer_kernel(plan, names, *refs):
    at = types.SimpleNamespace(**dict(zip(names, refs)))
    rows, span, count, width = plan.rows, plan.span, plan.count, plan.width
    pairs, heads, late = plan.pairs, plan.heads, 2 * plan.pairs
    attn_pieces = heads * HS // span
    per_piece = span // HS
    model = at.hidden.shape[1]
    ctx, dp = lax.axis_index("ctx"), lax.axis_index("dp")
    own_rows = pl.ds(0, rows)
    tensor_bits = axis_bits("tensor")
    halving = (("ctx", 1), ("ctx", 2), ("dp", 1), ("dp", 2))
    line_steps = halving[2:] + tuple(("tensor", bit) for bit in tensor_bits)
    scale = 1.0 / math.sqrt(HS)

    def up_load(piece):
        return pltpu.make_async_copy(
            at.up_weight.at[:, blocks_of(piece, span)], at.up_held, at.load_sem.at[0]
        )

    def up_load_aside(piece):
        return pltpu.make_async_copy(
            at.up_weight.at[:, blocks_of(piece, span)],
            at.qkv_held.at[:, pl.ds(0, span)],
            at.load_sem.at[2],
        )

    def down_load(piece):
        return pltpu.make_async_copy(
            at.down_weight.at[blocks_of(piece, span)], at.down_held, at.load_sem.at[1]
        )

    def qkv_load(head):
        return pltpu.make_async_copy(
            at.qkv_weight.at[:, blocks_of(head, 3 * HS)], at.qkv_held, at.load_sem.at[2]
        )

    def gate_load(head):
        return pltpu.make_async_copy(
            at.dense_weight.at[blocks_of(head, HS)], at.gate_held, at.load_sem.at[3]
        )

    def dense_load(head):
        return pltpu.make_async_copy(
            at.dense_weight.at[blocks_of(head, HS)], at.dense_held, at.load_sem.at[4]
        )

    def part_copy(kind, place, block):
        source = (at.low, at.hidden)[kind]
        target = (at.low_part, at.hidden_part)[kind]
        column = block * 4 + flip(ctx, place)
        return send_to(
            source.at[:, blocks_of(column, width)],
            target.at[pl.ds(ORDER.index(place) * rows, rows), pl.ds(block * width, width)],
            at.part_send.at[kind, place - 1, block],
            at.part_recv.at[kind, place - 1, block],
            "ctx",
            place,
        )

    def stats_copy(place):
        return send_to(
            at.stats_line.at[0],
            at.stats_line.at[ORDER.index(place)],
            at.stats_send.at[place - 1],
            at.stats_recv.at[place - 1],
            "ctx",
            place,
        )

    def across(piece):
        slot = piece % RING
        return send_to(
            at.rows_all.at[slot, own_rows],
            at.rows_all.at[slot, pl.ds(rows, rows)],
            at.ctx_send.at[slot, 0],
            at.ctx_recv.at[slot, 0],
            "ctx",
            2,
        )

    def beside(piece, part):
        slot = piece % RING
        return send_to(
            at.rows_all.at[slot, pl.ds(part * rows, rows)],
            at.rows_all.at[slot, pl.ds((2 + part) * rows, rows)],
            at.ctx_send.at[slot, 1 + part],
            at.ctx_recv.at[slot, 1 + part],
            "ctx",
            1,
        )

    def first(piece):
        return send_to(
            at.first_send.at[piece % 3],
            at.first_recv.at[piece % RING],
            at.dp_send.at[piece % RING, 0],
            at.dp_recv.at[piece % RING, 0],
            "dp",
            1,
        )

    def second(piece):
        return send_to(
            at.second_send.at[piece % 3],
            at.second_recv.at[piece % RING],
            at.dp_send.at[piece % RING, 1],
            at.dp_recv.at[piece % RING, 1],
            "dp",
            2,
        )

    def is_given(piece):
        return (piece < 4) | ((piece >= 8) & (piece % 4 < 2))

    def results(piece):
        slot = piece % 2
        turned, plain = at.turned.at[slot], at.plain.at[slot]
        feed = piece < late
        pair = jnp.where(piece < 8, piece % 4, piece // 4 * 2 + piece % 2)
        gives = is_given(piece)
        dense = (piece >= late) & (piece < late + attn_pieces)
        return (
            (feed & gives, turned, at.down_out.at[blocks_of(pair, span)]),
            (feed & jnp.logical_not(gives), plain, at.up_out.at[:, blocks_of(pair, span)]),
            (dense, turned, at.dense_out.at[blocks_of(piece - late, span)]),
            (
                piece >= late + attn_pieces,
                plain,
                at.qkv_out.at[:, blocks_of(piece - late - attn_pieces, span)],
            ),
        )

    def for_result(piece, act):
        for holds, source, target in results(piece):

            @pl.when(holds)
            def _():
                act(pltpu.make_async_copy(source, target, at.out_sem.at[piece % 2]))

    def kv_across(head):
        return send_to(
            at.kv.at[head, own_rows],
            at.kv.at[head, pl.ds(rows, rows)],
            at.kv_send.at[head, 0],
            at.kv_recv.at[head, 0],
            "ctx",
            2,
        )

    def kv_beside(head, part):
        return send_to(
            at.kv.at[head, pl.ds(part * rows, rows)],
            at.kv.at[head, pl.ds((2 + part) * rows, rows)],
            at.kv_send.at[head, 1 + part],
            at.kv_recv.at[head, 1 + part],
            "ctx",
            1,
        )

    def pair_beside(head):
        return send_to(
            at.pair_send,
            at.pair_recv.at[head],
            at.kv_send.at[head, 3],
            at.kv_recv.at[head, 3],
            "ctx",
            1,
        )

    def pair_across(head):
        return send_to(
            at.pair_send_low,
            at.pair_recv_low.at[head],
            at.kv_send.at[head, 4],
            at.kv_recv.at[head, 4],
            "ctx",
            2,
        )

    def tensor_copy(which, level):
        return send_to(
            at.sum_send.at[level],
            at.sum_recv.at[which, level],
            at.sum_sems.at[0, which, level],
            at.sum_sems.at[1, which, level],
            "tensor",
            tensor_bits[level],
        )

    quarter = at.small.shape[1] // 4

    def small_half(number):
        return send_to(
            at.small.at[:, blocks_of(flip(ctx, (1, 3)[number]), quarter)],
            at.small_recv.at[number],
            at.small_sems.at[0, number],
            at.small_sems.at[1, number],
            "ctx",
            1,
        )

    def small_rest():
        return send_to(
            at.small_held.at[1],
            at.small_recv.at[2],
            at.small_sems.at[0, 2],
            at.small_sems.at[1, 2],
            "ctx",
            2,
        )

    def line_copy(entry):
        axis, bit = line_steps[entry]
        return send_to(
            at.line.at[entry],
            at.line_recv.at[entry],
            at.small_sems.at[0, 3 + entry],
            at.small_sems.at[1, 3 + entry],
            axis,
            bit,
        )

    def small_spread(place):
        return send_to(
            at.line.at[len(line_steps)],
            at.small_full.at[:, blocks_of(ctx, quarter)],
            at.spread_sems.at[0, place - 1],
            at.spread_sems.at[1, place - 1],
            "ctx",
            place,
        )

    def turn(heads_rows, back):
        start_part = heads_rows[:, :LANES]
        ahead = pltpu.roll(start_part, LANES - ROT // 2, 1) * at.sine_ahead[...]
        behind = pltpu.roll(start_part, ROT // 2, 1) * at.sine_behind[...]
        straight = start_part * at.cosine[...]
        moved = straight - ahead - behind if back else straight + ahead + behind
        return jnp.concatenate([moved, heads_rows[:, LANES:]], 1)

    def late_block(block):
        piece = attn_pieces + block // per_piece
        return at.late.at[piece, :, blocks_of(block % per_piece, HS)]

    up_load(0).start()
    up_load_aside(1).start()
    down_load(0).start()
    gate_load(0).start()
    dense_load(0).start()
    barrier = pltpu.get_barrier_semaphore()
    partners = halving[:2] + line_steps + (("ctx", 3),)
    for axis, bits in partners:
        pl.semaphore_signal(
            barrier,
            1,
            device_id={axis: flip(lax.axis_index(axis), bits)},
            device_id_type=MESH,
        )
    pl.semaphore_wait(barrier, len(partners))
    step_rows = 32
    at.small[...] = jnp.zeros_like(at.small)
    ids = at.subset_ids[...]
    weight_line = jnp.zeros(ids.shape, F32)
    for number in range(at.subset_weights.shape[0]):
        weight_line = jnp.where(ids == number, at.subset_weights[number], weight_line)
    at.row_weight[...] = jnp.broadcast_to(weight_line, (LANES, rows)).T

    def grad_of(some):
        return at.cotangent[some].astype(F32) * at.row_weight[some, pl.ds(0, 1)]

    @pl.loop(0, rows // step_rows)
    def _(block):
        some = blocks_of(block, step_rows)
        at.low[some] = grad_of(some).astype(LOW)

    for place in (2, 3, 1):
        for block in range(4):
            part_copy(0, place, block).start()

    @pl.loop(0, rows // step_rows)
    def _(block):
        some = blocks_of(block, step_rows)
        inputs = at.hidden[some].astype(F32)
        mean = jnp.mean(inputs, -1, keepdims=True)
        centered = inputs - mean
        inv_std = lax.rsqrt(jnp.mean(centered * centered, -1, keepdims=True) + NORM_EPS)
        normed = centered * inv_std
        at.attn_in[some] = (normed * at.attn_gain[...] + at.attn_bias[...]).astype(LOW)
        at.mlp_in[some] = (normed * at.mlp_gain[...] + at.mlp_bias[...]).astype(LOW)
        lane = lax.broadcasted_iota(jnp.int32, (step_rows, LANES), 1)
        at.stats[some] = jnp.where(lane < LANES // 2, mean, inv_std)

    def send_hidden():
        line = at.stats[own_rows].T
        at.stats_line[0, pl.ds(0, 8)] = line[:8]
        at.stats_line[0, pl.ds(8, 8)] = line[LANES // 2 : LANES // 2 + 8]
        for place in (2, 3, 1):
            stats_copy(place).start()
            for block in range(4):
                part_copy(1, place, block).start()
        for block in range(4):
            column = blocks_of(block * 4 + ctx, width)
            at.hidden_part[own_rows, pl.ds(block * width, width)] = at.hidden[:, column]

    def low_left():
        for block in range(4):
            column = blocks_of(block * 4 + ctx, width)
            at.low_part[own_rows, pl.ds(block * width, width)] = at.low[:, column]
        for place in (1, 2, 3):
            for block in range(4):
                part_copy(0, place, block).wait_recv()
        for entry, bits in enumerate(ORDER):
            block = at.low_part[:, blocks_of(flip(dp, bits), width)]
            at.left[0, pl.ds(entry * width, width)] = block.T

    def hidden_left():
        for place in (1, 2, 3):
            stats_copy(place).wait_recv()
            for block in range(4):
                part_copy(1, place, block).wait_recv()
        for slot in range(1, 4):
            half = lax.broadcasted_iota(jnp.int32, (LANES, rows), 0) < LANES // 2
            line = jnp.where(half, at.stats_line[slot, :1], at.stats_line[slot, 8:9])
            at.stats[pl.ds(slot * rows, rows)] = line.T
        for entry, bits in enumerate(ORDER):
            place = flip(dp, bits)
            block = at.hidden_part[:, blocks_of(place, width)].astype(F32)
            normed = (block - at.stats[:, :1]) * at.stats[:, LANES // 2 : LANES // 2 + 1]
            column = blocks_of(place * 4 + ctx, width)
            to = pl.ds(entry * width, width)
            sides = ((at.mlp_gain, at.mlp_bias), (at.attn_gain, at.attn_bias))
            for number, (gain, bias) in enumerate(sides):
                at.left[1 + number, to] = (normed * gain[:, column] + bias[:, column]).astype(LOW).T

    def start_piece(piece):
        @pl.when(piece >= RING)
        def _():
            pl.semaphore_wait(at.free.at[0], 1)
            pl.semaphore_wait(at.free.at[1], 1)

        @pl.when(piece >= late)
        def _():
            at.rows_all[piece % RING, own_rows] = at.late[piece - late]

        across(piece).start()
        beside(piece, 0).start()

    def pre_act(pair, weights):
        pre = dot(at.mlp_in[...], weights) + at.up_bias[:, blocks_of(pair, span)]
        return pre, 0.5 * (1.0 + lax.erf(pre * math.sqrt(0.5)))

    def activate(pair):
        if pair % 2 == 0:
            up_load(pair).wait()
            pre, cumulative = pre_act(pair, at.up_held[...])
        else:
            up_load_aside(pair).wait()
            pre, cumulative = pre_act(pair, at.qkv_held[:, :span])
        at.rows_all[pair, own_rows] = (pre * cumulative).astype(LOW)
        start_piece(pair)
        if pair % 2 == 0:
            up_load((pair + 2) % 4).start()
        elif pair == 1:
            up_load_aside(3).start()
        else:
            qkv_load(0).start()
            send_hidden()

    def feed_forward(pair):
        up_load(pair).wait()
        down_load(pair).wait()
        pre, cumulative = pre_act(pair, at.up_held[...])
        feed_piece = jnp.where(pair < 4, pair, pair // 2 * 4 + pair % 2)
        grad_piece = feed_piece + jnp.where(pair < 4, 4, 2)

        @pl.when(pair >= 4)
        def _():
            at.rows_all[feed_piece % RING, own_rows] = (pre * cumulative).astype(LOW)
            start_piece(feed_piece)

        grad_act = dot_rows(at.low[...], at.down_held[...])
        density = jnp.exp(-0.5 * pre * pre) * (1.0 / math.sqrt(2.0 * math.pi))
        grad_pre = (grad_act * (cumulative + pre * density)).astype(LOW)
        at.rows_all[grad_piece % RING, own_rows] = grad_pre
        at.small[pl.ds(4, 1), blocks_of(pair, span)] = jnp.sum(
            grad_pre.astype(F32), 0, keepdims=True
        )
        @pl.when(pair < 4)
        def _():
            start_piece(grad_piece)

        @pl.when(pair == 0)
        def _():
            for held in (at.branch, at.grad_mlp, at.grad_attn):
                held[...] = jnp.zeros_like(held)

        at.branch[...] += dot(at.rows_all[feed_piece % RING, own_rows], at.down_held[...])
        at.grad_mlp[...] += dot_rows(at.rows_all[grad_piece % RING, own_rows], at.up_held[...])

        @pl.when(pair + 1 < pairs)
        def _():
            up_load(pair + 1).start()
            down_load(pair + 1).start()

    def project(head):
        qkv_load(head).wait()
        out = dot(at.attn_in[...], at.qkv_held[...]) + at.qkv_bias[:, blocks_of(head, 3 * HS)]
        at.kv[head, own_rows, pl.ds(0, HS)] = turn(out[:, HS : 2 * HS], False).astype(LOW)
        at.kv[head, own_rows, pl.ds(HS, HS)] = out[:, 2 * HS :].astype(LOW)

        @pl.when(ctx < 2)
        def _():
            kv_across(head).start()

        kv_beside(head, 0).start()
        at.query[head] = turn(out[:, :HS], False).astype(LOW)
        gate_load(head).wait()
        at.gate[head] = dot_rows(at.low[...], at.gate_held[...]).astype(LOW)
        qkv_load((head + 1) % heads).start()

        @pl.when(head + 1 < heads)
        def _():
            gate_load(head + 1).start()

    def kv_forward(head):
        @pl.when(ctx >= 2)
        def _():
            kv_across(head).wait_recv()
            kv_beside(head, 1).start()

        @pl.when(ctx < 2)
        def _():
            for slot in (1, 3):
                at.kv[head, pl.ds(slot * rows, rows)] = jnp.zeros((rows, 2 * HS), LOW)

    def attend(head):
        kv_beside(head, 0).wait_recv()

        @pl.when(ctx >= 2)
        def _():
            kv_beside(head, 1).wait_recv()

        query, gate = at.query[head], at.gate[head]
        keys, values = at.kv[head, :, :HS], at.kv[head, :, HS:]
        shape = (rows, 4 * rows)
        key_place = lax.broadcasted_iota(jnp.int32, shape, 1)
        shift = jnp.full(shape, flip(ctx, ORDER[3]) * rows - 3 * rows, jnp.int32)
        for entry in (2, 1, 0):
            here = flip(ctx, ORDER[entry]) * rows - entry * rows
            shift = jnp.where(key_place < (entry + 1) * rows, here, shift)
        query_place = lax.broadcasted_iota(jnp.int32, shape, 0) + ctx * rows
        scores = jnp.where(
            key_place + shift <= query_place, dot_rows(query, keys) * scale, -1e30
        )
        expd = jnp.exp(scores - jnp.max(scores, -1, keepdims=True))
        prob = expd * (1.0 / jnp.sum(expd, -1, keepdims=True))
        prob_low = prob.astype(LOW)
        attended = dot(prob_low, values).astype(LOW)
        at.late[head // per_piece, :, blocks_of(head % per_piece, HS)] = attended
        grad_prob = dot_rows(gate, values)
        delta = jnp.sum(grad_prob * prob, -1, keepdims=True)
        grad_scores = (prob * (grad_prob - delta)).astype(LOW)
        grad_key = dot(grad_scores.T, query) * scale
        grad_value = dot(prob_low.T, gate)
        at.pair_send[:, pl.ds(0, HS)] = grad_key[2 * rows :].astype(LOW)
        at.pair_send[:, pl.ds(HS, HS)] = grad_value[2 * rows :].astype(LOW)
        pair_beside(head).start()
        at.pair[:, pl.ds(0, HS)] = grad_key[: 2 * rows]
        at.pair[:, pl.ds(HS, HS)] = grad_value[: 2 * rows]
        late_block(3 * head)[...] = turn(dot(grad_scores, keys) * scale, True).astype(LOW)
        dense_load(head).wait()
        at.branch[...] += dot(attended, at.dense_held[...])

        @pl.when(head + 1 < heads)
        def _():
            dense_load(head + 1).start()

    def pair_halve(head):
        pair_beside(head).wait()

        @pl.when(ctx >= 2)
        def _():
            other = pl.ds(rows, rows)
            at.pair_send_low[...] = (
                at.pair[other] + at.pair_recv[head, other].astype(F32)
            ).astype(LOW)
            pair_across(head).start()

        at.pair_own[...] = at.pair[own_rows] + at.pair_recv[head, own_rows].astype(F32)

    def pair_finish(head):
        @pl.when(ctx < 2)
        def _():
            pair_across(head).wait_recv()
            at.pair_own[...] += at.pair_recv_low[head].astype(F32)

        @pl.when(ctx >= 2)
        def _():
            pair_across(head).wait_send()

        total = at.pair_own[...]
        late_block(3 * head + 1)[...] = turn(total[:, :HS], True).astype(LOW)
        late_block(3 * head + 2)[...] = total[:, HS:].astype(LOW)
        for number in range(3):
            at.small[pl.ds(3, 1), blocks_of(3 * head + number, HS)] = jnp.sum(
                late_block(3 * head + number)[...].astype(F32), 0, keepdims=True
            )

    def project_back(head):
        qkv_load(head).wait()
        at.grad_attn[...] += (
            dot_rows(late_block(3 * head)[...], at.qkv_held[:, :HS])
            + dot_rows(late_block(3 * head + 1)[...], at.qkv_held[:, HS : 2 * HS])
            + dot_rows(late_block(3 * head + 2)[...], at.qkv_held[:, 2 * HS :])
        )

        @pl.when(head + 1 < heads)
        def _():
            qkv_load(head + 1).start()

    def branch_send():
        at.sum_send[0] = at.branch[...].astype(LOW)
        tensor_copy(0, 0).start()

    def tensor_step(which, level):
        tensor_copy(which, level).wait()
        if level + 1 < len(tensor_bits):
            at.sum_send[level + 1] = (
                at.sum_send[level].astype(F32) + at.sum_recv[which, level].astype(F32)
            ).astype(LOW)
            tensor_copy(which, level + 1).start()
            return

        @pl.loop(0, rows // step_rows)
        def _(block):
            some = blocks_of(block, step_rows)
            total = at.sum_send[level, some].astype(F32) + at.sum_recv[which, level, some].astype(
                F32
            )
            if which == 0:
                total = (
                    at.hidden[some].astype(F32) + total + at.dense_bias[...] + at.down_bias[...]
                )
                at.mlp_in[some] = total.astype(LOW)
            else:
                at.attn_in[some] = (grad_of(some) + total).astype(LOW)

        row_result(which).start()

    def row_result(which):
        source = (at.mlp_in, at.attn_in)[which]
        target = (at.layer_out, at.input_grad)[which]
        return pltpu.make_async_copy(source, target, at.row_sem.at[which])

    def norm_back():
        @pl.loop(0, rows // step_rows)
        def _(block):
            some = blocks_of(block, step_rows)
            stats = at.stats[some]
            inv_std = stats[:, LANES // 2 : LANES // 2 + 1]
            normed = (at.hidden[some].astype(F32) - stats[:, :1]) * inv_std
            grad_attn, grad_mlp = at.grad_attn[some], at.grad_mlp[some]
            at.small[pl.ds(2, 1), pl.ds(0, model)] += jnp.sum(grad_of(some), 0, keepdims=True)
            for row, grad in enumerate((grad_attn, grad_mlp)):
                at.small[pl.ds(row, 1), pl.ds(0, model)] += jnp.sum(
                    grad * normed, 0, keepdims=True
                )
                at.small[pl.ds(row, 1), pl.ds(model, model)] += jnp.sum(grad, 0, keepdims=True)
            grad = grad_attn * at.attn_gain[...] + grad_mlp * at.mlp_gain[...]
            part = inv_std * (
                grad
                - jnp.mean(grad, -1, keepdims=True)
                - normed * jnp.mean(grad * normed, -1, keepdims=True)
            )
            at.sum_send[0, some] = part.astype(LOW)

        tensor_copy(1, 0).start()
        for number in range(2):
            small_half(number).start()

    def small_step(entry):
        if entry == 0:
            for number in range(2):
                small_half(number).wait()
                mine = blocks_of(flip(ctx, 2 * number), quarter)
                at.small_held[number] = at.small[:, mine] + at.small_recv[number]
            small_rest().start()
            return
        if entry == 1:
            small_rest().wait()
            at.line[0] = at.small_held[0] + at.small_recv[2]
        else:
            line_copy(entry - 2).wait()
            added = at.line[entry - 2] + at.line_recv[entry - 2]
            if line_steps[entry - 2][0] == "tensor":
                row = lax.broadcasted_iota(jnp.int32, added.shape, 0)
                added = jnp.where(row < 2, added, at.line[entry - 2])
            at.line[entry - 1] = added
        if entry - 1 < len(line_steps):
            line_copy(entry - 1).start()
            return
        for place in (2, 3, 1):
            small_spread(place).start()
        at.small_full[:, blocks_of(ctx, quarter)] = at.line[len(line_steps)]

    def small_finish():
        for place in (1, 2, 3):
            small_spread(place).wait()
        at.small_out[...] = at.small_full[...]

    lead, grad_lead = 3, 3
    assert pairs % 2 == 0 and pairs >= 4

    def places(base, *lags):
        return [
            [base + 2 * head + sum(lags[:stage]) for stage in range(5)] for head in range(heads)
        ]

    def in_time(jobs):
        for piece in range(attn_pieces):
            if jobs[(piece + 1) * per_piece - 1][2] > late + piece - lead:
                return False
        for block in range(3 * heads):
            if jobs[block // 3][4] > late + attn_pieces + block // per_piece - lead:
                return False
        return True

    jobs = next(pace for pace in (places(3, 3, 2, 2, 2), places(2, 1, 1, 1, 1)) if in_time(pace))
    project_at, forward_at, attend_at, halve_at, finish_at = jobs[0]
    feed_end = max(2 * (pairs - 1) - 4, 3)
    branch_at = max(attend_at + 2 * (heads - 1), feed_end) + 1
    back_at = max(finish_at + 2 * (heads - 1) + 2, branch_at + 4 * len(tensor_bits) + 1)
    total_steps = max(
        count + 5, back_at + 5 + len(line_steps), back_at + 4 * len(tensor_bits) + 1
    )

    def step(turn_number, carry):
        now = turn_number - 2

        def job(start, stride, times, act):
            index = now - start

            @pl.when((index >= 0) & (index < stride * times) & (index % stride == 0))
            def _():
                act(index // stride)

        multiply = now - 1

        @pl.when((multiply >= 0) & (multiply < count))
        def _():
            beside(multiply, 0).wait_recv()
            beside(multiply, 1).wait_recv()

            @pl.when(multiply >= RING)
            def _():
                pl.semaphore_wait(at.free.at[2], 1)

            @pl.when(multiply >= 3)
            def _():
                first(multiply - 3).wait_send()

            feed = multiply < late
            group = jnp.where(
                feed,
                jnp.where(is_given(multiply), 0, 1),
                jnp.where(multiply < late + attn_pieces, 0, 2),
            )
            at.first_send[multiply % 3] = dot(
                at.left[group, pl.ds(2 * width, 2 * width)], at.rows_all[multiply % RING]
            ).astype(LOW)
            first(multiply).start()
            at.held[multiply % 5] = dot(
                at.left[group, pl.ds(0, 2 * width)], at.rows_all[multiply % RING]
            )

        add = now - 3

        @pl.when((add >= 0) & (add < count))
        def _():
            first(add).wait_recv()

            @pl.when(add >= RING)
            def _():
                pl.semaphore_wait(at.free.at[3], 1)

            @pl.when(add >= 3)
            def _():
                second(add - 3).wait_send()

            lower = pl.ds(width, width)
            at.second_send[add % 3] = (
                at.held[add % 5, lower] + at.first_recv[add % RING, lower].astype(F32)
            ).astype(LOW)
            second(add).start()

        last = now - 5

        @pl.when((last >= 0) & (last < count))
        def _():
            second(last).wait_recv()

            @pl.when(last >= 2)
            def _():
                for_result(last - 2, lambda copy: copy.wait())

            upper = pl.ds(0, width)
            total = (
                at.held[last % 5, upper]
                + at.first_recv[last % RING, upper].astype(F32)
                + at.second_recv[last % RING].astype(F32)
            )
            flat = ((last < late) & jnp.logical_not(is_given(last))) | (last >= late + attn_pieces)

            @pl.when(flat)
            def _():
                at.plain[last % 2] = total

            @pl.when(jnp.logical_not(flat))
            def _():
                at.turned[last % 2] = total.T

            for_result(last, lambda copy: copy.start())

            @pl.when(last < count - RING)
            def _():
                for number, bit in ((2, 1), (3, 2)):
                    pl.semaphore_signal(
                        at.free.at[number],
                        1,
                        device_id={"dp": flip(dp, bit)},
                        device_id_type=MESH,
                    )

        @pl.when((now >= 0) & (now < count))
        def _():
            across(now).wait_recv()
            beside(now, 1).start()

        sent = now - 1

        @pl.when((sent >= 0) & (sent < count))
        def _():
            across(sent).wait_send()
            beside(sent, 0).wait_send()
            beside(sent, 1).wait_send()

            @pl.when(sent < count - RING)
            def _():
                for number, bit in ((0, 2), (1, 1)):
                    pl.semaphore_signal(
                        at.free.at[number],
                        1,
                        device_id={"ctx": flip(ctx, bit)},
                        device_id_type=MESH,
                    )

        job(4, 1, 1, lambda _: hidden_left())
        job(-2, 1, 1, lambda _: activate(0))
        job(-2, 1, 1, lambda _: activate(1))

        grads = now + grad_lead

        @pl.when((grads >= 8) & (grads < late) & (grads % 4 >= 2))
        def _():
            start_piece(grads)

        @pl.when(((now >= 0) & (now < 4)) | ((now % 2 == 0) & (now >= 4) & (now < 2 * pairs - 4)))
        def _():
            feed_forward(jnp.where(now < 4, now, now // 2 + 2))

        job(-1, 1, 1, lambda _: low_left())
        job(-1, 1, 1, lambda _: activate(2))
        job(-1, 1, 1, lambda _: activate(3))
        job(project_at, 2, heads, project)
        job(forward_at, 2, heads, kv_forward)
        job(finish_at, 2, heads, pair_finish)
        job(halve_at, 2, heads, pair_halve)
        job(attend_at, 2, heads, attend)
        job(finish_at + 1, 2, heads, project_back)
        job(branch_at, 1, 1, lambda _: branch_send())
        for level in range(len(tensor_bits)):
            job(branch_at + 4 * (level + 1), 1, 1, lambda _: tensor_step(0, level))
        job(back_at, 1, 1, lambda _: norm_back())
        for level in range(len(tensor_bits)):
            job(back_at + 4 * (level + 1), 1, 1, lambda _: tensor_step(1, level))
        for entry in range(len(line_steps) + 2):
            job(back_at + 1 + entry, 1, 1, lambda _: small_step(entry))
        job(back_at + 3 + len(line_steps), 1, 1, lambda _: small_finish())

        @pl.when((now + lead >= late) & (now + lead < count))
        def _():
            start_piece(now + lead)

        return carry

    lax.fori_loop(0, total_steps + 2, step, 0)

    for place in (1, 2, 3):
        stats_copy(place).wait_send()
        for kind in range(2):
            for block in range(4):
                part_copy(kind, place, block).wait_send()

    @pl.loop(0, heads)
    def _(head):
        kv_beside(head, 0).wait_send()

        @pl.when(ctx < 2)
        def _():
            kv_across(head).wait_send()

        @pl.when(ctx >= 2)
        def _():
            kv_beside(head, 1).wait_send()

    @pl.loop(count - 3, count)
    def _(piece):
        first(piece).wait_send()
        second(piece).wait_send()

        @pl.when(piece >= count - 2)
        def _():
            for_result(piece, lambda copy: copy.wait())

    row_result(0).wait()
    row_result(1).wait()


def hand_on(cuts, *refs):
    whole = 6
    sources, small = refs[:whole], refs[whole]
    targets, refs = refs[whole + 1 : 2 * whole + 1], refs[2 * whole + 1 :]
    pieces, refs = refs[: len(cuts)], refs[len(cuts) :]
    held, sem = refs[:whole], refs[whole]

    def halves(ref):
        size = ref.shape[0] // 2
        return [ref.at[pl.ds(half * size, size)] for half in range(2)]

    copies = []
    for number in range(whole):
        parts = zip(halves(sources[number]), halves(held[number]), halves(targets[number]))
        for half, (source, middle, target) in enumerate(parts):
            copies.append(
                (
                    pltpu.make_async_copy(source, middle, sem.at[0, number, half]),
                    pltpu.make_async_copy(middle, target, sem.at[1, number, half]),
                )
            )
    for fetch, _ in copies:
        fetch.start()
    for piece, (row, low, high) in zip(pieces, cuts):
        piece[...] = small[row : row + 1, low:high]
    for fetch, put in copies:
        fetch.wait()
        put.start()
    for _, put in copies:
        put.wait()


def local(
    hidden_in,
    attn_norm_gain,
    attn_norm_bias,
    qkv_weight,
    qkv_bias,
    dense_weight,
    dense_bias,
    mlp_norm_gain,
    mlp_norm_bias,
    up_weight,
    up_bias,
    down_weight,
    down_bias,
    out_cotangent,
    subset_ids,
    subset_weights,
):
    seq_count, rows, model = hidden_in.shape
    heads = qkv_weight.shape[1] // (3 * HS)
    units = up_weight.shape[1]
    width = model // (lax.axis_size("dp") * lax.axis_size("ctx"))
    span = min(512, math.gcd(units, heads * HS, heads * 3 * HS))
    pairs = units // span
    late_count = heads * 4 * HS // span
    plan = types.SimpleNamespace(
        rows=rows, span=span, width=width, pairs=pairs, heads=heads, count=2 * pairs + late_count
    )
    tokens = rows * lax.axis_size("ctx")

    half = ROT // 2
    lane = jnp.arange(LANES, dtype=jnp.int32)[None, :]
    positions = lax.axis_index("ctx") * rows + jnp.arange(rows, dtype=jnp.int32)
    freqs = 10000.0 ** (-((lane % half).astype(F32) * 2.0 / ROT))
    table = positions.astype(F32)[:, None] * freqs
    sine = jnp.sin(table)
    cosine = jnp.where(lane < ROT, jnp.cos(table), 1.0)
    sine_ahead = jnp.where(lane < half, -sine, 0.0)
    sine_behind = jnp.where((lane >= half) & (lane < ROT), sine, 0.0)

    bits = lax.axis_size("tensor").bit_length() - 1
    steps = 2 + bits
    small_width = max(2 * model, units, heads * 3 * HS)
    dma = pltpu.SemaphoreType.DMA
    vmem = pl.BlockSpec(memory_space=pltpu.VMEM)
    hbm = pl.BlockSpec(memory_space=pl.ANY)
    inputs = {
        "hidden": (hidden_in.reshape(rows, model), vmem),
        "cotangent": (out_cotangent.reshape(rows, model), vmem),
        "subset_ids": (subset_ids, vmem),
        "subset_weights": (subset_weights, pl.BlockSpec(memory_space=pltpu.SMEM)),
        "cosine": (cosine, vmem),
        "sine_ahead": (sine_ahead, vmem),
        "sine_behind": (sine_behind, vmem),
        "attn_gain": (attn_norm_gain[None], vmem),
        "attn_bias": (attn_norm_bias[None], vmem),
        "mlp_gain": (mlp_norm_gain[None], vmem),
        "mlp_bias": (mlp_norm_bias[None], vmem),
        "dense_bias": (dense_bias[None], vmem),
        "down_bias": (down_bias[None], vmem),
        "qkv_bias": (qkv_bias[None], vmem),
        "up_bias": (up_bias[None], vmem),
        "qkv_weight": (qkv_weight, hbm),
        "dense_weight": (dense_weight, hbm),
        "up_weight": (up_weight, hbm),
        "down_weight": (down_weight, hbm),
    }
    outputs = {
        "layer_out": ((rows, model), LOW, hbm),
        "input_grad": ((rows, model), LOW, hbm),
        "small_out": ((8, small_width), F32, vmem),
        "down_out": ((units, width), F32, hbm),
        "up_out": ((width, units), F32, hbm),
        "dense_out": ((heads * HS, width), F32, hbm),
        "qkv_out": ((width, heads * 3 * HS), F32, hbm),
    }
    scratch = {
        "rows_all": pltpu.VMEM((RING, tokens, span), LOW),
        "first_send": pltpu.VMEM((3, 2 * width, span), LOW),
        "first_recv": pltpu.VMEM((RING, 2 * width, span), LOW),
        "second_send": pltpu.VMEM((3, width, span), LOW),
        "second_recv": pltpu.VMEM((RING, width, span), LOW),
        "held": pltpu.VMEM((5, 2 * width, span), F32),
        "plain": pltpu.VMEM((2, width, span), F32),
        "turned": pltpu.VMEM((2, span, width), F32),
        "left": pltpu.VMEM((3, 4 * width, tokens), LOW),
        "low_part": pltpu.VMEM((tokens, 4 * width), LOW),
        "hidden_part": pltpu.VMEM((tokens, 4 * width), LOW),
        "stats": pltpu.VMEM((tokens, LANES), F32),
        "stats_line": pltpu.VMEM((4, 16, rows), F32),
        "row_weight": pltpu.VMEM((rows, LANES), F32),
        "attn_in": pltpu.VMEM((rows, model), LOW),
        "mlp_in": pltpu.VMEM((rows, model), LOW),
        "low": pltpu.VMEM((rows, model), LOW),
        "up_held": pltpu.VMEM((model, span), LOW),
        "down_held": pltpu.VMEM((span, model), LOW),
        "qkv_held": pltpu.VMEM((model, 3 * HS), LOW),
        "gate_held": pltpu.VMEM((HS, model), LOW),
        "dense_held": pltpu.VMEM((HS, model), LOW),
        "query": pltpu.VMEM((heads, rows, HS), LOW),
        "gate": pltpu.VMEM((heads, rows, HS), LOW),
        "kv": pltpu.VMEM((heads, tokens, 2 * HS), LOW),
        "pair": pltpu.VMEM((2 * rows, 2 * HS), F32),
        "pair_own": pltpu.VMEM((rows, 2 * HS), F32),
        "pair_send": pltpu.VMEM((2 * rows, 2 * HS), LOW),
        "pair_recv": pltpu.VMEM((heads, 2 * rows, 2 * HS), LOW),
        "pair_send_low": pltpu.VMEM((rows, 2 * HS), LOW),
        "pair_recv_low": pltpu.VMEM((heads, rows, 2 * HS), LOW),
        "late": pltpu.VMEM((late_count, rows, span), LOW),
        "branch": pltpu.VMEM((rows, model), F32),
        "grad_mlp": pltpu.VMEM((rows, model), F32),
        "grad_attn": pltpu.VMEM((rows, model), F32),
        "sum_send": pltpu.VMEM((bits, rows, model), LOW),
        "sum_recv": pltpu.VMEM((2, bits, rows, model), LOW),
        "small": pltpu.VMEM((8, small_width), F32),
        "small_full": pltpu.VMEM((8, small_width), F32),
        "small_held": pltpu.VMEM((2, 8, small_width // 4), F32),
        "small_recv": pltpu.VMEM((3, 8, small_width // 4), F32),
        "line": pltpu.VMEM((steps + 1, 8, small_width // 4), F32),
        "line_recv": pltpu.VMEM((steps, 8, small_width // 4), F32),
        "load_sem": dma((5,)),
        "part_send": dma((2, 3, 4)),
        "part_recv": dma((2, 3, 4)),
        "stats_send": dma((3,)),
        "stats_recv": dma((3,)),
        "ctx_send": dma((RING, 3)),
        "ctx_recv": dma((RING, 3)),
        "dp_send": dma((RING, 2)),
        "dp_recv": dma((RING, 2)),
        "out_sem": dma((2,)),
        "row_sem": dma((2,)),
        "kv_send": dma((heads, 5)),
        "kv_recv": dma((heads, 5)),
        "sum_sems": dma((2, 2, bits)),
        "small_sems": dma((2, 3 + steps)),
        "spread_sems": dma((2, 3)),
        "free": pltpu.SemaphoreType.REGULAR((4,)),
    }
    names = [*inputs, *outputs, *scratch]
    results = pl.pallas_call(
        functools.partial(layer_kernel, plan, names),
        out_shape=[jax.ShapeDtypeStruct(shape, kind) for shape, kind, _ in outputs.values()],
        in_specs=[spec for _, spec in inputs.values()],
        out_specs=[spec for _, _, spec in outputs.values()],
        scratch_shapes=list(scratch.values()),
        compiler_params=pltpu.CompilerParams(
            collective_id=0, has_side_effects=True, vmem_limit_bytes=63 << 20
        ),
        name="layer",
    )(*[array for array, _ in inputs.values()])
    cuts = [
        (0, 0, model),
        (0, model, 2 * model),
        (1, 0, model),
        (1, model, 2 * model),
        (2, 0, model),
        (2, 0, model),
        (3, 0, heads * 3 * HS),
        (4, 0, units),
    ]
    layer_out, input_grad, small, down_grad, up_grad, dense_grad, qkv_grad = results
    large = [layer_out, input_grad, down_grad, up_grad, dense_grad, qkv_grad]
    shapes = [jax.ShapeDtypeStruct(array.shape, array.dtype) for array in large]
    shapes += [jax.ShapeDtypeStruct((1, high - low), F32) for _, low, high in cuts]
    done = pl.pallas_call(
        functools.partial(hand_on, cuts),
        out_shape=shapes,
        in_specs=[hbm] * len(large) + [vmem],
        out_specs=[hbm] * len(large) + [vmem] * len(cuts),
        scratch_shapes=[pltpu.VMEM(array.shape, array.dtype) for array in large]
        + [dma((2, len(large), 2))],
        compiler_params=pltpu.CompilerParams(vmem_limit_bytes=60 << 20),
        name="hand_on",
    )(*large, small)
    layer_out, input_grad, down_grad, up_grad, dense_grad, qkv_grad = done[:6]
    vectors = [vector.reshape(-1) for vector in done[6:]]
    attn_gain, attn_bias, mlp_gain, mlp_bias, dense_sum, down_sum, qkv_sum, up_sum = vectors
    shape = (seq_count, rows, model)
    return (
        layer_out.reshape(shape),
        input_grad.reshape(shape),
        attn_gain,
        attn_bias,
        qkv_grad,
        qkv_sum,
        dense_grad,
        dense_sum,
        mlp_gain,
        mlp_bias,
        up_grad,
        up_sum,
        down_grad,
        down_sum,
    )


def solution(mesh):
    return jax.shard_map(
        local,
        mesh=mesh,
        in_specs=(
            P("dp", "ctx", None),
            P(),
            P(),
            P(None, "tensor"),
            P("tensor"),
            P("tensor", None),
            P(),
            P(),
            P(),
            P(None, "tensor"),
            P("tensor"),
            P("tensor", None),
            P(),
            P("dp", "ctx", None),
            P("dp", "ctx"),
            P(),
        ),
        out_specs=(
            P("dp", "ctx", None),
            P("dp", "ctx", None),
            P(),
            P(),
            P(("dp", "ctx"), "tensor"),
            P("tensor"),
            P("tensor", ("dp", "ctx")),
            P(),
            P(),
            P(),
            P(("dp", "ctx"), "tensor"),
            P("tensor"),
            P("tensor", ("dp", "ctx")),
            P(),
        ),
        check_vma=False,
    )
```

```python
import functools
import math
import types

import jax
import jax.numpy as jnp
from jax import lax
from jax.experimental import pallas as pl
from jax.experimental.pallas import tpu as pltpu
from jax.sharding import PartitionSpec as P

HS = 256
ROT = 64
LANES = 128
RING = 8
NORM_EPS = 1e-05
MESH = pl.DeviceIdType.MESH
ORDER = (0, 2, 1, 3)
LOW = jnp.bfloat16
F32 = jnp.float32


def flip(place, bits):
    bit = 1
    while bit <= bits:
        if bits & bit:
            place = place + bit - 2 * bit * ((place // bit) % 2)
        bit *= 2
    return place


def send_to(source, target, send_sem, recv_sem, axis, bits):
    return pltpu.make_async_remote_copy(
        src_ref=source,
        dst_ref=target,
        send_sem=send_sem,
        recv_sem=recv_sem,
        device_id={axis: flip(lax.axis_index(axis), bits)},
        device_id_type=MESH,
    )


def dot(left, right):
    return jnp.dot(left, right, preferred_element_type=F32)


def dot_rows(left, right):
    return lax.dot_general(left, right, (((1,), (1,)), ((), ())), preferred_element_type=F32)


def axis_bits(axis):
    return [1 << level for level in range(lax.axis_size(axis).bit_length() - 1)]


def blocks_of(total, size):
    return pl.ds(pl.multiple_of(total * size, size), size)


def layer_kernel(plan, names, *refs):
    at = types.SimpleNamespace(**dict(zip(names, refs)))
    rows, span, count, width = plan.rows, plan.span, plan.count, plan.width
    pairs, heads, late = plan.pairs, plan.heads, 2 * plan.pairs
    attn_pieces = heads * HS // span
    per_piece = span // HS
    model = at.hidden.shape[1]
    ctx, dp = lax.axis_index("ctx"), lax.axis_index("dp")
    own_rows = pl.ds(0, rows)
    tensor_bits = axis_bits("tensor")
    halving = (("ctx", 1), ("ctx", 2), ("dp", 1), ("dp", 2))
    line_steps = halving[2:] + tuple(("tensor", bit) for bit in tensor_bits)
    scale = 1.0 / math.sqrt(HS)

    def up_load(piece):
        return pltpu.make_async_copy(
            at.up_weight.at[:, blocks_of(piece, span)], at.up_held, at.load_sem.at[0]
        )

    def up_load_aside(piece):
        return pltpu.make_async_copy(
            at.up_weight.at[:, blocks_of(piece, span)],
            at.qkv_held.at[:, pl.ds(0, span)],
            at.load_sem.at[2],
        )

    def down_load(piece):
        return pltpu.make_async_copy(
            at.down_weight.at[blocks_of(piece, span)], at.down_held, at.load_sem.at[1]
        )

    def qkv_load(head):
        return pltpu.make_async_copy(
            at.qkv_weight.at[:, blocks_of(head, 3 * HS)], at.qkv_held, at.load_sem.at[2]
        )

    def gate_load(head):
        return pltpu.make_async_copy(
            at.dense_weight.at[blocks_of(head, HS)], at.gate_held, at.load_sem.at[3]
        )

    def dense_load(head):
        return pltpu.make_async_copy(
            at.dense_weight.at[blocks_of(head, HS)], at.dense_held, at.load_sem.at[4]
        )

    shared = lax.axis_size("tensor") == 2
    side = lax.axis_index("tensor")

    def part_numbers(place):
        return range(2 if shared and place > 1 else 4)

    def part_copy(kind, place, number):
        source = (at.low, at.hidden)[kind]
        target = (at.low_part, at.hidden_part)[kind]
        block = 2 * side + number if shared and place > 1 else number
        column = block * 4 + flip(ctx, place)
        return send_to(
            source.at[:, blocks_of(column, width)],
            target.at[pl.ds(ORDER.index(place) * rows, rows), blocks_of(block, width)],
            at.part_send.at[kind, place - 1, number],
            at.part_recv.at[kind, place - 1, number],
            "ctx",
            place,
        )

    def part_pass(kind, place):
        target = (at.low_part, at.hidden_part)[kind]
        half = target.at[pl.ds(ORDER.index(place) * rows, rows), blocks_of(side, 2 * width)]
        return send_to(
            half,
            half,
            at.pass_sems.at[0, kind, place - 2],
            at.pass_sems.at[1, kind, place - 2],
            "tensor",
            1,
        )

    def part_starts(kind):
        for place in (2, 3, 1):
            for number in part_numbers(place):
                part_copy(kind, place, number).start()

    def pass_on(kind):
        for place in (2, 3):
            for number in part_numbers(place):
                part_copy(kind, place, number).wait_recv()
            if shared:
                part_pass(kind, place).start()

    def part_waits(kind):
        for number in part_numbers(1):
            part_copy(kind, 1, number).wait_recv()
        if shared:
            for place in (2, 3):
                part_pass(kind, place).wait_recv()

    def stats_copy(place):
        return send_to(
            at.stats_line.at[0],
            at.stats_line.at[ORDER.index(place)],
            at.stats_send.at[place - 1],
            at.stats_recv.at[place - 1],
            "ctx",
            place,
        )

    def across(piece):
        slot = piece % RING
        return send_to(
            at.rows_all.at[slot, own_rows],
            at.rows_all.at[slot, pl.ds(rows, rows)],
            at.ctx_send.at[slot, 0],
            at.ctx_recv.at[slot, 0],
            "ctx",
            2,
        )

    def beside(piece, part):
        slot = piece % RING
        return send_to(
            at.rows_all.at[slot, pl.ds(part * rows, rows)],
            at.rows_all.at[slot, pl.ds((2 + part) * rows, rows)],
            at.ctx_send.at[slot, 1 + part],
            at.ctx_recv.at[slot, 1 + part],
            "ctx",
            1,
        )

    def first(piece):
        return send_to(
            at.first_send.at[piece % 3],
            at.first_recv.at[piece % RING],
            at.dp_send.at[piece % RING, 0],
            at.dp_recv.at[piece % RING, 0],
            "dp",
            1,
        )

    def second(piece):
        return send_to(
            at.second_send.at[piece % 3],
            at.second_recv.at[piece % RING],
            at.dp_send.at[piece % RING, 1],
            at.dp_recv.at[piece % RING, 1],
            "dp",
            2,
        )

    def results(piece):
        slot = piece % 2
        turned, plain = at.turned.at[slot], at.plain.at[slot]
        feed = piece < late
        gives = piece < pairs
        dense = (piece >= late) & (piece < late + attn_pieces)
        return (
            (gives, turned, at.down_out.at[blocks_of(piece, span)]),
            (
                feed & jnp.logical_not(gives),
                plain,
                at.up_out.at[:, blocks_of(piece - pairs, span)],
            ),
            (dense, turned, at.dense_out.at[blocks_of(piece - late, span)]),
            (
                piece >= late + attn_pieces,
                plain,
                at.qkv_out.at[:, blocks_of(piece - late - attn_pieces, span)],
            ),
        )

    def for_result(piece, act):
        for holds, source, target in results(piece):

            @pl.when(holds)
            def _():
                act(pltpu.make_async_copy(source, target, at.out_sem.at[piece % 2]))

    def kv_across(head):
        return send_to(
            at.kv.at[head, own_rows],
            at.kv.at[head, pl.ds(rows, rows)],
            at.kv_send.at[head, 0],
            at.kv_recv.at[head, 0],
            "ctx",
            2,
        )

    def kv_beside(head, part):
        return send_to(
            at.kv.at[head, pl.ds(part * rows, rows)],
            at.kv.at[head, pl.ds((2 + part) * rows, rows)],
            at.kv_send.at[head, 1 + part],
            at.kv_recv.at[head, 1 + part],
            "ctx",
            1,
        )

    def pair_beside(head):
        return send_to(
            at.pair_send,
            at.pair_recv.at[head],
            at.kv_send.at[head, 3],
            at.kv_recv.at[head, 3],
            "ctx",
            1,
        )

    def pair_across(head):
        return send_to(
            at.pair_send_low,
            at.pair_recv_low.at[head],
            at.kv_send.at[head, 4],
            at.kv_recv.at[head, 4],
            "ctx",
            2,
        )

    def tensor_copy(which, level):
        return send_to(
            at.sum_send.at[level],
            at.sum_recv.at[which, level],
            at.sum_sems.at[0, which, level],
            at.sum_sems.at[1, which, level],
            "tensor",
            tensor_bits[level],
        )

    quarter = at.small.shape[1] // 4

    def small_half(number):
        return send_to(
            at.small.at[:, blocks_of(flip(ctx, (1, 3)[number]), quarter)],
            at.small_recv.at[number],
            at.small_sems.at[0, number],
            at.small_sems.at[1, number],
            "ctx",
            1,
        )

    def small_rest():
        return send_to(
            at.small_held.at[1],
            at.small_recv.at[2],
            at.small_sems.at[0, 2],
            at.small_sems.at[1, 2],
            "ctx",
            2,
        )

    def line_copy(entry):
        axis, bit = line_steps[entry]
        return send_to(
            at.line.at[entry],
            at.line_recv.at[entry],
            at.small_sems.at[0, 3 + entry],
            at.small_sems.at[1, 3 + entry],
            axis,
            bit,
        )

    def small_spread(place):
        return send_to(
            at.line.at[len(line_steps)],
            at.small_full.at[:, blocks_of(ctx, quarter)],
            at.spread_sems.at[0, place - 1],
            at.spread_sems.at[1, place - 1],
            "ctx",
            place,
        )

    def turn(heads_rows, back):
        start_part = heads_rows[:, :LANES]
        ahead = pltpu.roll(start_part, LANES - ROT // 2, 1) * at.sine_ahead[...]
        behind = pltpu.roll(start_part, ROT // 2, 1) * at.sine_behind[...]
        straight = start_part * at.cosine[...]
        moved = straight - ahead - behind if back else straight + ahead + behind
        return jnp.concatenate([moved, heads_rows[:, LANES:]], 1)

    def late_block(block):
        piece = attn_pieces + block // per_piece
        return at.late.at[piece, :, blocks_of(block % per_piece, HS)]

    up_load(0).start()
    up_load_aside(1).start()
    down_load(0).start()
    gate_load(0).start()
    dense_load(0).start()
    barrier = pltpu.get_barrier_semaphore()
    partners = halving[:2] + line_steps + (("ctx", 3),)
    for axis, bits in partners:
        pl.semaphore_signal(
            barrier,
            1,
            device_id={axis: flip(lax.axis_index(axis), bits)},
            device_id_type=MESH,
        )
    pl.semaphore_wait(barrier, len(partners))
    step_rows = 32
    at.small[...] = jnp.zeros_like(at.small)
    ids = at.subset_ids[...]
    weight_line = jnp.zeros(ids.shape, F32)
    for number in range(at.subset_weights.shape[0]):
        weight_line = jnp.where(ids == number, at.subset_weights[number], weight_line)
    at.row_weight[...] = jnp.broadcast_to(weight_line, (LANES, rows)).T

    def grad_of(some):
        return at.cotangent[some].astype(F32) * at.row_weight[some, pl.ds(0, 1)]

    @pl.loop(0, rows // step_rows)
    def _(block):
        some = blocks_of(block, step_rows)
        at.low[some] = grad_of(some).astype(LOW)

    part_starts(0)

    @pl.loop(0, rows // step_rows)
    def _(block):
        some = blocks_of(block, step_rows)
        inputs = at.hidden[some].astype(F32)
        mean = jnp.mean(inputs, -1, keepdims=True)
        centered = inputs - mean
        inv_std = lax.rsqrt(jnp.mean(centered * centered, -1, keepdims=True) + NORM_EPS)
        normed = centered * inv_std
        at.attn_in[some] = (normed * at.attn_gain[...] + at.attn_bias[...]).astype(LOW)
        at.mlp_in[some] = (normed * at.mlp_gain[...] + at.mlp_bias[...]).astype(LOW)
        lane = lax.broadcasted_iota(jnp.int32, (step_rows, LANES), 1)
        at.stats[some] = jnp.where(lane < LANES // 2, mean, inv_std)

    def send_hidden():
        line = at.stats[own_rows].T
        at.stats_line[0, pl.ds(0, 8)] = line[:8]
        at.stats_line[0, pl.ds(8, 8)] = line[LANES // 2 : LANES // 2 + 8]
        for place in (2, 3, 1):
            stats_copy(place).start()
        part_starts(1)
        for block in range(4):
            column = blocks_of(block * 4 + ctx, width)
            at.hidden_part[own_rows, pl.ds(block * width, width)] = at.hidden[:, column]

    def low_left():
        for block in range(4):
            column = blocks_of(block * 4 + ctx, width)
            at.low_part[own_rows, pl.ds(block * width, width)] = at.low[:, column]
        part_waits(0)
        for entry, bits in enumerate(ORDER):
            block = at.low_part[:, blocks_of(flip(dp, bits), width)]
            at.left[0, pl.ds(entry * width, width)] = block.T

    def hidden_left():
        for place in (1, 2, 3):
            stats_copy(place).wait_recv()
        part_waits(1)
        for slot in range(1, 4):
            half = lax.broadcasted_iota(jnp.int32, (LANES, rows), 0) < LANES // 2
            line = jnp.where(half, at.stats_line[slot, :1], at.stats_line[slot, 8:9])
            at.stats[pl.ds(slot * rows, rows)] = line.T
        for entry, bits in enumerate(ORDER):
            place = flip(dp, bits)
            block = at.hidden_part[:, blocks_of(place, width)].astype(F32)
            normed = (block - at.stats[:, :1]) * at.stats[:, LANES // 2 : LANES // 2 + 1]
            column = blocks_of(place * 4 + ctx, width)
            to = pl.ds(entry * width, width)
            sides = ((at.mlp_gain, at.mlp_bias), (at.attn_gain, at.attn_bias))
            for number, (gain, bias) in enumerate(sides):
                at.left[1 + number, to] = (normed * gain[:, column] + bias[:, column]).astype(LOW).T

    def start_piece(piece):
        @pl.when(piece >= RING)
        def _():
            pl.semaphore_wait(at.free.at[0], 1)
            pl.semaphore_wait(at.free.at[1], 1)

        @pl.when(piece >= late)
        def _():
            at.rows_all[piece % RING, own_rows] = at.late[piece - late]

        across(piece).start()
        beside(piece, 0).start()

    def pre_act(pair, weights):
        pre = dot(at.mlp_in[...], weights) + at.up_bias[:, blocks_of(pair, span)]
        return pre, 0.5 * (1.0 + lax.erf(pre * math.sqrt(0.5)))

    def activate(pair):
        if pair in (1, 3):
            up_load_aside(pair).wait()
            pre, cumulative = pre_act(pair, at.qkv_held[:, :span])
        else:
            up_load(pair).wait()
            pre, cumulative = pre_act(pair, at.up_held[...])
        at.rows_all[pair % RING, own_rows] = (pre * cumulative).astype(LOW)
        start_piece(pair)
        if pair == 1:
            up_load_aside(3).start()
        elif pair == 3:
            qkv_load(0).start()
        else:
            following = {0: 2, 2: 4}.get(pair, pair + 1)
            up_load(following if following < pairs else 0).start()
        if pair == max(pairs - 2, 3):
            send_hidden()

    def feed_forward(pair):
        up_load(pair).wait()
        down_load(pair).wait()
        pre, cumulative = pre_act(pair, at.up_held[...])
        given = (pre * cumulative).astype(LOW)
        grad_act = dot_rows(at.low[...], at.down_held[...])
        density = jnp.exp(-0.5 * pre * pre) * (1.0 / math.sqrt(2.0 * math.pi))
        grad_pre = (grad_act * (cumulative + pre * density)).astype(LOW)
        at.rows_all[(pairs + pair) % RING, own_rows] = grad_pre
        at.small[pl.ds(4, 1), blocks_of(pair, span)] = jnp.sum(
            grad_pre.astype(F32), 0, keepdims=True
        )
        start_piece(pairs + pair)

        @pl.when(pair == 0)
        def _():
            for held in (at.branch, at.grad_mlp, at.grad_attn):
                held[...] = jnp.zeros_like(held)

        at.branch[...] += dot(given, at.down_held[...])
        at.grad_mlp[...] += dot_rows(grad_pre, at.up_held[...])

        @pl.when(pair + 1 < pairs)
        def _():
            up_load(pair + 1).start()
            down_load(pair + 1).start()

    def project(head):
        qkv_load(head).wait()
        out = dot(at.attn_in[...], at.qkv_held[...]) + at.qkv_bias[:, blocks_of(head, 3 * HS)]
        at.kv[head, own_rows, pl.ds(0, HS)] = turn(out[:, HS : 2 * HS], False).astype(LOW)
        at.kv[head, own_rows, pl.ds(HS, HS)] = out[:, 2 * HS :].astype(LOW)

        @pl.when(ctx < 2)
        def _():
            kv_across(head).start()

        kv_beside(head, 0).start()
        at.query[head] = turn(out[:, :HS], False).astype(LOW)
        gate_load(head).wait()
        at.gate[head] = dot_rows(at.low[...], at.gate_held[...]).astype(LOW)
        qkv_load((head + 1) % heads).start()

        @pl.when(head + 1 < heads)
        def _():
            gate_load(head + 1).start()

    def kv_forward(head):
        @pl.when(ctx >= 2)
        def _():
            kv_across(head).wait_recv()
            kv_beside(head, 1).start()

        @pl.when(ctx < 2)
        def _():
            for slot in (1, 3):
                at.kv[head, pl.ds(slot * rows, rows)] = jnp.zeros((rows, 2 * HS), LOW)

    def attend(head):
        kv_beside(head, 0).wait_recv()

        @pl.when(ctx >= 2)
        def _():
            kv_beside(head, 1).wait_recv()

        query, gate = at.query[head], at.gate[head]
        keys, values = at.kv[head, :, :HS], at.kv[head, :, HS:]
        shape = (rows, 4 * rows)
        key_place = lax.broadcasted_iota(jnp.int32, shape, 1)
        shift = jnp.full(shape, flip(ctx, ORDER[3]) * rows - 3 * rows, jnp.int32)
        for entry in (2, 1, 0):
            here = flip(ctx, ORDER[entry]) * rows - entry * rows
            shift = jnp.where(key_place < (entry + 1) * rows, here, shift)
        query_place = lax.broadcasted_iota(jnp.int32, shape, 0) + ctx * rows
        scores = jnp.where(
            key_place + shift <= query_place, dot_rows(query, keys) * scale, -1e30
        )
        expd = jnp.exp(scores - jnp.max(scores, -1, keepdims=True))
        prob = expd * (1.0 / jnp.sum(expd, -1, keepdims=True))
        prob_low = prob.astype(LOW)
        attended = dot(prob_low, values).astype(LOW)
        at.late[head // per_piece, :, blocks_of(head % per_piece, HS)] = attended
        grad_prob = dot_rows(gate, values)
        delta = jnp.sum(grad_prob * prob, -1, keepdims=True)
        grad_scores = (prob * (grad_prob - delta)).astype(LOW)
        grad_key = dot(grad_scores.T, query) * scale
        grad_value = dot(prob_low.T, gate)
        at.pair_send[:, pl.ds(0, HS)] = grad_key[2 * rows :].astype(LOW)
        at.pair_send[:, pl.ds(HS, HS)] = grad_value[2 * rows :].astype(LOW)
        pair_beside(head).start()
        at.pair[:, pl.ds(0, HS)] = grad_key[: 2 * rows]
        at.pair[:, pl.ds(HS, HS)] = grad_value[: 2 * rows]
        late_block(3 * head)[...] = turn(dot(grad_scores, keys) * scale, True).astype(LOW)
        dense_load(head).wait()
        at.branch[...] += dot(attended, at.dense_held[...])

        @pl.when(head + 1 < heads)
        def _():
            dense_load(head + 1).start()

    def pair_halve(head):
        pair_beside(head).wait()

        @pl.when(ctx >= 2)
        def _():
            other = pl.ds(rows, rows)
            at.pair_send_low[...] = (
                at.pair[other] + at.pair_recv[head, other].astype(F32)
            ).astype(LOW)
            pair_across(head).start()

        at.pair_own[...] = at.pair[own_rows] + at.pair_recv[head, own_rows].astype(F32)

    def pair_finish(head):
        @pl.when(ctx < 2)
        def _():
            pair_across(head).wait_recv()
            at.pair_own[...] += at.pair_recv_low[head].astype(F32)

        @pl.when(ctx >= 2)
        def _():
            pair_across(head).wait_send()

        total = at.pair_own[...]
        late_block(3 * head + 1)[...] = turn(total[:, :HS], True).astype(LOW)
        late_block(3 * head + 2)[...] = total[:, HS:].astype(LOW)
        for number in range(3):
            at.small[pl.ds(3, 1), blocks_of(3 * head + number, HS)] = jnp.sum(
                late_block(3 * head + number)[...].astype(F32), 0, keepdims=True
            )

    def project_back(head):
        qkv_load(head).wait()
        at.grad_attn[...] += (
            dot_rows(late_block(3 * head)[...], at.qkv_held[:, :HS])
            + dot_rows(late_block(3 * head + 1)[...], at.qkv_held[:, HS : 2 * HS])
            + dot_rows(late_block(3 * head + 2)[...], at.qkv_held[:, 2 * HS :])
        )

        @pl.when(head + 1 < heads)
        def _():
            qkv_load(head + 1).start()

    def branch_send():
        at.sum_send[0] = at.branch[...].astype(LOW)
        tensor_copy(0, 0).start()

    def tensor_step(which, level):
        tensor_copy(which, level).wait()
        if level + 1 < len(tensor_bits):
            at.sum_send[level + 1] = (
                at.sum_send[level].astype(F32) + at.sum_recv[which, level].astype(F32)
            ).astype(LOW)
            tensor_copy(which, level + 1).start()
            return

        @pl.loop(0, rows // step_rows)
        def _(block):
            some = blocks_of(block, step_rows)
            total = at.sum_send[level, some].astype(F32) + at.sum_recv[which, level, some].astype(
                F32
            )
            if which == 0:
                total = (
                    at.hidden[some].astype(F32) + total + at.dense_bias[...] + at.down_bias[...]
                )
                at.mlp_in[some] = total.astype(LOW)
            else:
                at.attn_in[some] = (grad_of(some) + total).astype(LOW)

        row_result(which).start()

    def row_result(which):
        source = (at.mlp_in, at.attn_in)[which]
        target = (at.layer_out, at.input_grad)[which]
        return pltpu.make_async_copy(source, target, at.row_sem.at[which])

    def norm_back():
        @pl.loop(0, rows // step_rows)
        def _(block):
            some = blocks_of(block, step_rows)
            stats = at.stats[some]
            inv_std = stats[:, LANES // 2 : LANES // 2 + 1]
            normed = (at.hidden[some].astype(F32) - stats[:, :1]) * inv_std
            grad_attn, grad_mlp = at.grad_attn[some], at.grad_mlp[some]
            at.small[pl.ds(2, 1), pl.ds(0, model)] += jnp.sum(grad_of(some), 0, keepdims=True)
            for row, grad in enumerate((grad_attn, grad_mlp)):
                at.small[pl.ds(row, 1), pl.ds(0, model)] += jnp.sum(
                    grad * normed, 0, keepdims=True
                )
                at.small[pl.ds(row, 1), pl.ds(model, model)] += jnp.sum(grad, 0, keepdims=True)
            grad = grad_attn * at.attn_gain[...] + grad_mlp * at.mlp_gain[...]
            part = inv_std * (
                grad
                - jnp.mean(grad, -1, keepdims=True)
                - normed * jnp.mean(grad * normed, -1, keepdims=True)
            )
            at.sum_send[0, some] = part.astype(LOW)

        tensor_copy(1, 0).start()
        for number in range(2):
            small_half(number).start()

    def small_step(entry):
        if entry == 0:
            for number in range(2):
                small_half(number).wait()
                mine = blocks_of(flip(ctx, 2 * number), quarter)
                at.small_held[number] = at.small[:, mine] + at.small_recv[number]
            small_rest().start()
            return
        if entry == 1:
            small_rest().wait()
            at.line[0] = at.small_held[0] + at.small_recv[2]
        else:
            line_copy(entry - 2).wait()
            added = at.line[entry - 2] + at.line_recv[entry - 2]
            if line_steps[entry - 2][0] == "tensor":
                row = lax.broadcasted_iota(jnp.int32, added.shape, 0)
                added = jnp.where(row < 2, added, at.line[entry - 2])
            at.line[entry - 1] = added
        if entry - 1 < len(line_steps):
            line_copy(entry - 1).start()
            return
        for place in (2, 3, 1):
            small_spread(place).start()
        at.small_full[:, blocks_of(ctx, quarter)] = at.line[len(line_steps)]

    def small_finish():
        for place in (1, 2, 3):
            small_spread(place).wait()
        at.small_out[...] = at.small_full[...]

    lead = 3
    assert pairs in (4, 8)

    def places(base, *lags):
        return [
            [base + 2 * head + sum(lags[:stage]) for stage in range(5)] for head in range(heads)
        ]

    def in_time(jobs):
        for piece in range(attn_pieces):
            if jobs[(piece + 1) * per_piece - 1][2] > late + piece - lead:
                return False
        for block in range(3 * heads):
            if jobs[block // 3][4] > late + attn_pieces + block // per_piece - lead:
                return False
        return True

    jobs = next(pace for pace in (places(3, 3, 2, 2, 2), places(2, 1, 1, 1, 1)) if in_time(pace))
    project_at, forward_at, attend_at, halve_at, finish_at = jobs[0]
    feed_at = max(pairs - 4, 1)
    feed_end = feed_at + pairs - 1
    branch_at = max(attend_at + 2 * (heads - 1), feed_end) + 1
    back_at = max(finish_at + 2 * (heads - 1) + 2, branch_at + 4 * len(tensor_bits) + 1)
    total_steps = max(
        count + 5, back_at + 5 + len(line_steps), back_at + 4 * len(tensor_bits) + 1
    )

    def step(turn_number, carry):
        now = turn_number - 2

        def job(start, stride, times, act):
            index = now - start

            @pl.when((index >= 0) & (index < stride * times) & (index % stride == 0))
            def _():
                act(index // stride)

        multiply = now - 1

        @pl.when((multiply >= 0) & (multiply < count))
        def _():
            beside(multiply, 0).wait_recv()
            beside(multiply, 1).wait_recv()

            @pl.when(multiply >= RING)
            def _():
                pl.semaphore_wait(at.free.at[2], 1)

            @pl.when(multiply >= 3)
            def _():
                first(multiply - 3).wait_send()

            feed = multiply < late
            group = jnp.where(
                feed,
                jnp.where(multiply < pairs, 0, 1),
                jnp.where(multiply < late + attn_pieces, 0, 2),
            )
            at.first_send[multiply % 3] = dot(
                at.left[group, pl.ds(2 * width, 2 * width)], at.rows_all[multiply % RING]
            ).astype(LOW)
            first(multiply).start()
            at.held[multiply % 5] = dot(
                at.left[group, pl.ds(0, 2 * width)], at.rows_all[multiply % RING]
            )

        add = now - 3

        @pl.when((add >= 0) & (add < count))
        def _():
            first(add).wait_recv()

            @pl.when(add >= RING)
            def _():
                pl.semaphore_wait(at.free.at[3], 1)

            @pl.when(add >= 3)
            def _():
                second(add - 3).wait_send()

            lower = pl.ds(width, width)
            at.second_send[add % 3] = (
                at.held[add % 5, lower] + at.first_recv[add % RING, lower].astype(F32)
            ).astype(LOW)
            second(add).start()

        last = now - 5

        @pl.when((last >= 0) & (last < count))
        def _():
            second(last).wait_recv()

            @pl.when(last >= 2)
            def _():
                for_result(last - 2, lambda copy: copy.wait())

            upper = pl.ds(0, width)
            total = (
                at.held[last % 5, upper]
                + at.first_recv[last % RING, upper].astype(F32)
                + at.second_recv[last % RING].astype(F32)
            )
            flat = ((last < late) & (last >= pairs)) | (last >= late + attn_pieces)

            @pl.when(flat)
            def _():
                at.plain[last % 2] = total

            @pl.when(jnp.logical_not(flat))
            def _():
                at.turned[last % 2] = total.T

            for_result(last, lambda copy: copy.start())

            @pl.when(last < count - RING)
            def _():
                for number, bit in ((2, 1), (3, 2)):
                    pl.semaphore_signal(
                        at.free.at[number],
                        1,
                        device_id={"dp": flip(dp, bit)},
                        device_id_type=MESH,
                    )

        @pl.when((now >= 0) & (now < count))
        def _():
            across(now).wait_recv()
            beside(now, 1).start()

        sent = now - 1

        @pl.when((sent >= 0) & (sent < count))
        def _():
            across(sent).wait_send()
            beside(sent, 0).wait_send()
            beside(sent, 1).wait_send()

            @pl.when(sent < count - RING)
            def _():
                for number, bit in ((0, 2), (1, 1)):
                    pl.semaphore_signal(
                        at.free.at[number],
                        1,
                        device_id={"ctx": flip(ctx, bit)},
                        device_id_type=MESH,
                    )

        for pair, place in enumerate((-2, -2, -1, 0, 1, 2, 3, 3)[:pairs]):
            job(place, 1, 1, lambda _: activate(pair))
            if pair == 0:
                job(-2, 1, 1, lambda _: pass_on(0))
            if pair == 2:
                job(-1, 1, 1, lambda _: low_left())
        job(pairs - 2, 1, 1, lambda _: pass_on(1))
        job(pairs - 1, 1, 1, lambda _: hidden_left())
        job(feed_at, 1, pairs, feed_forward)
        job(project_at, 2, heads, project)
        job(forward_at, 2, heads, kv_forward)
        job(finish_at, 2, heads, pair_finish)
        job(halve_at, 2, heads, pair_halve)
        job(attend_at, 2, heads, attend)
        job(finish_at + 1, 2, heads, project_back)
        job(branch_at, 1, 1, lambda _: branch_send())
        for level in range(len(tensor_bits)):
            job(branch_at + 4 * (level + 1), 1, 1, lambda _: tensor_step(0, level))
        job(back_at, 1, 1, lambda _: norm_back())
        for level in range(len(tensor_bits)):
            job(back_at + 4 * (level + 1), 1, 1, lambda _: tensor_step(1, level))
        for entry in range(len(line_steps) + 2):
            job(back_at + 1 + entry, 1, 1, lambda _: small_step(entry))
        job(back_at + 3 + len(line_steps), 1, 1, lambda _: small_finish())

        @pl.when((now + lead >= late) & (now + lead < count))
        def _():
            start_piece(now + lead)

        return carry

    lax.fori_loop(0, total_steps + 2, step, 0)

    for place in (1, 2, 3):
        stats_copy(place).wait_send()
        for kind in range(2):
            for number in part_numbers(place):
                part_copy(kind, place, number).wait_send()
            if shared and place > 1:
                part_pass(kind, place).wait_send()

    @pl.loop(0, heads)
    def _(head):
        kv_beside(head, 0).wait_send()

        @pl.when(ctx < 2)
        def _():
            kv_across(head).wait_send()

        @pl.when(ctx >= 2)
        def _():
            kv_beside(head, 1).wait_send()

    @pl.loop(count - 3, count)
    def _(piece):
        first(piece).wait_send()
        second(piece).wait_send()

        @pl.when(piece >= count - 2)
        def _():
            for_result(piece, lambda copy: copy.wait())

    row_result(0).wait()
    row_result(1).wait()


def hand_on(cuts, *refs):
    whole = 6
    sources, small = refs[:whole], refs[whole]
    targets, refs = refs[whole + 1 : 2 * whole + 1], refs[2 * whole + 1 :]
    pieces, refs = refs[: len(cuts)], refs[len(cuts) :]
    held, sem = refs[:whole], refs[whole]

    def halves(ref):
        size = ref.shape[0] // 2
        return [ref.at[pl.ds(half * size, size)] for half in range(2)]

    copies = []
    for number in range(whole):
        parts = zip(halves(sources[number]), halves(held[number]), halves(targets[number]))
        for half, (source, middle, target) in enumerate(parts):
            copies.append(
                (
                    pltpu.make_async_copy(source, middle, sem.at[0, number, half]),
                    pltpu.make_async_copy(middle, target, sem.at[1, number, half]),
                )
            )
    for fetch, _ in copies:
        fetch.start()
    for piece, (row, low, high) in zip(pieces, cuts):
        piece[...] = small[row : row + 1, low:high]
    for fetch, put in copies:
        fetch.wait()
        put.start()
    for _, put in copies:
        put.wait()


def local(
    hidden_in,
    attn_norm_gain,
    attn_norm_bias,
    qkv_weight,
    qkv_bias,
    dense_weight,
    dense_bias,
    mlp_norm_gain,
    mlp_norm_bias,
    up_weight,
    up_bias,
    down_weight,
    down_bias,
    out_cotangent,
    subset_ids,
    subset_weights,
):
    seq_count, rows, model = hidden_in.shape
    heads = qkv_weight.shape[1] // (3 * HS)
    units = up_weight.shape[1]
    width = model // (lax.axis_size("dp") * lax.axis_size("ctx"))
    span = min(512, math.gcd(units, heads * HS, heads * 3 * HS))
    pairs = units // span
    late_count = heads * 4 * HS // span
    plan = types.SimpleNamespace(
        rows=rows, span=span, width=width, pairs=pairs, heads=heads, count=2 * pairs + late_count
    )
    tokens = rows * lax.axis_size("ctx")

    half = ROT // 2
    lane = jnp.arange(LANES, dtype=jnp.int32)[None, :]
    positions = lax.axis_index("ctx") * rows + jnp.arange(rows, dtype=jnp.int32)
    freqs = 10000.0 ** (-((lane % half).astype(F32) * 2.0 / ROT))
    table = positions.astype(F32)[:, None] * freqs
    sine = jnp.sin(table)
    cosine = jnp.where(lane < ROT, jnp.cos(table), 1.0)
    sine_ahead = jnp.where(lane < half, -sine, 0.0)
    sine_behind = jnp.where((lane >= half) & (lane < ROT), sine, 0.0)

    bits = lax.axis_size("tensor").bit_length() - 1
    steps = 2 + bits
    small_width = max(2 * model, units, heads * 3 * HS)
    dma = pltpu.SemaphoreType.DMA
    vmem = pl.BlockSpec(memory_space=pltpu.VMEM)
    hbm = pl.BlockSpec(memory_space=pl.ANY)
    inputs = {
        "hidden": (hidden_in.reshape(rows, model), vmem),
        "cotangent": (out_cotangent.reshape(rows, model), vmem),
        "subset_ids": (subset_ids, vmem),
        "subset_weights": (subset_weights, pl.BlockSpec(memory_space=pltpu.SMEM)),
        "cosine": (cosine, vmem),
        "sine_ahead": (sine_ahead, vmem),
        "sine_behind": (sine_behind, vmem),
        "attn_gain": (attn_norm_gain[None], vmem),
        "attn_bias": (attn_norm_bias[None], vmem),
        "mlp_gain": (mlp_norm_gain[None], vmem),
        "mlp_bias": (mlp_norm_bias[None], vmem),
        "dense_bias": (dense_bias[None], vmem),
        "down_bias": (down_bias[None], vmem),
        "qkv_bias": (qkv_bias[None], vmem),
        "up_bias": (up_bias[None], vmem),
        "qkv_weight": (qkv_weight, hbm),
        "dense_weight": (dense_weight, hbm),
        "up_weight": (up_weight, hbm),
        "down_weight": (down_weight, hbm),
    }
    outputs = {
        "layer_out": ((rows, model), LOW, hbm),
        "input_grad": ((rows, model), LOW, hbm),
        "small_out": ((8, small_width), F32, vmem),
        "down_out": ((units, width), F32, hbm),
        "up_out": ((width, units), F32, hbm),
        "dense_out": ((heads * HS, width), F32, hbm),
        "qkv_out": ((width, heads * 3 * HS), F32, hbm),
    }
    scratch = {
        "rows_all": pltpu.VMEM((RING, tokens, span), LOW),
        "first_send": pltpu.VMEM((3, 2 * width, span), LOW),
        "first_recv": pltpu.VMEM((RING, 2 * width, span), LOW),
        "second_send": pltpu.VMEM((3, width, span), LOW),
        "second_recv": pltpu.VMEM((RING, width, span), LOW),
        "held": pltpu.VMEM((5, 2 * width, span), F32),
        "plain": pltpu.VMEM((2, width, span), F32),
        "turned": pltpu.VMEM((2, span, width), F32),
        "left": pltpu.VMEM((3, 4 * width, tokens), LOW),
        "low_part": pltpu.VMEM((tokens, 4 * width), LOW),
        "hidden_part": pltpu.VMEM((tokens, 4 * width), LOW),
        "stats": pltpu.VMEM((tokens, LANES), F32),
        "stats_line": pltpu.VMEM((4, 16, rows), F32),
        "row_weight": pltpu.VMEM((rows, LANES), F32),
        "attn_in": pltpu.VMEM((rows, model), LOW),
        "mlp_in": pltpu.VMEM((rows, model), LOW),
        "low": pltpu.VMEM((rows, model), LOW),
        "up_held": pltpu.VMEM((model, span), LOW),
        "down_held": pltpu.VMEM((span, model), LOW),
        "qkv_held": pltpu.VMEM((model, 3 * HS), LOW),
        "gate_held": pltpu.VMEM((HS, model), LOW),
        "dense_held": pltpu.VMEM((HS, model), LOW),
        "query": pltpu.VMEM((heads, rows, HS), LOW),
        "gate": pltpu.VMEM((heads, rows, HS), LOW),
        "kv": pltpu.VMEM((heads, tokens, 2 * HS), LOW),
        "pair": pltpu.VMEM((2 * rows, 2 * HS), F32),
        "pair_own": pltpu.VMEM((rows, 2 * HS), F32),
        "pair_send": pltpu.VMEM((2 * rows, 2 * HS), LOW),
        "pair_recv": pltpu.VMEM((heads, 2 * rows, 2 * HS), LOW),
        "pair_send_low": pltpu.VMEM((rows, 2 * HS), LOW),
        "pair_recv_low": pltpu.VMEM((heads, rows, 2 * HS), LOW),
        "late": pltpu.VMEM((late_count, rows, span), LOW),
        "branch": pltpu.VMEM((rows, model), F32),
        "grad_mlp": pltpu.VMEM((rows, model), F32),
        "grad_attn": pltpu.VMEM((rows, model), F32),
        "sum_send": pltpu.VMEM((bits, rows, model), LOW),
        "sum_recv": pltpu.VMEM((2, bits, rows, model), LOW),
        "small": pltpu.VMEM((8, small_width), F32),
        "small_full": pltpu.VMEM((8, small_width), F32),
        "small_held": pltpu.VMEM((2, 8, small_width // 4), F32),
        "small_recv": pltpu.VMEM((3, 8, small_width // 4), F32),
        "line": pltpu.VMEM((steps + 1, 8, small_width // 4), F32),
        "line_recv": pltpu.VMEM((steps, 8, small_width // 4), F32),
        "load_sem": dma((5,)),
        "part_send": dma((2, 3, 4)),
        "part_recv": dma((2, 3, 4)),
        "pass_sems": dma((2, 2, 2)),
        "stats_send": dma((3,)),
        "stats_recv": dma((3,)),
        "ctx_send": dma((RING, 3)),
        "ctx_recv": dma((RING, 3)),
        "dp_send": dma((RING, 2)),
        "dp_recv": dma((RING, 2)),
        "out_sem": dma((2,)),
        "row_sem": dma((2,)),
        "kv_send": dma((heads, 5)),
        "kv_recv": dma((heads, 5)),
        "sum_sems": dma((2, 2, bits)),
        "small_sems": dma((2, 3 + steps)),
        "spread_sems": dma((2, 3)),
        "free": pltpu.SemaphoreType.REGULAR((4,)),
    }
    names = [*inputs, *outputs, *scratch]
    results = pl.pallas_call(
        functools.partial(layer_kernel, plan, names),
        out_shape=[jax.ShapeDtypeStruct(shape, kind) for shape, kind, _ in outputs.values()],
        in_specs=[spec for _, spec in inputs.values()],
        out_specs=[spec for _, _, spec in outputs.values()],
        scratch_shapes=list(scratch.values()),
        compiler_params=pltpu.CompilerParams(
            collective_id=0, has_side_effects=True, vmem_limit_bytes=63 << 20
        ),
        name="layer",
    )(*[array for array, _ in inputs.values()])
    cuts = [
        (0, 0, model),
        (0, model, 2 * model),
        (1, 0, model),
        (1, model, 2 * model),
        (2, 0, model),
        (2, 0, model),
        (3, 0, heads * 3 * HS),
        (4, 0, units),
    ]
    layer_out, input_grad, small, down_grad, up_grad, dense_grad, qkv_grad = results
    large = [layer_out, input_grad, down_grad, up_grad, dense_grad, qkv_grad]
    shapes = [jax.ShapeDtypeStruct(array.shape, array.dtype) for array in large]
    shapes += [jax.ShapeDtypeStruct((1, high - low), F32) for _, low, high in cuts]
    done = pl.pallas_call(
        functools.partial(hand_on, cuts),
        out_shape=shapes,
        in_specs=[hbm] * len(large) + [vmem],
        out_specs=[hbm] * len(large) + [vmem] * len(cuts),
        scratch_shapes=[pltpu.VMEM(array.shape, array.dtype) for array in large]
        + [dma((2, len(large), 2))],
        compiler_params=pltpu.CompilerParams(vmem_limit_bytes=60 << 20),
        name="hand_on",
    )(*large, small)
    layer_out, input_grad, down_grad, up_grad, dense_grad, qkv_grad = done[:6]
    vectors = [vector.reshape(-1) for vector in done[6:]]
    attn_gain, attn_bias, mlp_gain, mlp_bias, dense_sum, down_sum, qkv_sum, up_sum = vectors
    shape = (seq_count, rows, model)
    return (
        layer_out.reshape(shape),
        input_grad.reshape(shape),
        attn_gain,
        attn_bias,
        qkv_grad,
        qkv_sum,
        dense_grad,
        dense_sum,
        mlp_gain,
        mlp_bias,
        up_grad,
        up_sum,
        down_grad,
        down_sum,
    )


def solution(mesh):
    return jax.shard_map(
        local,
        mesh=mesh,
        in_specs=(
            P("dp", "ctx", None),
            P(),
            P(),
            P(None, "tensor"),
            P("tensor"),
            P("tensor", None),
            P(),
            P(),
            P(),
            P(None, "tensor"),
            P("tensor"),
            P("tensor", None),
            P(),
            P("dp", "ctx", None),
            P("dp", "ctx"),
            P(),
        ),
        out_specs=(
            P("dp", "ctx", None),
            P("dp", "ctx", None),
            P(),
            P(),
            P(("dp", "ctx"), "tensor"),
            P("tensor"),
            P("tensor", ("dp", "ctx")),
            P(),
            P(),
            P(),
            P(("dp", "ctx"), "tensor"),
            P("tensor"),
            P("tensor", ("dp", "ctx")),
            P(),
        ),
        check_vma=False,
    )
```

```python
import functools
import math
import types

import jax
import jax.numpy as jnp
from jax import lax
from jax.experimental import pallas as pl
from jax.experimental.pallas import tpu as pltpu
from jax.sharding import PartitionSpec as P

HS = 256
ROT = 64
LANES = 128
RING = 8
NORM_EPS = 1e-05
MESH = pl.DeviceIdType.MESH
ORDER = (0, 2, 1, 3)
LOW = jnp.bfloat16
F32 = jnp.float32


def flip(place, bits):
    bit = 1
    while bit <= bits:
        if bits & bit:
            place = place + bit - 2 * bit * ((place // bit) % 2)
        bit *= 2
    return place


def send_to(source, target, send_sem, recv_sem, axis, bits):
    return pltpu.make_async_remote_copy(
        src_ref=source,
        dst_ref=target,
        send_sem=send_sem,
        recv_sem=recv_sem,
        device_id={axis: flip(lax.axis_index(axis), bits)},
        device_id_type=MESH,
    )


def dot(left, right):
    return jnp.dot(left, right, preferred_element_type=F32)


def dot_rows(left, right):
    return lax.dot_general(left, right, (((1,), (1,)), ((), ())), preferred_element_type=F32)


def axis_bits(axis):
    return [1 << level for level in range(lax.axis_size(axis).bit_length() - 1)]


def blocks_of(total, size):
    return pl.ds(pl.multiple_of(total * size, size), size)


def layer_kernel(plan, names, *refs):
    at = types.SimpleNamespace(**dict(zip(names, refs)))
    rows, span, count, width = plan.rows, plan.span, plan.count, plan.width
    pairs, heads, late = plan.pairs, plan.heads, 2 * plan.pairs
    attn_pieces = heads * HS // span
    per_piece = span // HS
    model = at.hidden.shape[1]
    ctx, dp = lax.axis_index("ctx"), lax.axis_index("dp")
    own_rows = pl.ds(0, rows)
    tensor_bits = axis_bits("tensor")
    halving = (("ctx", 1), ("ctx", 2), ("dp", 1), ("dp", 2))
    line_steps = halving[2:] + tuple(("tensor", bit) for bit in tensor_bits)
    scale = 1.0 / math.sqrt(HS)

    def up_load(piece):
        return pltpu.make_async_copy(
            at.up_weight.at[:, blocks_of(piece, span)], at.up_held, at.load_sem.at[0]
        )

    def up_load_aside(piece):
        return pltpu.make_async_copy(
            at.up_weight.at[:, blocks_of(piece, span)],
            at.qkv_held.at[:, pl.ds(0, span)],
            at.load_sem.at[2],
        )

    def down_load(piece):
        return pltpu.make_async_copy(
            at.down_weight.at[blocks_of(piece, span)], at.down_held, at.load_sem.at[1]
        )

    def qkv_load(head):
        return pltpu.make_async_copy(
            at.qkv_weight.at[:, blocks_of(head, 3 * HS)], at.qkv_held, at.load_sem.at[2]
        )

    def gate_load(head):
        return pltpu.make_async_copy(
            at.dense_weight.at[blocks_of(head, HS)], at.gate_held, at.load_sem.at[3]
        )

    def dense_load(head):
        return pltpu.make_async_copy(
            at.dense_weight.at[blocks_of(head, HS)], at.dense_held, at.load_sem.at[4]
        )

    shared = lax.axis_size("tensor") == 2
    side = lax.axis_index("tensor")

    def part_numbers(place):
        return range(2 if shared and place > 1 else 4)

    def part_copy(kind, place, number):
        source = (at.low, at.hidden)[kind]
        target = (at.low_part, at.hidden_part)[kind]
        block = 2 * side + number if shared and place > 1 else number
        column = block * 4 + flip(ctx, place)
        return send_to(
            source.at[:, blocks_of(column, width)],
            target.at[pl.ds(ORDER.index(place) * rows, rows), blocks_of(block, width)],
            at.part_send.at[kind, place - 1, number],
            at.part_recv.at[kind, place - 1, number],
            "ctx",
            place,
        )

    def part_pass(kind, place):
        target = (at.low_part, at.hidden_part)[kind]
        half = target.at[pl.ds(ORDER.index(place) * rows, rows), blocks_of(side, 2 * width)]
        return send_to(
            half,
            half,
            at.pass_sems.at[0, kind, place - 2],
            at.pass_sems.at[1, kind, place - 2],
            "tensor",
            1,
        )

    def part_starts(kind):
        for place in (2, 3, 1):
            for number in part_numbers(place):
                part_copy(kind, place, number).start()

    def pass_on(kind):
        for place in (2, 3):
            for number in part_numbers(place):
                part_copy(kind, place, number).wait_recv()
            if shared:
                part_pass(kind, place).start()

    def part_waits(kind):
        for number in part_numbers(1):
            part_copy(kind, 1, number).wait_recv()
        if shared:
            for place in (2, 3):
                part_pass(kind, place).wait_recv()

    def stats_copy(place):
        return send_to(
            at.stats_line.at[0],
            at.stats_line.at[ORDER.index(place)],
            at.stats_send.at[place - 1],
            at.stats_recv.at[place - 1],
            "ctx",
            place,
        )

    def across(piece):
        slot = piece % RING
        return send_to(
            at.rows_all.at[slot, own_rows],
            at.rows_all.at[slot, pl.ds(rows, rows)],
            at.ctx_send.at[slot, 0],
            at.ctx_recv.at[slot, 0],
            "ctx",
            2,
        )

    def beside(piece, part):
        slot = piece % RING
        return send_to(
            at.rows_all.at[slot, pl.ds(part * rows, rows)],
            at.rows_all.at[slot, pl.ds((2 + part) * rows, rows)],
            at.ctx_send.at[slot, 1 + part],
            at.ctx_recv.at[slot, 1 + part],
            "ctx",
            1,
        )

    def first(piece):
        return send_to(
            at.first_send.at[piece % 3],
            at.first_recv.at[piece % RING],
            at.dp_send.at[piece % RING, 0],
            at.dp_recv.at[piece % RING, 0],
            "dp",
            1,
        )

    def second(piece):
        return send_to(
            at.second_send.at[piece % 3],
            at.second_recv.at[piece % RING],
            at.dp_send.at[piece % RING, 1],
            at.dp_recv.at[piece % RING, 1],
            "dp",
            2,
        )

    def results(piece):
        slot = piece % 2
        turned, plain = at.turned.at[slot], at.plain.at[slot]
        feed = piece < late
        gives = piece < pairs
        dense = (piece >= late) & (piece < late + attn_pieces)
        return (
            (gives, turned, at.down_out.at[blocks_of(piece, span)]),
            (
                feed & jnp.logical_not(gives),
                plain,
                at.up_out.at[:, blocks_of(piece - pairs, span)],
            ),
            (dense, turned, at.dense_out.at[blocks_of(piece - late, span)]),
            (
                piece >= late + attn_pieces,
                plain,
                at.qkv_out.at[:, blocks_of(piece - late - attn_pieces, span)],
            ),
        )

    def for_result(piece, act):
        for holds, source, target in results(piece):

            @pl.when(holds)
            def _():
                act(pltpu.make_async_copy(source, target, at.out_sem.at[piece % 2]))

    def kv_across(head):
        return send_to(
            at.kv.at[head, own_rows],
            at.kv.at[head, pl.ds(rows, rows)],
            at.kv_send.at[head, 0],
            at.kv_recv.at[head, 0],
            "ctx",
            2,
        )

    def kv_beside(head, part):
        return send_to(
            at.kv.at[head, pl.ds(part * rows, rows)],
            at.kv.at[head, pl.ds((2 + part) * rows, rows)],
            at.kv_send.at[head, 1 + part],
            at.kv_recv.at[head, 1 + part],
            "ctx",
            1,
        )

    def pair_beside(head):
        return send_to(
            at.pair_send,
            at.pair_recv.at[head],
            at.kv_send.at[head, 3],
            at.kv_recv.at[head, 3],
            "ctx",
            1,
        )

    def pair_across(head):
        return send_to(
            at.pair_send_low,
            at.pair_recv_low.at[head],
            at.kv_send.at[head, 4],
            at.kv_recv.at[head, 4],
            "ctx",
            2,
        )

    def tensor_copy(which, level):
        return send_to(
            at.sum_send.at[level],
            at.sum_recv.at[which, level],
            at.sum_sems.at[0, which, level],
            at.sum_sems.at[1, which, level],
            "tensor",
            tensor_bits[level],
        )

    quarter = at.small.shape[1] // 4

    def small_half(number):
        return send_to(
            at.small.at[:, blocks_of(flip(ctx, (1, 3)[number]), quarter)],
            at.small_recv.at[number],
            at.small_sems.at[0, number],
            at.small_sems.at[1, number],
            "ctx",
            1,
        )

    def small_rest():
        return send_to(
            at.small_held.at[1],
            at.small_recv.at[2],
            at.small_sems.at[0, 2],
            at.small_sems.at[1, 2],
            "ctx",
            2,
        )

    def line_copy(entry):
        axis, bit = line_steps[entry]
        return send_to(
            at.line.at[entry],
            at.line_recv.at[entry],
            at.small_sems.at[0, 3 + entry],
            at.small_sems.at[1, 3 + entry],
            axis,
            bit,
        )

    def small_spread(place):
        return send_to(
            at.line.at[len(line_steps)],
            at.small_full.at[:, blocks_of(ctx, quarter)],
            at.spread_sems.at[0, place - 1],
            at.spread_sems.at[1, place - 1],
            "ctx",
            place,
        )

    def turn(heads_rows, back):
        start_part = heads_rows[:, :LANES]
        ahead = pltpu.roll(start_part, LANES - ROT // 2, 1) * at.sine_ahead[...]
        behind = pltpu.roll(start_part, ROT // 2, 1) * at.sine_behind[...]
        straight = start_part * at.cosine[...]
        moved = straight - ahead - behind if back else straight + ahead + behind
        return jnp.concatenate([moved, heads_rows[:, LANES:]], 1)

    def late_block(block):
        piece = attn_pieces + block // per_piece
        return at.late.at[piece, :, blocks_of(block % per_piece, HS)]

    up_load(0).start()
    up_load_aside(1).start()
    down_load(0).start()
    gate_load(0).start()
    dense_load(0).start()
    barrier = pltpu.get_barrier_semaphore()
    partners = halving[:2] + line_steps + (("ctx", 3),)
    for axis, bits in partners:
        pl.semaphore_signal(
            barrier,
            1,
            device_id={axis: flip(lax.axis_index(axis), bits)},
            device_id_type=MESH,
        )
    pl.semaphore_wait(barrier, len(partners))
    step_rows = 32
    at.small[...] = jnp.zeros_like(at.small)
    ids = at.subset_ids[...]
    weight_line = jnp.zeros(ids.shape, F32)
    for number in range(at.subset_weights.shape[0]):
        weight_line = jnp.where(ids == number, at.subset_weights[number], weight_line)
    at.row_weight[...] = jnp.broadcast_to(weight_line, (LANES, rows)).T

    def grad_of(some):
        return at.cotangent[some].astype(F32) * at.row_weight[some, pl.ds(0, 1)]

    @pl.loop(0, rows // step_rows)
    def _(block):
        some = blocks_of(block, step_rows)
        at.low[some] = grad_of(some).astype(LOW)

    part_starts(0)

    @pl.loop(0, rows // step_rows)
    def _(block):
        some = blocks_of(block, step_rows)
        inputs = at.hidden[some].astype(F32)
        mean = jnp.mean(inputs, -1, keepdims=True)
        centered = inputs - mean
        inv_std = lax.rsqrt(jnp.mean(centered * centered, -1, keepdims=True) + NORM_EPS)
        normed = centered * inv_std
        at.attn_in[some] = (normed * at.attn_gain[...] + at.attn_bias[...]).astype(LOW)
        at.mlp_in[some] = (normed * at.mlp_gain[...] + at.mlp_bias[...]).astype(LOW)
        lane = lax.broadcasted_iota(jnp.int32, (step_rows, LANES), 1)
        at.stats[some] = jnp.where(lane < LANES // 2, mean, inv_std)

    def send_hidden():
        line = at.stats[own_rows].T
        at.stats_line[0, pl.ds(0, 8)] = line[:8]
        at.stats_line[0, pl.ds(8, 8)] = line[LANES // 2 : LANES // 2 + 8]
        for place in (2, 3, 1):
            stats_copy(place).start()
        part_starts(1)
        for block in range(4):
            column = blocks_of(block * 4 + ctx, width)
            at.hidden_part[own_rows, pl.ds(block * width, width)] = at.hidden[:, column]

    def low_left():
        for block in range(4):
            column = blocks_of(block * 4 + ctx, width)
            at.low_part[own_rows, pl.ds(block * width, width)] = at.low[:, column]
        part_waits(0)
        for entry, bits in enumerate(ORDER):
            block = at.low_part[:, blocks_of(flip(dp, bits), width)]
            at.left[0, pl.ds(entry * width, width)] = block.T

    def hidden_left():
        for place in (1, 2, 3):
            stats_copy(place).wait_recv()
        part_waits(1)
        for slot in range(1, 4):
            half = lax.broadcasted_iota(jnp.int32, (LANES, rows), 0) < LANES // 2
            line = jnp.where(half, at.stats_line[slot, :1], at.stats_line[slot, 8:9])
            at.stats[pl.ds(slot * rows, rows)] = line.T
        for entry, bits in enumerate(ORDER):
            place = flip(dp, bits)
            block = at.hidden_part[:, blocks_of(place, width)].astype(F32)
            normed = (block - at.stats[:, :1]) * at.stats[:, LANES // 2 : LANES // 2 + 1]
            column = blocks_of(place * 4 + ctx, width)
            to = pl.ds(entry * width, width)
            sides = ((at.mlp_gain, at.mlp_bias), (at.attn_gain, at.attn_bias))
            for number, (gain, bias) in enumerate(sides):
                at.left[1 + number, to] = (normed * gain[:, column] + bias[:, column]).astype(LOW).T

    def start_piece(piece):
        @pl.when(piece >= RING)
        def _():
            pl.semaphore_wait(at.free.at[0], 1)
            pl.semaphore_wait(at.free.at[1], 1)

        @pl.when(piece >= late)
        def _():
            at.rows_all[piece % RING, own_rows] = at.late[piece - late]

        across(piece).start()
        beside(piece, 0).start()

    def pre_act(pair, weights):
        pre = dot(at.mlp_in[...], weights) + at.up_bias[:, blocks_of(pair, span)]
        return pre, 0.5 * (1.0 + lax.erf(pre * math.sqrt(0.5)))

    def activate(pair):
        if pair in (1, 3):
            up_load_aside(pair).wait()
            pre, cumulative = pre_act(pair, at.qkv_held[:, :span])
        else:
            up_load(pair).wait()
            pre, cumulative = pre_act(pair, at.up_held[...])
        at.rows_all[pair % RING, own_rows] = (pre * cumulative).astype(LOW)
        start_piece(pair)
        if pair == 1:
            up_load_aside(3).start()
        elif pair == 3:
            qkv_load(0).start()
        else:
            following = {0: 2, 2: 4}.get(pair, pair + 1)
            up_load(following if following < pairs else 0).start()
        if pair == max(pairs - 2, 3):
            send_hidden()

    def feed_forward(pair):
        up_load(pair).wait()
        down_load(pair).wait()
        pre, cumulative = pre_act(pair, at.up_held[...])
        given = (pre * cumulative).astype(LOW)
        grad_act = dot_rows(at.low[...], at.down_held[...])
        density = jnp.exp(-0.5 * pre * pre) * (1.0 / math.sqrt(2.0 * math.pi))
        grad_pre = (grad_act * (cumulative + pre * density)).astype(LOW)
        at.rows_all[(pairs + pair) % RING, own_rows] = grad_pre
        at.small[pl.ds(4, 1), blocks_of(pair, span)] = jnp.sum(
            grad_pre.astype(F32), 0, keepdims=True
        )
        start_piece(pairs + pair)

        @pl.when(pair == 0)
        def _():
            for held in (at.branch, at.grad_mlp, at.grad_attn):
                held[...] = jnp.zeros_like(held)

        at.branch[...] += dot(given, at.down_held[...])
        at.grad_mlp[...] += dot_rows(grad_pre, at.up_held[...])

        @pl.when(pair + 1 < pairs)
        def _():
            up_load(pair + 1).start()
            down_load(pair + 1).start()

    def project(head):
        qkv_load(head).wait()
        out = dot(at.attn_in[...], at.qkv_held[...]) + at.qkv_bias[:, blocks_of(head, 3 * HS)]
        at.kv[head, own_rows, pl.ds(0, HS)] = turn(out[:, HS : 2 * HS], False).astype(LOW)
        at.kv[head, own_rows, pl.ds(HS, HS)] = out[:, 2 * HS :].astype(LOW)

        @pl.when(ctx < 2)
        def _():
            kv_across(head).start()

        kv_beside(head, 0).start()
        at.query[head] = turn(out[:, :HS], False).astype(LOW)
        gate_load(head).wait()
        at.gate[head] = dot_rows(at.low[...], at.gate_held[...]).astype(LOW)
        qkv_load((head + 1) % heads).start()

        @pl.when(head + 1 < heads)
        def _():
            gate_load(head + 1).start()

    def kv_forward(head):
        @pl.when(ctx >= 2)
        def _():
            kv_across(head).wait_recv()
            kv_beside(head, 1).start()

        @pl.when(ctx < 2)
        def _():
            for slot in (1, 3):
                at.kv[head, pl.ds(slot * rows, rows)] = jnp.zeros((rows, 2 * HS), LOW)

    def attend(head):
        kv_beside(head, 0).wait_recv()

        @pl.when(ctx >= 2)
        def _():
            kv_beside(head, 1).wait_recv()

        query, gate = at.query[head], at.gate[head]
        keys, values = at.kv[head, :, :HS], at.kv[head, :, HS:]
        shape = (rows, 4 * rows)
        key_place = lax.broadcasted_iota(jnp.int32, shape, 1)
        shift = jnp.full(shape, flip(ctx, ORDER[3]) * rows - 3 * rows, jnp.int32)
        for entry in (2, 1, 0):
            here = flip(ctx, ORDER[entry]) * rows - entry * rows
            shift = jnp.where(key_place < (entry + 1) * rows, here, shift)
        query_place = lax.broadcasted_iota(jnp.int32, shape, 0) + ctx * rows
        scores = jnp.where(
            key_place + shift <= query_place, dot_rows(query, keys) * scale, -1e30
        )
        expd = jnp.exp(scores - jnp.max(scores, -1, keepdims=True))
        prob = expd * (1.0 / jnp.sum(expd, -1, keepdims=True))
        prob_low = prob.astype(LOW)
        attended = dot(prob_low, values).astype(LOW)
        at.late[head // per_piece, :, blocks_of(head % per_piece, HS)] = attended
        grad_prob = dot_rows(gate, values)
        delta = jnp.sum(grad_prob * prob, -1, keepdims=True)
        grad_scores = (prob * (grad_prob - delta)).astype(LOW)
        grad_key = dot(grad_scores.T, query) * scale
        grad_value = dot(prob_low.T, gate)
        at.pair_send[:, pl.ds(0, HS)] = grad_key[2 * rows :].astype(LOW)
        at.pair_send[:, pl.ds(HS, HS)] = grad_value[2 * rows :].astype(LOW)
        pair_beside(head).start()
        at.pair[:, pl.ds(0, HS)] = grad_key[: 2 * rows]
        at.pair[:, pl.ds(HS, HS)] = grad_value[: 2 * rows]
        late_block(3 * head)[...] = turn(dot(grad_scores, keys) * scale, True).astype(LOW)
        dense_load(head).wait()
        at.branch[...] += dot(attended, at.dense_held[...])

        @pl.when(head + 1 < heads)
        def _():
            dense_load(head + 1).start()

    def pair_halve(head):
        pair_beside(head).wait()

        @pl.when(ctx >= 2)
        def _():
            other = pl.ds(rows, rows)
            at.pair_send_low[...] = (
                at.pair[other] + at.pair_recv[head, other].astype(F32)
            ).astype(LOW)
            pair_across(head).start()

        at.pair_own[...] = at.pair[own_rows] + at.pair_recv[head, own_rows].astype(F32)

    def pair_finish(head):
        @pl.when(ctx < 2)
        def _():
            pair_across(head).wait_recv()
            at.pair_own[...] += at.pair_recv_low[head].astype(F32)

        @pl.when(ctx >= 2)
        def _():
            pair_across(head).wait_send()

        total = at.pair_own[...]
        late_block(3 * head + 1)[...] = turn(total[:, :HS], True).astype(LOW)
        late_block(3 * head + 2)[...] = total[:, HS:].astype(LOW)
        for number in range(3):
            at.small[pl.ds(3, 1), blocks_of(3 * head + number, HS)] = jnp.sum(
                late_block(3 * head + number)[...].astype(F32), 0, keepdims=True
            )

    def project_back(head):
        qkv_load(head).wait()
        at.grad_attn[...] += (
            dot_rows(late_block(3 * head)[...], at.qkv_held[:, :HS])
            + dot_rows(late_block(3 * head + 1)[...], at.qkv_held[:, HS : 2 * HS])
            + dot_rows(late_block(3 * head + 2)[...], at.qkv_held[:, 2 * HS :])
        )

        @pl.when(head + 1 < heads)
        def _():
            qkv_load(head + 1).start()

    def branch_send():
        at.sum_send[0] = at.branch[...].astype(LOW)
        tensor_copy(0, 0).start()

    def tensor_step(which, level):
        tensor_copy(which, level).wait()
        if level + 1 < len(tensor_bits):
            at.sum_send[level + 1] = (
                at.sum_send[level].astype(F32) + at.sum_recv[which, level].astype(F32)
            ).astype(LOW)
            tensor_copy(which, level + 1).start()
            return

        @pl.loop(0, rows // step_rows)
        def _(block):
            some = blocks_of(block, step_rows)
            total = at.sum_send[level, some].astype(F32) + at.sum_recv[which, level, some].astype(
                F32
            )
            if which == 0:
                total = (
                    at.hidden[some].astype(F32) + total + at.dense_bias[...] + at.down_bias[...]
                )
                at.mlp_in[some] = total.astype(LOW)
            else:
                at.attn_in[some] = (grad_of(some) + total).astype(LOW)

        row_result(which).start()

    def row_result(which):
        source = (at.mlp_in, at.attn_in)[which]
        target = (at.layer_out, at.input_grad)[which]
        return pltpu.make_async_copy(source, target, at.row_sem.at[which])

    def norm_back():
        @pl.loop(0, rows // step_rows)
        def _(block):
            some = blocks_of(block, step_rows)
            stats = at.stats[some]
            inv_std = stats[:, LANES // 2 : LANES // 2 + 1]
            normed = (at.hidden[some].astype(F32) - stats[:, :1]) * inv_std
            grad_attn, grad_mlp = at.grad_attn[some], at.grad_mlp[some]
            at.small[pl.ds(2, 1), pl.ds(0, model)] += jnp.sum(grad_of(some), 0, keepdims=True)
            for row, grad in enumerate((grad_attn, grad_mlp)):
                at.small[pl.ds(row, 1), pl.ds(0, model)] += jnp.sum(
                    grad * normed, 0, keepdims=True
                )
                at.small[pl.ds(row, 1), pl.ds(model, model)] += jnp.sum(grad, 0, keepdims=True)
            grad = grad_attn * at.attn_gain[...] + grad_mlp * at.mlp_gain[...]
            part = inv_std * (
                grad
                - jnp.mean(grad, -1, keepdims=True)
                - normed * jnp.mean(grad * normed, -1, keepdims=True)
            )
            at.sum_send[0, some] = part.astype(LOW)

        tensor_copy(1, 0).start()
        for number in range(2):
            small_half(number).start()

    def small_step(entry):
        if entry == 0:
            for number in range(2):
                small_half(number).wait()
                mine = blocks_of(flip(ctx, 2 * number), quarter)
                at.small_held[number] = at.small[:, mine] + at.small_recv[number]
            small_rest().start()
            return
        if entry == 1:
            small_rest().wait()
            at.line[0] = at.small_held[0] + at.small_recv[2]
        else:
            line_copy(entry - 2).wait()
            added = at.line[entry - 2] + at.line_recv[entry - 2]
            if line_steps[entry - 2][0] == "tensor":
                row = lax.broadcasted_iota(jnp.int32, added.shape, 0)
                added = jnp.where(row < 2, added, at.line[entry - 2])
            at.line[entry - 1] = added
        if entry - 1 < len(line_steps):
            line_copy(entry - 1).start()
            return
        for place in (2, 3, 1):
            small_spread(place).start()
        at.small_full[:, blocks_of(ctx, quarter)] = at.line[len(line_steps)]

    def small_finish():
        for place in (1, 2, 3):
            small_spread(place).wait()
        at.small_out[...] = at.small_full[...]

    lead = 3
    assert pairs in (4, 8)

    def places(base, *lags):
        return [
            [base + 2 * head + sum(lags[:stage]) for stage in range(5)] for head in range(heads)
        ]

    def in_time(jobs):
        for piece in range(attn_pieces):
            if jobs[(piece + 1) * per_piece - 1][2] > late + piece - lead:
                return False
        for block in range(3 * heads):
            if jobs[block // 3][4] > late + attn_pieces + block // per_piece - lead:
                return False
        return True

    jobs = next(pace for pace in (places(1, 5, 2, 2, 2), places(2, 1, 1, 1, 1)) if in_time(pace))
    project_at, forward_at, attend_at, halve_at, finish_at = jobs[0]
    feed_at = max(pairs - 4, 1)
    feed_end = feed_at + pairs - 1
    branch_at = max(attend_at + 2 * (heads - 1), feed_end) + 1
    back_at = max(finish_at + 2 * (heads - 1) + 2, branch_at + 4 * len(tensor_bits) + 1)
    total_steps = max(
        count + 5, back_at + 5 + len(line_steps), back_at + 4 * len(tensor_bits) + 1
    )

    def step(turn_number, carry):
        now = turn_number - 2

        def job(start, stride, times, act):
            index = now - start

            @pl.when((index >= 0) & (index < stride * times) & (index % stride == 0))
            def _():
                act(index // stride)

        multiply = now - 1

        @pl.when((multiply >= 0) & (multiply < count))
        def _():
            beside(multiply, 0).wait_recv()
            beside(multiply, 1).wait_recv()

            @pl.when(multiply >= RING)
            def _():
                pl.semaphore_wait(at.free.at[2], 1)

            @pl.when(multiply >= 3)
            def _():
                first(multiply - 3).wait_send()

            feed = multiply < late
            group = jnp.where(
                feed,
                jnp.where(multiply < pairs, 0, 1),
                jnp.where(multiply < late + attn_pieces, 0, 2),
            )
            at.first_send[multiply % 3] = dot(
                at.left[group, pl.ds(2 * width, 2 * width)], at.rows_all[multiply % RING]
            ).astype(LOW)
            first(multiply).start()
            at.held[multiply % 5] = dot(
                at.left[group, pl.ds(0, 2 * width)], at.rows_all[multiply % RING]
            )

        add = now - 3

        @pl.when((add >= 0) & (add < count))
        def _():
            first(add).wait_recv()

            @pl.when(add >= RING)
            def _():
                pl.semaphore_wait(at.free.at[3], 1)

            @pl.when(add >= 3)
            def _():
                second(add - 3).wait_send()

            lower = pl.ds(width, width)
            at.second_send[add % 3] = (
                at.held[add % 5, lower] + at.first_recv[add % RING, lower].astype(F32)
            ).astype(LOW)
            second(add).start()

        last = now - 5

        @pl.when((last >= 0) & (last < count))
        def _():
            second(last).wait_recv()

            @pl.when(last >= 2)
            def _():
                for_result(last - 2, lambda copy: copy.wait())

            upper = pl.ds(0, width)
            total = (
                at.held[last % 5, upper]
                + at.first_recv[last % RING, upper].astype(F32)
                + at.second_recv[last % RING].astype(F32)
            )
            flat = ((last < late) & (last >= pairs)) | (last >= late + attn_pieces)

            @pl.when(flat)
            def _():
                at.plain[last % 2] = total

            @pl.when(jnp.logical_not(flat))
            def _():
                at.turned[last % 2] = total.T

            for_result(last, lambda copy: copy.start())

            @pl.when(last < count - RING)
            def _():
                for number, bit in ((2, 1), (3, 2)):
                    pl.semaphore_signal(
                        at.free.at[number],
                        1,
                        device_id={"dp": flip(dp, bit)},
                        device_id_type=MESH,
                    )

        @pl.when((now >= 0) & (now < count))
        def _():
            across(now).wait_recv()
            beside(now, 1).start()

        sent = now - 1

        @pl.when((sent >= 0) & (sent < count))
        def _():
            across(sent).wait_send()
            beside(sent, 0).wait_send()
            beside(sent, 1).wait_send()

            @pl.when(sent < count - RING)
            def _():
                for number, bit in ((0, 2), (1, 1)):
                    pl.semaphore_signal(
                        at.free.at[number],
                        1,
                        device_id={"ctx": flip(ctx, bit)},
                        device_id_type=MESH,
                    )

        for pair, place in enumerate((-2, -2, -1, 0, 1, 2, 3, 3)[:pairs]):
            job(place, 1, 1, lambda _: activate(pair))
            if pair == 0:
                job(-2, 1, 1, lambda _: pass_on(0))
            if pair == 3:
                job(0, 1, 1, lambda _: low_left())
        job(pairs - 2, 1, 1, lambda _: pass_on(1))
        job(pairs - 1, 1, 1, lambda _: hidden_left())
        job(feed_at, 1, pairs, feed_forward)
        job(project_at, 2, heads, project)
        job(forward_at, 2, heads, kv_forward)
        job(finish_at, 2, heads, pair_finish)
        job(halve_at, 2, heads, pair_halve)
        job(attend_at, 2, heads, attend)
        job(finish_at + 1, 2, heads, project_back)
        job(branch_at, 1, 1, lambda _: branch_send())
        for level in range(len(tensor_bits)):
            job(branch_at + 4 * (level + 1), 1, 1, lambda _: tensor_step(0, level))
        job(back_at, 1, 1, lambda _: norm_back())
        for level in range(len(tensor_bits)):
            job(back_at + 4 * (level + 1), 1, 1, lambda _: tensor_step(1, level))
        for entry in range(len(line_steps) + 2):
            job(back_at + 1 + entry, 1, 1, lambda _: small_step(entry))
        job(back_at + 3 + len(line_steps), 1, 1, lambda _: small_finish())

        @pl.when((now + lead >= late) & (now + lead < count))
        def _():
            start_piece(now + lead)

        return carry

    lax.fori_loop(0, total_steps + 2, step, 0)

    for place in (1, 2, 3):
        stats_copy(place).wait_send()
        for kind in range(2):
            for number in part_numbers(place):
                part_copy(kind, place, number).wait_send()
            if shared and place > 1:
                part_pass(kind, place).wait_send()

    @pl.loop(0, heads)
    def _(head):
        kv_beside(head, 0).wait_send()

        @pl.when(ctx < 2)
        def _():
            kv_across(head).wait_send()

        @pl.when(ctx >= 2)
        def _():
            kv_beside(head, 1).wait_send()

    @pl.loop(count - 3, count)
    def _(piece):
        first(piece).wait_send()
        second(piece).wait_send()

        @pl.when(piece >= count - 2)
        def _():
            for_result(piece, lambda copy: copy.wait())

    row_result(0).wait()
    row_result(1).wait()


def hand_on(cuts, *refs):
    whole = 6
    sources, small = refs[:whole], refs[whole]
    targets, refs = refs[whole + 1 : 2 * whole + 1], refs[2 * whole + 1 :]
    pieces, refs = refs[: len(cuts)], refs[len(cuts) :]
    held, sem = refs[:whole], refs[whole]

    def halves(ref):
        size = ref.shape[0] // 2
        return [ref.at[pl.ds(half * size, size)] for half in range(2)]

    copies = []
    for number in range(whole):
        parts = zip(halves(sources[number]), halves(held[number]), halves(targets[number]))
        for half, (source, middle, target) in enumerate(parts):
            copies.append(
                (
                    pltpu.make_async_copy(source, middle, sem.at[0, number, half]),
                    pltpu.make_async_copy(middle, target, sem.at[1, number, half]),
                )
            )
    for fetch, _ in copies:
        fetch.start()
    for piece, (row, low, high) in zip(pieces, cuts):
        piece[...] = small[row : row + 1, low:high]
    for fetch, put in copies:
        fetch.wait()
        put.start()
    for _, put in copies:
        put.wait()


def local(
    hidden_in,
    attn_norm_gain,
    attn_norm_bias,
    qkv_weight,
    qkv_bias,
    dense_weight,
    dense_bias,
    mlp_norm_gain,
    mlp_norm_bias,
    up_weight,
    up_bias,
    down_weight,
    down_bias,
    out_cotangent,
    subset_ids,
    subset_weights,
):
    seq_count, rows, model = hidden_in.shape
    heads = qkv_weight.shape[1] // (3 * HS)
    units = up_weight.shape[1]
    width = model // (lax.axis_size("dp") * lax.axis_size("ctx"))
    span = min(512, math.gcd(units, heads * HS, heads * 3 * HS))
    pairs = units // span
    late_count = heads * 4 * HS // span
    plan = types.SimpleNamespace(
        rows=rows, span=span, width=width, pairs=pairs, heads=heads, count=2 * pairs + late_count
    )
    tokens = rows * lax.axis_size("ctx")

    half = ROT // 2
    lane = jnp.arange(LANES, dtype=jnp.int32)[None, :]
    positions = lax.axis_index("ctx") * rows + jnp.arange(rows, dtype=jnp.int32)
    freqs = 10000.0 ** (-((lane % half).astype(F32) * 2.0 / ROT))
    table = positions.astype(F32)[:, None] * freqs
    sine = jnp.sin(table)
    cosine = jnp.where(lane < ROT, jnp.cos(table), 1.0)
    sine_ahead = jnp.where(lane < half, -sine, 0.0)
    sine_behind = jnp.where((lane >= half) & (lane < ROT), sine, 0.0)

    bits = lax.axis_size("tensor").bit_length() - 1
    steps = 2 + bits
    small_width = max(2 * model, units, heads * 3 * HS)
    dma = pltpu.SemaphoreType.DMA
    vmem = pl.BlockSpec(memory_space=pltpu.VMEM)
    hbm = pl.BlockSpec(memory_space=pl.ANY)
    inputs = {
        "hidden": (hidden_in.reshape(rows, model), vmem),
        "cotangent": (out_cotangent.reshape(rows, model), vmem),
        "subset_ids": (subset_ids, vmem),
        "subset_weights": (subset_weights, pl.BlockSpec(memory_space=pltpu.SMEM)),
        "cosine": (cosine, vmem),
        "sine_ahead": (sine_ahead, vmem),
        "sine_behind": (sine_behind, vmem),
        "attn_gain": (attn_norm_gain[None], vmem),
        "attn_bias": (attn_norm_bias[None], vmem),
        "mlp_gain": (mlp_norm_gain[None], vmem),
        "mlp_bias": (mlp_norm_bias[None], vmem),
        "dense_bias": (dense_bias[None], vmem),
        "down_bias": (down_bias[None], vmem),
        "qkv_bias": (qkv_bias[None], vmem),
        "up_bias": (up_bias[None], vmem),
        "qkv_weight": (qkv_weight, hbm),
        "dense_weight": (dense_weight, hbm),
        "up_weight": (up_weight, hbm),
        "down_weight": (down_weight, hbm),
    }
    outputs = {
        "layer_out": ((rows, model), LOW, hbm),
        "input_grad": ((rows, model), LOW, hbm),
        "small_out": ((8, small_width), F32, vmem),
        "down_out": ((units, width), F32, hbm),
        "up_out": ((width, units), F32, hbm),
        "dense_out": ((heads * HS, width), F32, hbm),
        "qkv_out": ((width, heads * 3 * HS), F32, hbm),
    }
    scratch = {
        "rows_all": pltpu.VMEM((RING, tokens, span), LOW),
        "first_send": pltpu.VMEM((3, 2 * width, span), LOW),
        "first_recv": pltpu.VMEM((RING, 2 * width, span), LOW),
        "second_send": pltpu.VMEM((3, width, span), LOW),
        "second_recv": pltpu.VMEM((RING, width, span), LOW),
        "held": pltpu.VMEM((5, 2 * width, span), F32),
        "plain": pltpu.VMEM((2, width, span), F32),
        "turned": pltpu.VMEM((2, span, width), F32),
        "left": pltpu.VMEM((3, 4 * width, tokens), LOW),
        "low_part": pltpu.VMEM((tokens, 4 * width), LOW),
        "hidden_part": pltpu.VMEM((tokens, 4 * width), LOW),
        "stats": pltpu.VMEM((tokens, LANES), F32),
        "stats_line": pltpu.VMEM((4, 16, rows), F32),
        "row_weight": pltpu.VMEM((rows, LANES), F32),
        "attn_in": pltpu.VMEM((rows, model), LOW),
        "mlp_in": pltpu.VMEM((rows, model), LOW),
        "low": pltpu.VMEM((rows, model), LOW),
        "up_held": pltpu.VMEM((model, span), LOW),
        "down_held": pltpu.VMEM((span, model), LOW),
        "qkv_held": pltpu.VMEM((model, 3 * HS), LOW),
        "gate_held": pltpu.VMEM((HS, model), LOW),
        "dense_held": pltpu.VMEM((HS, model), LOW),
        "query": pltpu.VMEM((heads, rows, HS), LOW),
        "gate": pltpu.VMEM((heads, rows, HS), LOW),
        "kv": pltpu.VMEM((heads, tokens, 2 * HS), LOW),
        "pair": pltpu.VMEM((2 * rows, 2 * HS), F32),
        "pair_own": pltpu.VMEM((rows, 2 * HS), F32),
        "pair_send": pltpu.VMEM((2 * rows, 2 * HS), LOW),
        "pair_recv": pltpu.VMEM((heads, 2 * rows, 2 * HS), LOW),
        "pair_send_low": pltpu.VMEM((rows, 2 * HS), LOW),
        "pair_recv_low": pltpu.VMEM((heads, rows, 2 * HS), LOW),
        "late": pltpu.VMEM((late_count, rows, span), LOW),
        "branch": pltpu.VMEM((rows, model), F32),
        "grad_mlp": pltpu.VMEM((rows, model), F32),
        "grad_attn": pltpu.VMEM((rows, model), F32),
        "sum_send": pltpu.VMEM((bits, rows, model), LOW),
        "sum_recv": pltpu.VMEM((2, bits, rows, model), LOW),
        "small": pltpu.VMEM((8, small_width), F32),
        "small_full": pltpu.VMEM((8, small_width), F32),
        "small_held": pltpu.VMEM((2, 8, small_width // 4), F32),
        "small_recv": pltpu.VMEM((3, 8, small_width // 4), F32),
        "line": pltpu.VMEM((steps + 1, 8, small_width // 4), F32),
        "line_recv": pltpu.VMEM((steps, 8, small_width // 4), F32),
        "load_sem": dma((5,)),
        "part_send": dma((2, 3, 4)),
        "part_recv": dma((2, 3, 4)),
        "pass_sems": dma((2, 2, 2)),
        "stats_send": dma((3,)),
        "stats_recv": dma((3,)),
        "ctx_send": dma((RING, 3)),
        "ctx_recv": dma((RING, 3)),
        "dp_send": dma((RING, 2)),
        "dp_recv": dma((RING, 2)),
        "out_sem": dma((2,)),
        "row_sem": dma((2,)),
        "kv_send": dma((heads, 5)),
        "kv_recv": dma((heads, 5)),
        "sum_sems": dma((2, 2, bits)),
        "small_sems": dma((2, 3 + steps)),
        "spread_sems": dma((2, 3)),
        "free": pltpu.SemaphoreType.REGULAR((4,)),
    }
    names = [*inputs, *outputs, *scratch]
    results = pl.pallas_call(
        functools.partial(layer_kernel, plan, names),
        out_shape=[jax.ShapeDtypeStruct(shape, kind) for shape, kind, _ in outputs.values()],
        in_specs=[spec for _, spec in inputs.values()],
        out_specs=[spec for _, _, spec in outputs.values()],
        scratch_shapes=list(scratch.values()),
        compiler_params=pltpu.CompilerParams(
            collective_id=0, has_side_effects=True, vmem_limit_bytes=63 << 20
        ),
        name="layer",
    )(*[array for array, _ in inputs.values()])
    cuts = [
        (0, 0, model),
        (0, model, 2 * model),
        (1, 0, model),
        (1, model, 2 * model),
        (2, 0, model),
        (2, 0, model),
        (3, 0, heads * 3 * HS),
        (4, 0, units),
    ]
    layer_out, input_grad, small, down_grad, up_grad, dense_grad, qkv_grad = results
    large = [layer_out, input_grad, down_grad, up_grad, dense_grad, qkv_grad]
    shapes = [jax.ShapeDtypeStruct(array.shape, array.dtype) for array in large]
    shapes += [jax.ShapeDtypeStruct((1, high - low), F32) for _, low, high in cuts]
    done = pl.pallas_call(
        functools.partial(hand_on, cuts),
        out_shape=shapes,
        in_specs=[hbm] * len(large) + [vmem],
        out_specs=[hbm] * len(large) + [vmem] * len(cuts),
        scratch_shapes=[pltpu.VMEM(array.shape, array.dtype) for array in large]
        + [dma((2, len(large), 2))],
        compiler_params=pltpu.CompilerParams(vmem_limit_bytes=60 << 20),
        name="hand_on",
    )(*large, small)
    layer_out, input_grad, down_grad, up_grad, dense_grad, qkv_grad = done[:6]
    vectors = [vector.reshape(-1) for vector in done[6:]]
    attn_gain, attn_bias, mlp_gain, mlp_bias, dense_sum, down_sum, qkv_sum, up_sum = vectors
    shape = (seq_count, rows, model)
    return (
        layer_out.reshape(shape),
        input_grad.reshape(shape),
        attn_gain,
        attn_bias,
        qkv_grad,
        qkv_sum,
        dense_grad,
        dense_sum,
        mlp_gain,
        mlp_bias,
        up_grad,
        up_sum,
        down_grad,
        down_sum,
    )


def solution(mesh):
    return jax.shard_map(
        local,
        mesh=mesh,
        in_specs=(
            P("dp", "ctx", None),
            P(),
            P(),
            P(None, "tensor"),
            P("tensor"),
            P("tensor", None),
            P(),
            P(),
            P(),
            P(None, "tensor"),
            P("tensor"),
            P("tensor", None),
            P(),
            P("dp", "ctx", None),
            P("dp", "ctx"),
            P(),
        ),
        out_specs=(
            P("dp", "ctx", None),
            P("dp", "ctx", None),
            P(),
            P(),
            P(("dp", "ctx"), "tensor"),
            P("tensor"),
            P("tensor", ("dp", "ctx")),
            P(),
            P(),
            P(),
            P(("dp", "ctx"), "tensor"),
            P("tensor"),
            P("tensor", ("dp", "ctx")),
            P(),
        ),
        check_vma=False,
    )
```

```python
import functools
import math
import types

import jax
import jax.numpy as jnp
import numpy as np
from jax import lax
from jax.experimental import pallas as pl
from jax.experimental.pallas import tpu as pltpu
from jax.sharding import PartitionSpec as P

HS = 256
ROT = 64
LANES = 128
RING = 8
NORM_EPS = 1e-05
MESH = pl.DeviceIdType.MESH
ORDER = (0, 2, 1, 3)
LOW = jnp.bfloat16
F32 = jnp.float32


def flip(place, bits):
    bit = 1
    while bit <= bits:
        if bits & bit:
            place = place + bit - 2 * bit * ((place // bit) % 2)
        bit *= 2
    return place


def send_to(source, target, send_sem, recv_sem, axis, bits):
    return pltpu.make_async_remote_copy(
        src_ref=source,
        dst_ref=target,
        send_sem=send_sem,
        recv_sem=recv_sem,
        device_id={axis: flip(lax.axis_index(axis), bits)},
        device_id_type=MESH,
    )


def dot(left, right):
    return jnp.dot(left, right, preferred_element_type=F32)


def dot_rows(left, right):
    return lax.dot_general(left, right, (((1,), (1,)), ((), ())), preferred_element_type=F32)


def axis_bits(axis):
    return [1 << level for level in range(lax.axis_size(axis).bit_length() - 1)]


def blocks_of(total, size):
    return pl.ds(pl.multiple_of(total * size, size), size)


def layer_kernel(plan, names, *refs):
    at = types.SimpleNamespace(**dict(zip(names, refs)))
    rows, span, count, width = plan.rows, plan.span, plan.count, plan.width
    pairs, heads, late = plan.pairs, plan.heads, 2 * plan.pairs
    attn_pieces = heads * HS // span
    per_piece = span // HS
    model = at.hidden.shape[1]
    ctx, dp = lax.axis_index("ctx"), lax.axis_index("dp")
    own_rows = pl.ds(0, rows)
    tensor_bits = axis_bits("tensor")
    halving = (("ctx", 1), ("ctx", 2), ("dp", 1), ("dp", 2))
    line_steps = halving[2:] + tuple(("tensor", bit) for bit in tensor_bits)
    scale = 1.0 / math.sqrt(HS)

    def up_load(piece):
        return pltpu.make_async_copy(
            at.up_weight.at[:, blocks_of(piece, span)], at.up_held, at.load_sem.at[0]
        )

    def up_load_aside(piece):
        return pltpu.make_async_copy(
            at.up_weight.at[:, blocks_of(piece, span)],
            at.qkv_held.at[:, pl.ds(0, span)],
            at.load_sem.at[2],
        )

    def down_load(piece):
        return pltpu.make_async_copy(
            at.down_weight.at[blocks_of(piece, span)], at.down_held, at.load_sem.at[1]
        )

    def qkv_load(head):
        return pltpu.make_async_copy(
            at.qkv_weight.at[:, blocks_of(head, 3 * HS)], at.qkv_held, at.load_sem.at[2]
        )

    def gate_load(head):
        return pltpu.make_async_copy(
            at.dense_weight.at[blocks_of(head, HS)], at.gate_held, at.load_sem.at[3]
        )

    def dense_load(head):
        return pltpu.make_async_copy(
            at.dense_weight.at[blocks_of(head, HS)], at.dense_held, at.load_sem.at[4]
        )

    shared = lax.axis_size("tensor") == 2
    side = lax.axis_index("tensor")

    def part_numbers(place):
        return range(2 if shared and place > 1 else 4)

    def part_copy(kind, place, number):
        source = (at.low, at.hidden)[kind]
        target = (at.low_part, at.hidden_part)[kind]
        block = 2 * side + number if shared and place > 1 else number
        column = block * 4 + flip(ctx, place)
        return send_to(
            source.at[:, blocks_of(column, width)],
            target.at[pl.ds(ORDER.index(place) * rows, rows), blocks_of(block, width)],
            at.part_send.at[kind, place - 1, number],
            at.part_recv.at[kind, place - 1, number],
            "ctx",
            place,
        )

    def part_pass(kind, place):
        target = (at.low_part, at.hidden_part)[kind]
        half = target.at[pl.ds(ORDER.index(place) * rows, rows), blocks_of(side, 2 * width)]
        return send_to(
            half,
            half,
            at.pass_sems.at[0, kind, place - 2],
            at.pass_sems.at[1, kind, place - 2],
            "tensor",
            1,
        )

    def part_starts(kind):
        for place in (2, 3, 1):
            for number in part_numbers(place):
                part_copy(kind, place, number).start()

    def pass_on(kind):
        for place in (2, 3):
            for number in part_numbers(place):
                part_copy(kind, place, number).wait_recv()
            if shared:
                part_pass(kind, place).start()

    def part_waits(kind):
        for number in part_numbers(1):
            part_copy(kind, 1, number).wait_recv()
        if shared:
            for place in (2, 3):
                part_pass(kind, place).wait_recv()

    def stats_copy(place):
        return send_to(
            at.stats_line.at[0],
            at.stats_line.at[ORDER.index(place)],
            at.stats_send.at[place - 1],
            at.stats_recv.at[place - 1],
            "ctx",
            place,
        )

    def across(piece):
        slot = piece % RING
        return send_to(
            at.rows_all.at[slot, own_rows],
            at.rows_all.at[slot, pl.ds(rows, rows)],
            at.ctx_send.at[slot, 0],
            at.ctx_recv.at[slot, 0],
            "ctx",
            2,
        )

    def beside(piece, part):
        slot = piece % RING
        return send_to(
            at.rows_all.at[slot, pl.ds(part * rows, rows)],
            at.rows_all.at[slot, pl.ds((2 + part) * rows, rows)],
            at.ctx_send.at[slot, 1 + part],
            at.ctx_recv.at[slot, 1 + part],
            "ctx",
            1,
        )

    def first(piece):
        return send_to(
            at.first_send.at[piece % 3],
            at.first_recv.at[piece % RING],
            at.dp_send.at[piece % RING, 0],
            at.dp_recv.at[piece % RING, 0],
            "dp",
            1,
        )

    def second(piece):
        return send_to(
            at.second_send.at[piece % 3],
            at.second_recv.at[piece % RING],
            at.dp_send.at[piece % RING, 1],
            at.dp_recv.at[piece % RING, 1],
            "dp",
            2,
        )

    def results(piece):
        slot = piece % 2
        turned, plain = at.turned.at[slot], at.plain.at[slot]
        feed = piece < late
        gives = piece < pairs
        dense = (piece >= late) & (piece < late + attn_pieces)
        return (
            (gives, turned, at.down_out.at[blocks_of(piece, span)]),
            (
                feed & jnp.logical_not(gives),
                plain,
                at.up_out.at[:, blocks_of(piece - pairs, span)],
            ),
            (dense, turned, at.dense_out.at[blocks_of(piece - late, span)]),
            (
                piece >= late + attn_pieces,
                plain,
                at.qkv_out.at[:, blocks_of(piece - late - attn_pieces, span)],
            ),
        )

    def for_result(piece, act):
        for holds, source, target in results(piece):

            @pl.when(holds)
            def _():
                act(pltpu.make_async_copy(source, target, at.out_sem.at[piece % 2]))

    def kv_across(head):
        return send_to(
            at.kv.at[head, own_rows],
            at.kv.at[head, pl.ds(rows, rows)],
            at.kv_send.at[head, 0],
            at.kv_recv.at[head, 0],
            "ctx",
            2,
        )

    def kv_beside(head, part):
        return send_to(
            at.kv.at[head, pl.ds(part * rows, rows)],
            at.kv.at[head, pl.ds((2 + part) * rows, rows)],
            at.kv_send.at[head, 1 + part],
            at.kv_recv.at[head, 1 + part],
            "ctx",
            1,
        )

    def pair_beside(head):
        return send_to(
            at.pair_send,
            at.pair_recv.at[head],
            at.kv_send.at[head, 3],
            at.kv_recv.at[head, 3],
            "ctx",
            1,
        )

    def pair_across(head):
        return send_to(
            at.pair_send_low,
            at.pair_recv_low.at[head],
            at.kv_send.at[head, 4],
            at.kv_recv.at[head, 4],
            "ctx",
            2,
        )

    def tensor_copy(which, level):
        return send_to(
            at.sum_send.at[level],
            at.sum_recv.at[which, level],
            at.sum_sems.at[0, which, level],
            at.sum_sems.at[1, which, level],
            "tensor",
            tensor_bits[level],
        )

    quarter = at.small.shape[1] // 4

    def small_half(number):
        return send_to(
            at.small.at[:, blocks_of(flip(ctx, (1, 3)[number]), quarter)],
            at.small_recv.at[number],
            at.small_sems.at[0, number],
            at.small_sems.at[1, number],
            "ctx",
            1,
        )

    def small_rest():
        return send_to(
            at.small_held.at[1],
            at.small_recv.at[2],
            at.small_sems.at[0, 2],
            at.small_sems.at[1, 2],
            "ctx",
            2,
        )

    def line_copy(entry):
        axis, bit = line_steps[entry]
        return send_to(
            at.line.at[entry],
            at.line_recv.at[entry],
            at.small_sems.at[0, 3 + entry],
            at.small_sems.at[1, 3 + entry],
            axis,
            bit,
        )

    def small_spread(place):
        return send_to(
            at.line.at[len(line_steps)],
            at.small_full.at[:, blocks_of(ctx, quarter)],
            at.spread_sems.at[0, place - 1],
            at.spread_sems.at[1, place - 1],
            "ctx",
            place,
        )

    def turn(heads_rows, back):
        start_part = heads_rows[:, :LANES]
        ahead = pltpu.roll(start_part, LANES - ROT // 2, 1) * at.sine_ahead[...]
        behind = pltpu.roll(start_part, ROT // 2, 1) * at.sine_behind[...]
        straight = start_part * at.cosine[...]
        moved = straight - ahead - behind if back else straight + ahead + behind
        return jnp.concatenate([moved, heads_rows[:, LANES:]], 1)

    def late_block(block):
        piece = attn_pieces + block // per_piece
        return at.late.at[piece, :, blocks_of(block % per_piece, HS)]

    up_load(0).start()
    up_load_aside(1).start()
    down_load(0).start()
    gate_load(0).start()
    dense_load(0).start()
    barrier = pltpu.get_barrier_semaphore()
    partners = halving[:2] + line_steps + (("ctx", 3),)
    for axis, bits in partners:
        pl.semaphore_signal(
            barrier,
            1,
            device_id={axis: flip(lax.axis_index(axis), bits)},
            device_id_type=MESH,
        )
    pl.semaphore_wait(barrier, len(partners))
    step_rows = 32
    at.small[...] = jnp.zeros_like(at.small)
    ids = at.subset_ids[...]
    weight_line = jnp.zeros(ids.shape, F32)
    for number in range(at.subset_weights.shape[0]):
        weight_line = jnp.where(ids == number, at.subset_weights[number], weight_line)
    at.row_weight[...] = jnp.broadcast_to(weight_line, (LANES, rows)).T

    def grad_of(some):
        return at.cotangent[some].astype(F32) * at.row_weight[some, pl.ds(0, 1)]

    @pl.loop(0, rows // step_rows)
    def _(block):
        some = blocks_of(block, step_rows)
        at.low[some] = grad_of(some).astype(LOW)

    part_starts(0)

    @pl.loop(0, rows // step_rows)
    def _(block):
        some = blocks_of(block, step_rows)
        inputs = at.hidden[some].astype(F32)
        mean = jnp.mean(inputs, -1, keepdims=True)
        centered = inputs - mean
        inv_std = lax.rsqrt(jnp.mean(centered * centered, -1, keepdims=True) + NORM_EPS)
        normed = centered * inv_std
        at.mlp_in[some] = (normed * at.mlp_gain[...] + at.mlp_bias[...]).astype(LOW)
        lane = lax.broadcasted_iota(jnp.int32, (step_rows, LANES), 1)
        at.stats[some] = jnp.where(lane < LANES // 2, mean, inv_std)

    def send_hidden():
        line = at.stats[own_rows].T
        at.stats_line[0, pl.ds(0, 8)] = line[:8]
        at.stats_line[0, pl.ds(8, 8)] = line[LANES // 2 : LANES // 2 + 8]
        for place in (2, 3, 1):
            stats_copy(place).start()
        part_starts(1)
        for block in range(4):
            column = blocks_of(block * 4 + ctx, width)
            at.hidden_part[own_rows, pl.ds(block * width, width)] = at.hidden[:, column]

    def attention_inputs():
        lane = lax.broadcasted_iota(jnp.int32, (rows, LANES), 1)
        place = lax.broadcasted_iota(jnp.int32, (rows, LANES), 0) + ctx * rows
        table = place.astype(F32) * at.freqs[...]
        sine = jnp.sin(table)
        at.cosine[...] = jnp.where(lane < ROT, jnp.cos(table), 1.0)
        at.sine_ahead[...] = jnp.where(lane < ROT // 2, -sine, 0.0)
        at.sine_behind[...] = jnp.where((lane >= ROT // 2) & (lane < ROT), sine, 0.0)

        @pl.loop(0, rows // step_rows)
        def _(block):
            some = blocks_of(block, step_rows)
            stats = at.stats[some]
            centered = at.hidden[some].astype(F32) - stats[:, :1]
            normed = centered * stats[:, LANES // 2 : LANES // 2 + 1]
            at.attn_in[some] = (normed * at.attn_gain[...] + at.attn_bias[...]).astype(LOW)

    def low_left():
        for block in range(4):
            column = blocks_of(block * 4 + ctx, width)
            at.low_part[own_rows, pl.ds(block * width, width)] = at.low[:, column]
        part_waits(0)
        for entry, bits in enumerate(ORDER):
            block = at.low_part[:, blocks_of(flip(dp, bits), width)]
            at.left[0, pl.ds(entry * width, width)] = block.T

    def hidden_left():
        for place in (1, 2, 3):
            stats_copy(place).wait_recv()
        part_waits(1)
        for slot in range(1, 4):
            half = lax.broadcasted_iota(jnp.int32, (LANES, rows), 0) < LANES // 2
            line = jnp.where(half, at.stats_line[slot, :1], at.stats_line[slot, 8:9])
            at.stats[pl.ds(slot * rows, rows)] = line.T
        for entry, bits in enumerate(ORDER):
            place = flip(dp, bits)
            block = at.hidden_part[:, blocks_of(place, width)].astype(F32)
            normed = (block - at.stats[:, :1]) * at.stats[:, LANES // 2 : LANES // 2 + 1]
            column = blocks_of(place * 4 + ctx, width)
            to = pl.ds(entry * width, width)
            sides = ((at.mlp_gain, at.mlp_bias), (at.attn_gain, at.attn_bias))
            for number, (gain, bias) in enumerate(sides):
                at.left[1 + number, to] = (normed * gain[:, column] + bias[:, column]).astype(LOW).T

    def start_piece(piece):
        @pl.when(piece >= RING)
        def _():
            pl.semaphore_wait(at.free.at[0], 1)
            pl.semaphore_wait(at.free.at[1], 1)

        @pl.when(piece >= late)
        def _():
            at.rows_all[piece % RING, own_rows] = at.late[piece - late]

        across(piece).start()
        beside(piece, 0).start()

    def pre_act(pair, weights):
        pre = dot(at.mlp_in[...], weights) + at.up_bias[:, blocks_of(pair, span)]
        return pre, 0.5 * (1.0 + lax.erf(pre * math.sqrt(0.5)))

    def activate(pair):
        if pair in (1, 3):
            up_load_aside(pair).wait()
            pre, cumulative = pre_act(pair, at.qkv_held[:, :span])
        else:
            up_load(pair).wait()
            pre, cumulative = pre_act(pair, at.up_held[...])
        at.rows_all[pair % RING, own_rows] = (pre * cumulative).astype(LOW)
        start_piece(pair)
        if pair == 1:
            up_load_aside(3).start()
        elif pair == 3:
            qkv_load(0).start()
        else:
            following = {0: 2, 2: 4}.get(pair, pair + 1)
            up_load(following if following < pairs else 0).start()
        if pair == max(pairs - 2, 3):
            send_hidden()

    def feed_forward(pair):
        up_load(pair).wait()
        down_load(pair).wait()
        pre, cumulative = pre_act(pair, at.up_held[...])
        given = (pre * cumulative).astype(LOW)
        grad_act = dot_rows(at.low[...], at.down_held[...])
        density = jnp.exp(-0.5 * pre * pre) * (1.0 / math.sqrt(2.0 * math.pi))
        grad_pre = (grad_act * (cumulative + pre * density)).astype(LOW)
        at.rows_all[(pairs + pair) % RING, own_rows] = grad_pre
        at.small[pl.ds(4, 1), blocks_of(pair, span)] = jnp.sum(
            grad_pre.astype(F32), 0, keepdims=True
        )
        start_piece(pairs + pair)

        @pl.when(pair == 0)
        def _():
            for held in (at.branch, at.grad_mlp, at.grad_attn):
                held[...] = jnp.zeros_like(held)

        at.branch[...] += dot(given, at.down_held[...])
        at.grad_mlp[...] += dot_rows(grad_pre, at.up_held[...])

        @pl.when(pair + 1 < pairs)
        def _():
            up_load(pair + 1).start()
            down_load(pair + 1).start()

    def project(head):
        qkv_load(head).wait()
        out = dot(at.attn_in[...], at.qkv_held[...]) + at.qkv_bias[:, blocks_of(head, 3 * HS)]
        at.kv[head, own_rows, pl.ds(0, HS)] = turn(out[:, HS : 2 * HS], False).astype(LOW)
        at.kv[head, own_rows, pl.ds(HS, HS)] = out[:, 2 * HS :].astype(LOW)

        @pl.when(ctx < 2)
        def _():
            kv_across(head).start()

        kv_beside(head, 0).start()
        at.query[head] = turn(out[:, :HS], False).astype(LOW)
        gate_load(head).wait()
        at.gate[head] = dot_rows(at.low[...], at.gate_held[...]).astype(LOW)
        qkv_load((head + 1) % heads).start()

        @pl.when(head + 1 < heads)
        def _():
            gate_load(head + 1).start()

    def kv_forward(head):
        @pl.when(ctx >= 2)
        def _():
            kv_across(head).wait_recv()
            kv_beside(head, 1).start()

        @pl.when(ctx < 2)
        def _():
            for slot in (1, 3):
                at.kv[head, pl.ds(slot * rows, rows)] = jnp.zeros((rows, 2 * HS), LOW)

    def attend(head):
        kv_beside(head, 0).wait_recv()

        @pl.when(ctx >= 2)
        def _():
            kv_beside(head, 1).wait_recv()

        query, gate = at.query[head], at.gate[head]
        keys, values = at.kv[head, :, :HS], at.kv[head, :, HS:]
        shape = (rows, 4 * rows)
        key_place = lax.broadcasted_iota(jnp.int32, shape, 1)
        shift = jnp.full(shape, flip(ctx, ORDER[3]) * rows - 3 * rows, jnp.int32)
        for entry in (2, 1, 0):
            here = flip(ctx, ORDER[entry]) * rows - entry * rows
            shift = jnp.where(key_place < (entry + 1) * rows, here, shift)
        query_place = lax.broadcasted_iota(jnp.int32, shape, 0) + ctx * rows
        scores = jnp.where(
            key_place + shift <= query_place, dot_rows(query, keys) * scale, -1e30
        )
        expd = jnp.exp(scores - jnp.max(scores, -1, keepdims=True))
        prob = expd * (1.0 / jnp.sum(expd, -1, keepdims=True))
        prob_low = prob.astype(LOW)
        attended = dot(prob_low, values).astype(LOW)
        at.late[head // per_piece, :, blocks_of(head % per_piece, HS)] = attended
        grad_prob = dot_rows(gate, values)
        delta = jnp.sum(grad_prob * prob, -1, keepdims=True)
        grad_scores = (prob * (grad_prob - delta)).astype(LOW)
        grad_key = dot(grad_scores.T, query) * scale
        grad_value = dot(prob_low.T, gate)
        at.pair_send[:, pl.ds(0, HS)] = grad_key[2 * rows :].astype(LOW)
        at.pair_send[:, pl.ds(HS, HS)] = grad_value[2 * rows :].astype(LOW)
        pair_beside(head).start()
        at.pair[:, pl.ds(0, HS)] = grad_key[: 2 * rows]
        at.pair[:, pl.ds(HS, HS)] = grad_value[: 2 * rows]
        late_block(3 * head)[...] = turn(dot(grad_scores, keys) * scale, True).astype(LOW)
        dense_load(head).wait()
        at.branch[...] += dot(attended, at.dense_held[...])

        @pl.when(head + 1 < heads)
        def _():
            dense_load(head + 1).start()

    def pair_halve(head):
        pair_beside(head).wait()

        @pl.when(ctx >= 2)
        def _():
            other = pl.ds(rows, rows)
            at.pair_send_low[...] = (
                at.pair[other] + at.pair_recv[head, other].astype(F32)
            ).astype(LOW)
            pair_across(head).start()

        at.pair_own[...] = at.pair[own_rows] + at.pair_recv[head, own_rows].astype(F32)

    def pair_finish(head):
        @pl.when(ctx < 2)
        def _():
            pair_across(head).wait_recv()
            at.pair_own[...] += at.pair_recv_low[head].astype(F32)

        @pl.when(ctx >= 2)
        def _():
            pair_across(head).wait_send()

        total = at.pair_own[...]
        late_block(3 * head + 1)[...] = turn(total[:, :HS], True).astype(LOW)
        late_block(3 * head + 2)[...] = total[:, HS:].astype(LOW)
        for number in range(3):
            at.small[pl.ds(3, 1), blocks_of(3 * head + number, HS)] = jnp.sum(
                late_block(3 * head + number)[...].astype(F32), 0, keepdims=True
            )

    def project_back(head):
        qkv_load(head).wait()
        at.grad_attn[...] += (
            dot_rows(late_block(3 * head)[...], at.qkv_held[:, :HS])
            + dot_rows(late_block(3 * head + 1)[...], at.qkv_held[:, HS : 2 * HS])
            + dot_rows(late_block(3 * head + 2)[...], at.qkv_held[:, 2 * HS :])
        )

        @pl.when(head + 1 < heads)
        def _():
            qkv_load(head + 1).start()

    def branch_send():
        at.sum_send[0] = at.branch[...].astype(LOW)
        tensor_copy(0, 0).start()

    def tensor_step(which, level):
        tensor_copy(which, level).wait()
        if level + 1 < len(tensor_bits):
            at.sum_send[level + 1] = (
                at.sum_send[level].astype(F32) + at.sum_recv[which, level].astype(F32)
            ).astype(LOW)
            tensor_copy(which, level + 1).start()
            return

        @pl.loop(0, rows // step_rows)
        def _(block):
            some = blocks_of(block, step_rows)
            total = at.sum_send[level, some].astype(F32) + at.sum_recv[which, level, some].astype(
                F32
            )
            if which == 0:
                total = (
                    at.hidden[some].astype(F32) + total + at.dense_bias[...] + at.down_bias[...]
                )
                at.mlp_in[some] = total.astype(LOW)
            else:
                at.attn_in[some] = (grad_of(some) + total).astype(LOW)

        row_result(which).start()

    def row_result(which):
        source = (at.mlp_in, at.attn_in)[which]
        target = (at.layer_out, at.input_grad)[which]
        return pltpu.make_async_copy(source, target, at.row_sem.at[which])

    def norm_back():
        @pl.loop(0, rows // step_rows)
        def _(block):
            some = blocks_of(block, step_rows)
            stats = at.stats[some]
            inv_std = stats[:, LANES // 2 : LANES // 2 + 1]
            normed = (at.hidden[some].astype(F32) - stats[:, :1]) * inv_std
            grad_attn, grad_mlp = at.grad_attn[some], at.grad_mlp[some]
            at.small[pl.ds(2, 1), pl.ds(0, model)] += jnp.sum(grad_of(some), 0, keepdims=True)
            for row, grad in enumerate((grad_attn, grad_mlp)):
                at.small[pl.ds(row, 1), pl.ds(0, model)] += jnp.sum(
                    grad * normed, 0, keepdims=True
                )
                at.small[pl.ds(row, 1), pl.ds(model, model)] += jnp.sum(grad, 0, keepdims=True)
            grad = grad_attn * at.attn_gain[...] + grad_mlp * at.mlp_gain[...]
            part = inv_std * (
                grad
                - jnp.mean(grad, -1, keepdims=True)
                - normed * jnp.mean(grad * normed, -1, keepdims=True)
            )
            at.sum_send[0, some] = part.astype(LOW)

        tensor_copy(1, 0).start()
        for number in range(2):
            small_half(number).start()

    def small_step(entry):
        if entry == 0:
            for number in range(2):
                small_half(number).wait()
                mine = blocks_of(flip(ctx, 2 * number), quarter)
                at.small_held[number] = at.small[:, mine] + at.small_recv[number]
            small_rest().start()
            return
        if entry == 1:
            small_rest().wait()
            at.line[0] = at.small_held[0] + at.small_recv[2]
        else:
            line_copy(entry - 2).wait()
            added = at.line[entry - 2] + at.line_recv[entry - 2]
            if line_steps[entry - 2][0] == "tensor":
                row = lax.broadcasted_iota(jnp.int32, added.shape, 0)
                added = jnp.where(row < 2, added, at.line[entry - 2])
            at.line[entry - 1] = added
        if entry - 1 < len(line_steps):
            line_copy(entry - 1).start()
            return
        for place in (2, 3, 1):
            small_spread(place).start()
        at.small_full[:, blocks_of(ctx, quarter)] = at.line[len(line_steps)]

    def small_finish():
        for place in (1, 2, 3):
            small_spread(place).wait()
        at.small_out[...] = at.small_full[...]

    lead = 3
    assert pairs in (4, 8)

    def places(base, *lags):
        return [
            [base + 2 * head + sum(lags[:stage]) for stage in range(5)] for head in range(heads)
        ]

    def in_time(jobs):
        for piece in range(attn_pieces):
            if jobs[(piece + 1) * per_piece - 1][2] > late + piece - lead:
                return False
        for block in range(3 * heads):
            if jobs[block // 3][4] > late + attn_pieces + block // per_piece - lead:
                return False
        return True

    jobs = next(pace for pace in (places(1, 5, 2, 2, 2), places(2, 1, 1, 1, 1)) if in_time(pace))
    project_at, forward_at, attend_at, halve_at, finish_at = jobs[0]
    feed_at = max(pairs - 4, 1)
    feed_end = feed_at + pairs - 1
    branch_at = max(attend_at + 2 * (heads - 1), feed_end) + 1
    back_at = max(finish_at + 2 * (heads - 1) + 2, branch_at + 4 * len(tensor_bits) + 1)
    total_steps = max(
        count + 5, back_at + 5 + len(line_steps), back_at + 4 * len(tensor_bits) + 1
    )

    def step(turn_number, carry):
        now = turn_number - 2

        def job(start, stride, times, act):
            index = now - start

            @pl.when((index >= 0) & (index < stride * times) & (index % stride == 0))
            def _():
                act(index // stride)

        multiply = now - 1

        @pl.when((multiply >= 0) & (multiply < count))
        def _():
            beside(multiply, 0).wait_recv()
            beside(multiply, 1).wait_recv()

            @pl.when(multiply >= RING)
            def _():
                pl.semaphore_wait(at.free.at[2], 1)

            @pl.when(multiply >= 3)
            def _():
                first(multiply - 3).wait_send()

            feed = multiply < late
            group = jnp.where(
                feed,
                jnp.where(multiply < pairs, 0, 1),
                jnp.where(multiply < late + attn_pieces, 0, 2),
            )
            at.first_send[multiply % 3] = dot(
                at.left[group, pl.ds(2 * width, 2 * width)], at.rows_all[multiply % RING]
            ).astype(LOW)
            first(multiply).start()
            at.held[multiply % 5] = dot(
                at.left[group, pl.ds(0, 2 * width)], at.rows_all[multiply % RING]
            )

        add = now - 3

        @pl.when((add >= 0) & (add < count))
        def _():
            first(add).wait_recv()

            @pl.when(add >= RING)
            def _():
                pl.semaphore_wait(at.free.at[3], 1)

            @pl.when(add >= 3)
            def _():
                second(add - 3).wait_send()

            lower = pl.ds(width, width)
            at.second_send[add % 3] = (
                at.held[add % 5, lower] + at.first_recv[add % RING, lower].astype(F32)
            ).astype(LOW)
            second(add).start()

        last = now - 5

        @pl.when((last >= 0) & (last < count))
        def _():
            second(last).wait_recv()

            @pl.when(last >= 2)
            def _():
                for_result(last - 2, lambda copy: copy.wait())

            upper = pl.ds(0, width)
            total = (
                at.held[last % 5, upper]
                + at.first_recv[last % RING, upper].astype(F32)
                + at.second_recv[last % RING].astype(F32)
            )
            flat = ((last < late) & (last >= pairs)) | (last >= late + attn_pieces)

            @pl.when(flat)
            def _():
                at.plain[last % 2] = total

            @pl.when(jnp.logical_not(flat))
            def _():
                at.turned[last % 2] = total.T

            for_result(last, lambda copy: copy.start())

            @pl.when(last < count - RING)
            def _():
                for number, bit in ((2, 1), (3, 2)):
                    pl.semaphore_signal(
                        at.free.at[number],
                        1,
                        device_id={"dp": flip(dp, bit)},
                        device_id_type=MESH,
                    )

        @pl.when((now >= 0) & (now < count))
        def _():
            across(now).wait_recv()
            beside(now, 1).start()

        sent = now - 1

        @pl.when((sent >= 0) & (sent < count))
        def _():
            across(sent).wait_send()
            beside(sent, 0).wait_send()
            beside(sent, 1).wait_send()

            @pl.when(sent < count - RING)
            def _():
                for number, bit in ((0, 2), (1, 1)):
                    pl.semaphore_signal(
                        at.free.at[number],
                        1,
                        device_id={"ctx": flip(ctx, bit)},
                        device_id_type=MESH,
                    )

        for pair, place in enumerate((-2, -2, -1, 0, 1, 2, 3, 3)[:pairs]):
            job(place, 1, 1, lambda _: activate(pair))
            if pair == 0:
                job(-2, 1, 1, lambda _: pass_on(0))
            if pair == 3:
                job(0, 1, 1, lambda _: low_left())
                job(min(0, project_at - 1), 1, 1, lambda _: attention_inputs())
        job(pairs - 2, 1, 1, lambda _: pass_on(1))
        job(pairs - 1, 1, 1, lambda _: hidden_left())
        job(feed_at, 1, pairs, feed_forward)
        job(project_at, 2, heads, project)
        job(forward_at, 2, heads, kv_forward)
        job(finish_at, 2, heads, pair_finish)
        job(halve_at, 2, heads, pair_halve)
        job(attend_at, 2, heads, attend)
        job(finish_at + 1, 2, heads, project_back)
        job(branch_at, 1, 1, lambda _: branch_send())
        for level in range(len(tensor_bits)):
            job(branch_at + 4 * (level + 1), 1, 1, lambda _: tensor_step(0, level))
        job(back_at, 1, 1, lambda _: norm_back())
        for level in range(len(tensor_bits)):
            job(back_at + 4 * (level + 1), 1, 1, lambda _: tensor_step(1, level))
        for entry in range(len(line_steps) + 2):
            job(back_at + 1 + entry, 1, 1, lambda _: small_step(entry))
        job(back_at + 3 + len(line_steps), 1, 1, lambda _: small_finish())

        @pl.when((now + lead >= late) & (now + lead < count))
        def _():
            start_piece(now + lead)

        return carry

    lax.fori_loop(0, total_steps + 2, step, 0)

    for place in (1, 2, 3):
        stats_copy(place).wait_send()
        for kind in range(2):
            for number in part_numbers(place):
                part_copy(kind, place, number).wait_send()
            if shared and place > 1:
                part_pass(kind, place).wait_send()

    @pl.loop(0, heads)
    def _(head):
        kv_beside(head, 0).wait_send()

        @pl.when(ctx < 2)
        def _():
            kv_across(head).wait_send()

        @pl.when(ctx >= 2)
        def _():
            kv_beside(head, 1).wait_send()

    @pl.loop(count - 3, count)
    def _(piece):
        first(piece).wait_send()
        second(piece).wait_send()

        @pl.when(piece >= count - 2)
        def _():
            for_result(piece, lambda copy: copy.wait())

    row_result(0).wait()
    row_result(1).wait()


def hand_on(cuts, *refs):
    whole = 6
    sources, small = refs[:whole], refs[whole]
    targets, refs = refs[whole + 1 : 2 * whole + 1], refs[2 * whole + 1 :]
    pieces, refs = refs[: len(cuts)], refs[len(cuts) :]
    held, sem = refs[:whole], refs[whole]

    def halves(ref):
        size = ref.shape[0] // 2
        return [ref.at[pl.ds(half * size, size)] for half in range(2)]

    copies = []
    for number in range(whole):
        parts = zip(halves(sources[number]), halves(held[number]), halves(targets[number]))
        for half, (source, middle, target) in enumerate(parts):
            copies.append(
                (
                    pltpu.make_async_copy(source, middle, sem.at[0, number, half]),
                    pltpu.make_async_copy(middle, target, sem.at[1, number, half]),
                )
            )
    for fetch, _ in copies:
        fetch.start()
    for piece, (row, low, high) in zip(pieces, cuts):
        piece[...] = small[row : row + 1, low:high]
    for fetch, put in copies:
        fetch.wait()
        put.start()
    for _, put in copies:
        put.wait()


def local(
    hidden_in,
    attn_norm_gain,
    attn_norm_bias,
    qkv_weight,
    qkv_bias,
    dense_weight,
    dense_bias,
    mlp_norm_gain,
    mlp_norm_bias,
    up_weight,
    up_bias,
    down_weight,
    down_bias,
    out_cotangent,
    subset_ids,
    subset_weights,
):
    seq_count, rows, model = hidden_in.shape
    heads = qkv_weight.shape[1] // (3 * HS)
    units = up_weight.shape[1]
    width = model // (lax.axis_size("dp") * lax.axis_size("ctx"))
    span = min(512, math.gcd(units, heads * HS, heads * 3 * HS))
    pairs = units // span
    late_count = heads * 4 * HS // span
    plan = types.SimpleNamespace(
        rows=rows, span=span, width=width, pairs=pairs, heads=heads, count=2 * pairs + late_count
    )
    tokens = rows * lax.axis_size("ctx")

    turns = np.arange(LANES) % (ROT // 2)
    freqs = np.float32(10000.0) ** -(turns.astype(np.float32) * np.float32(2.0 / ROT))

    bits = lax.axis_size("tensor").bit_length() - 1
    steps = 2 + bits
    small_width = max(2 * model, units, heads * 3 * HS)
    dma = pltpu.SemaphoreType.DMA
    vmem = pl.BlockSpec(memory_space=pltpu.VMEM)
    hbm = pl.BlockSpec(memory_space=pl.ANY)
    inputs = {
        "hidden": (hidden_in.reshape(rows, model), vmem),
        "cotangent": (out_cotangent.reshape(rows, model), vmem),
        "subset_ids": (subset_ids, vmem),
        "subset_weights": (subset_weights, pl.BlockSpec(memory_space=pltpu.SMEM)),
        "freqs": (jnp.asarray(freqs[None], F32), vmem),
        "attn_gain": (attn_norm_gain[None], vmem),
        "attn_bias": (attn_norm_bias[None], vmem),
        "mlp_gain": (mlp_norm_gain[None], vmem),
        "mlp_bias": (mlp_norm_bias[None], vmem),
        "dense_bias": (dense_bias[None], vmem),
        "down_bias": (down_bias[None], vmem),
        "qkv_bias": (qkv_bias[None], vmem),
        "up_bias": (up_bias[None], vmem),
        "qkv_weight": (qkv_weight, hbm),
        "dense_weight": (dense_weight, hbm),
        "up_weight": (up_weight, hbm),
        "down_weight": (down_weight, hbm),
    }
    outputs = {
        "layer_out": ((rows, model), LOW, hbm),
        "input_grad": ((rows, model), LOW, hbm),
        "small_out": ((8, small_width), F32, vmem),
        "down_out": ((units, width), F32, hbm),
        "up_out": ((width, units), F32, hbm),
        "dense_out": ((heads * HS, width), F32, hbm),
        "qkv_out": ((width, heads * 3 * HS), F32, hbm),
    }
    scratch = {
        "rows_all": pltpu.VMEM((RING, tokens, span), LOW),
        "first_send": pltpu.VMEM((3, 2 * width, span), LOW),
        "first_recv": pltpu.VMEM((RING, 2 * width, span), LOW),
        "second_send": pltpu.VMEM((3, width, span), LOW),
        "second_recv": pltpu.VMEM((RING, width, span), LOW),
        "held": pltpu.VMEM((5, 2 * width, span), F32),
        "plain": pltpu.VMEM((2, width, span), F32),
        "turned": pltpu.VMEM((2, span, width), F32),
        "left": pltpu.VMEM((3, 4 * width, tokens), LOW),
        "low_part": pltpu.VMEM((tokens, 4 * width), LOW),
        "hidden_part": pltpu.VMEM((tokens, 4 * width), LOW),
        "stats": pltpu.VMEM((tokens, LANES), F32),
        "stats_line": pltpu.VMEM((4, 16, rows), F32),
        "row_weight": pltpu.VMEM((rows, LANES), F32),
        "cosine": pltpu.VMEM((rows, LANES), F32),
        "sine_ahead": pltpu.VMEM((rows, LANES), F32),
        "sine_behind": pltpu.VMEM((rows, LANES), F32),
        "attn_in": pltpu.VMEM((rows, model), LOW),
        "mlp_in": pltpu.VMEM((rows, model), LOW),
        "low": pltpu.VMEM((rows, model), LOW),
        "up_held": pltpu.VMEM((model, span), LOW),
        "down_held": pltpu.VMEM((span, model), LOW),
        "qkv_held": pltpu.VMEM((model, 3 * HS), LOW),
        "gate_held": pltpu.VMEM((HS, model), LOW),
        "dense_held": pltpu.VMEM((HS, model), LOW),
        "query": pltpu.VMEM((heads, rows, HS), LOW),
        "gate": pltpu.VMEM((heads, rows, HS), LOW),
        "kv": pltpu.VMEM((heads, tokens, 2 * HS), LOW),
        "pair": pltpu.VMEM((2 * rows, 2 * HS), F32),
        "pair_own": pltpu.VMEM((rows, 2 * HS), F32),
        "pair_send": pltpu.VMEM((2 * rows, 2 * HS), LOW),
        "pair_recv": pltpu.VMEM((heads, 2 * rows, 2 * HS), LOW),
        "pair_send_low": pltpu.VMEM((rows, 2 * HS), LOW),
        "pair_recv_low": pltpu.VMEM((heads, rows, 2 * HS), LOW),
        "late": pltpu.VMEM((late_count, rows, span), LOW),
        "branch": pltpu.VMEM((rows, model), F32),
        "grad_mlp": pltpu.VMEM((rows, model), F32),
        "grad_attn": pltpu.VMEM((rows, model), F32),
        "sum_send": pltpu.VMEM((bits, rows, model), LOW),
        "sum_recv": pltpu.VMEM((2, bits, rows, model), LOW),
        "small": pltpu.VMEM((8, small_width), F32),
        "small_full": pltpu.VMEM((8, small_width), F32),
        "small_held": pltpu.VMEM((2, 8, small_width // 4), F32),
        "small_recv": pltpu.VMEM((3, 8, small_width // 4), F32),
        "line": pltpu.VMEM((steps + 1, 8, small_width // 4), F32),
        "line_recv": pltpu.VMEM((steps, 8, small_width // 4), F32),
        "load_sem": dma((5,)),
        "part_send": dma((2, 3, 4)),
        "part_recv": dma((2, 3, 4)),
        "pass_sems": dma((2, 2, 2)),
        "stats_send": dma((3,)),
        "stats_recv": dma((3,)),
        "ctx_send": dma((RING, 3)),
        "ctx_recv": dma((RING, 3)),
        "dp_send": dma((RING, 2)),
        "dp_recv": dma((RING, 2)),
        "out_sem": dma((2,)),
        "row_sem": dma((2,)),
        "kv_send": dma((heads, 5)),
        "kv_recv": dma((heads, 5)),
        "sum_sems": dma((2, 2, bits)),
        "small_sems": dma((2, 3 + steps)),
        "spread_sems": dma((2, 3)),
        "free": pltpu.SemaphoreType.REGULAR((4,)),
    }
    names = [*inputs, *outputs, *scratch]
    results = pl.pallas_call(
        functools.partial(layer_kernel, plan, names),
        out_shape=[jax.ShapeDtypeStruct(shape, kind) for shape, kind, _ in outputs.values()],
        in_specs=[spec for _, spec in inputs.values()],
        out_specs=[spec for _, _, spec in outputs.values()],
        scratch_shapes=list(scratch.values()),
        compiler_params=pltpu.CompilerParams(
            collective_id=0, has_side_effects=True, vmem_limit_bytes=63 << 20
        ),
        name="layer",
    )(*[array for array, _ in inputs.values()])
    cuts = [
        (0, 0, model),
        (0, model, 2 * model),
        (1, 0, model),
        (1, model, 2 * model),
        (2, 0, model),
        (2, 0, model),
        (3, 0, heads * 3 * HS),
        (4, 0, units),
    ]
    layer_out, input_grad, small, down_grad, up_grad, dense_grad, qkv_grad = results
    large = [layer_out, input_grad, down_grad, up_grad, dense_grad, qkv_grad]
    shapes = [jax.ShapeDtypeStruct(array.shape, array.dtype) for array in large]
    shapes += [jax.ShapeDtypeStruct((1, high - low), F32) for _, low, high in cuts]
    done = pl.pallas_call(
        functools.partial(hand_on, cuts),
        out_shape=shapes,
        in_specs=[hbm] * len(large) + [vmem],
        out_specs=[hbm] * len(large) + [vmem] * len(cuts),
        scratch_shapes=[pltpu.VMEM(array.shape, array.dtype) for array in large]
        + [dma((2, len(large), 2))],
        compiler_params=pltpu.CompilerParams(vmem_limit_bytes=60 << 20),
        name="hand_on",
    )(*large, small)
    layer_out, input_grad, down_grad, up_grad, dense_grad, qkv_grad = done[:6]
    vectors = [vector.reshape(-1) for vector in done[6:]]
    attn_gain, attn_bias, mlp_gain, mlp_bias, dense_sum, down_sum, qkv_sum, up_sum = vectors
    shape = (seq_count, rows, model)
    return (
        layer_out.reshape(shape),
        input_grad.reshape(shape),
        attn_gain,
        attn_bias,
        qkv_grad,
        qkv_sum,
        dense_grad,
        dense_sum,
        mlp_gain,
        mlp_bias,
        up_grad,
        up_sum,
        down_grad,
        down_sum,
    )


def solution(mesh):
    return jax.shard_map(
        local,
        mesh=mesh,
        in_specs=(
            P("dp", "ctx", None),
            P(),
            P(),
            P(None, "tensor"),
            P("tensor"),
            P("tensor", None),
            P(),
            P(),
            P(),
            P(None, "tensor"),
            P("tensor"),
            P("tensor", None),
            P(),
            P("dp", "ctx", None),
            P("dp", "ctx"),
            P(),
        ),
        out_specs=(
            P("dp", "ctx", None),
            P("dp", "ctx", None),
            P(),
            P(),
            P(("dp", "ctx"), "tensor"),
            P("tensor"),
            P("tensor", ("dp", "ctx")),
            P(),
            P(),
            P(),
            P(("dp", "ctx"), "tensor"),
            P("tensor"),
            P("tensor", ("dp", "ctx")),
            P(),
        ),
        check_vma=False,
    )
```

```python
import functools
import math
import types

import jax
import jax.numpy as jnp
import numpy as np
from jax import lax
from jax.experimental import pallas as pl
from jax.experimental.pallas import tpu as pltpu
from jax.sharding import PartitionSpec as P

HS = 256
ROT = 64
LANES = 128
RING = 8
NORM_EPS = 1e-05
MESH = pl.DeviceIdType.MESH
ORDER = (0, 2, 1, 3)
LOW = jnp.bfloat16
F32 = jnp.float32


def flip(place, bits):
    bit = 1
    while bit <= bits:
        if bits & bit:
            place = place + bit - 2 * bit * ((place // bit) % 2)
        bit *= 2
    return place


def send_to(source, target, send_sem, recv_sem, axis, bits):
    return pltpu.make_async_remote_copy(
        src_ref=source,
        dst_ref=target,
        send_sem=send_sem,
        recv_sem=recv_sem,
        device_id={axis: flip(lax.axis_index(axis), bits)},
        device_id_type=MESH,
    )


def dot(left, right):
    return jnp.dot(left, right, preferred_element_type=F32)


def dot_rows(left, right):
    return lax.dot_general(left, right, (((1,), (1,)), ((), ())), preferred_element_type=F32)


def axis_bits(axis):
    return [1 << level for level in range(lax.axis_size(axis).bit_length() - 1)]


def blocks_of(total, size):
    return pl.ds(pl.multiple_of(total * size, size), size)


def layer_kernel(plan, names, *refs):
    at = types.SimpleNamespace(**dict(zip(names, refs)))
    rows, span, count, width = plan.rows, plan.span, plan.count, plan.width
    pairs, heads, late = plan.pairs, plan.heads, 2 * plan.pairs
    attn_pieces = heads * HS // span
    per_piece = span // HS
    model = at.hidden.shape[1]
    ctx, dp = lax.axis_index("ctx"), lax.axis_index("dp")
    own_rows = pl.ds(0, rows)
    tensor_bits = axis_bits("tensor")
    halving = (("ctx", 1), ("ctx", 2), ("dp", 1), ("dp", 2))
    line_steps = halving[2:] + tuple(("tensor", bit) for bit in tensor_bits)
    scale = 1.0 / math.sqrt(HS)

    def up_load(piece):
        return pltpu.make_async_copy(
            at.up_weight.at[:, blocks_of(piece, span)], at.up_held, at.load_sem.at[0]
        )

    def up_load_aside(piece):
        return pltpu.make_async_copy(
            at.up_weight.at[:, blocks_of(piece, span)],
            at.qkv_held.at[:, pl.ds(0, span)],
            at.load_sem.at[2],
        )

    def down_load(piece):
        return pltpu.make_async_copy(
            at.down_weight.at[blocks_of(piece, span)], at.down_held, at.load_sem.at[1]
        )

    def qkv_load(head):
        return pltpu.make_async_copy(
            at.qkv_weight.at[:, blocks_of(head, 3 * HS)], at.qkv_held, at.load_sem.at[2]
        )

    def gate_load(head):
        return pltpu.make_async_copy(
            at.dense_weight.at[blocks_of(head, HS)], at.gate_held, at.load_sem.at[3]
        )

    def dense_load(head):
        return pltpu.make_async_copy(
            at.dense_weight.at[blocks_of(head, HS)], at.dense_held, at.load_sem.at[4]
        )

    shared = lax.axis_size("tensor") == 2
    side = lax.axis_index("tensor")

    def part_numbers(place):
        return range(2 if shared and place > 1 else 4)

    def part_copy(kind, place, number):
        source = (at.low, at.hidden)[kind]
        target = (at.low_part, at.hidden_part)[kind]
        block = 2 * side + number if shared and place > 1 else number
        column = block * 4 + flip(ctx, place)
        return send_to(
            source.at[:, blocks_of(column, width)],
            target.at[pl.ds(ORDER.index(place) * rows, rows), blocks_of(block, width)],
            at.part_send.at[kind, place - 1, number],
            at.part_recv.at[kind, place - 1, number],
            "ctx",
            place,
        )

    def part_pass(kind, place):
        target = (at.low_part, at.hidden_part)[kind]
        half = target.at[pl.ds(ORDER.index(place) * rows, rows), blocks_of(side, 2 * width)]
        return send_to(
            half,
            half,
            at.pass_sems.at[0, kind, place - 2],
            at.pass_sems.at[1, kind, place - 2],
            "tensor",
            1,
        )

    def part_starts(kind):
        for place in (2, 3, 1):
            for number in part_numbers(place):
                part_copy(kind, place, number).start()

    def pass_on(kind):
        for place in (2, 3):
            for number in part_numbers(place):
                part_copy(kind, place, number).wait_recv()
            if shared:
                part_pass(kind, place).start()

    def part_waits(kind):
        for number in part_numbers(1):
            part_copy(kind, 1, number).wait_recv()
        if shared:
            for place in (2, 3):
                part_pass(kind, place).wait_recv()

    def stats_copy(place):
        return send_to(
            at.stats_line.at[0],
            at.stats_line.at[ORDER.index(place)],
            at.stats_send.at[place - 1],
            at.stats_recv.at[place - 1],
            "ctx",
            place,
        )

    def across(piece):
        slot = piece % RING
        return send_to(
            at.rows_all.at[slot, own_rows],
            at.rows_all.at[slot, pl.ds(rows, rows)],
            at.ctx_send.at[slot, 0],
            at.ctx_recv.at[slot, 0],
            "ctx",
            2,
        )

    def beside(piece, part):
        slot = piece % RING
        return send_to(
            at.rows_all.at[slot, pl.ds(part * rows, rows)],
            at.rows_all.at[slot, pl.ds((2 + part) * rows, rows)],
            at.ctx_send.at[slot, 1 + part],
            at.ctx_recv.at[slot, 1 + part],
            "ctx",
            1,
        )

    def first(piece):
        return send_to(
            at.first_send.at[piece % 3],
            at.first_recv.at[piece % RING],
            at.dp_send.at[piece % RING, 0],
            at.dp_recv.at[piece % RING, 0],
            "dp",
            1,
        )

    def second(piece):
        return send_to(
            at.second_send.at[piece % 3],
            at.second_recv.at[piece % RING],
            at.dp_send.at[piece % RING, 1],
            at.dp_recv.at[piece % RING, 1],
            "dp",
            2,
        )

    def results(piece):
        slot = piece % 2
        turned, plain = at.turned.at[slot], at.plain.at[slot]
        feed = piece < late
        gives = piece < pairs
        dense = (piece >= late) & (piece < late + attn_pieces)
        return (
            (gives, turned, at.down_out.at[blocks_of(piece, span)]),
            (
                feed & jnp.logical_not(gives),
                plain,
                at.up_out.at[:, blocks_of(piece - pairs, span)],
            ),
            (dense, turned, at.dense_out.at[blocks_of(piece - late, span)]),
            (
                piece >= late + attn_pieces,
                plain,
                at.qkv_out.at[:, blocks_of(piece - late - attn_pieces, span)],
            ),
        )

    def for_result(piece, act):
        for holds, source, target in results(piece):

            @pl.when(holds)
            def _():
                act(pltpu.make_async_copy(source, target, at.out_sem.at[piece % 2]))

    def kv_across(head):
        return send_to(
            at.kv.at[head, own_rows],
            at.kv.at[head, pl.ds(rows, rows)],
            at.kv_send.at[head, 0],
            at.kv_recv.at[head, 0],
            "ctx",
            2,
        )

    def kv_beside(head, part):
        return send_to(
            at.kv.at[head, pl.ds(part * rows, rows)],
            at.kv.at[head, pl.ds((2 + part) * rows, rows)],
            at.kv_send.at[head, 1 + part],
            at.kv_recv.at[head, 1 + part],
            "ctx",
            1,
        )

    def pair_beside(head):
        return send_to(
            at.pair_send,
            at.pair_recv.at[head],
            at.kv_send.at[head, 3],
            at.kv_recv.at[head, 3],
            "ctx",
            1,
        )

    def pair_across(head):
        return send_to(
            at.pair_send_low,
            at.pair_recv_low.at[head],
            at.kv_send.at[head, 4],
            at.kv_recv.at[head, 4],
            "ctx",
            2,
        )

    def tensor_copy(which, level):
        return send_to(
            at.sum_send.at[level],
            at.sum_recv.at[which, level],
            at.sum_sems.at[0, which, level],
            at.sum_sems.at[1, which, level],
            "tensor",
            tensor_bits[level],
        )

    quarter = at.small.shape[1] // 4

    def small_half(number):
        return send_to(
            at.small.at[:, blocks_of(flip(ctx, (1, 3)[number]), quarter)],
            at.small_recv.at[number],
            at.small_sems.at[0, number],
            at.small_sems.at[1, number],
            "ctx",
            1,
        )

    def small_rest():
        return send_to(
            at.small_held.at[1],
            at.small_recv.at[2],
            at.small_sems.at[0, 2],
            at.small_sems.at[1, 2],
            "ctx",
            2,
        )

    def line_copy(entry):
        axis, bit = line_steps[entry]
        return send_to(
            at.line.at[entry],
            at.line_recv.at[entry],
            at.small_sems.at[0, 3 + entry],
            at.small_sems.at[1, 3 + entry],
            axis,
            bit,
        )

    def small_spread(place):
        return send_to(
            at.line.at[len(line_steps)],
            at.small_full.at[:, blocks_of(ctx, quarter)],
            at.spread_sems.at[0, place - 1],
            at.spread_sems.at[1, place - 1],
            "ctx",
            place,
        )

    def turn(heads_rows, back):
        start_part = heads_rows[:, :LANES]
        ahead = pltpu.roll(start_part, LANES - ROT // 2, 1) * at.sine_ahead[...]
        behind = pltpu.roll(start_part, ROT // 2, 1) * at.sine_behind[...]
        straight = start_part * at.cosine[...]
        moved = straight - ahead - behind if back else straight + ahead + behind
        return jnp.concatenate([moved, heads_rows[:, LANES:]], 1)

    def late_block(block):
        piece = attn_pieces + block // per_piece
        return at.late.at[piece, :, blocks_of(block % per_piece, HS)]

    up_load(0).start()
    up_load_aside(1).start()
    down_load(0).start()
    gate_load(0).start()
    dense_load(0).start()
    barrier = pltpu.get_barrier_semaphore()
    partners = halving[:2] + line_steps + (("ctx", 3),)
    for axis, bits in partners:
        pl.semaphore_signal(
            barrier,
            1,
            device_id={axis: flip(lax.axis_index(axis), bits)},
            device_id_type=MESH,
        )
    pl.semaphore_wait(barrier, len(partners))
    step_rows = 32
    at.small[...] = jnp.zeros_like(at.small)
    ids = at.subset_ids[...]
    weight_line = jnp.zeros(ids.shape, F32)
    for number in range(at.subset_weights.shape[0]):
        weight_line = jnp.where(ids == number, at.subset_weights[number], weight_line)
    at.row_weight[...] = jnp.broadcast_to(weight_line, (LANES, rows)).T

    def grad_of(some):
        return at.cotangent[some].astype(F32) * at.row_weight[some, pl.ds(0, 1)]

    @pl.loop(0, rows // step_rows)
    def _(block):
        some = blocks_of(block, step_rows)
        at.low[some] = grad_of(some).astype(LOW)

    part_starts(0)

    @pl.loop(0, rows // step_rows)
    def _(block):
        some = blocks_of(block, step_rows)
        inputs = at.hidden[some].astype(F32)
        mean = jnp.mean(inputs, -1, keepdims=True)
        centered = inputs - mean
        inv_std = lax.rsqrt(jnp.mean(centered * centered, -1, keepdims=True) + NORM_EPS)
        normed = centered * inv_std
        at.mlp_in[some] = (normed * at.mlp_gain[...] + at.mlp_bias[...]).astype(LOW)
        lane = lax.broadcasted_iota(jnp.int32, (step_rows, LANES), 1)
        at.stats[some] = jnp.where(lane < LANES // 2, mean, inv_std)

    def send_hidden():
        line = at.stats[own_rows].T
        at.stats_line[0, pl.ds(0, 8)] = line[:8]
        at.stats_line[0, pl.ds(8, 8)] = line[LANES // 2 : LANES // 2 + 8]
        for place in (2, 3, 1):
            stats_copy(place).start()
        part_starts(1)
        for block in range(4):
            column = blocks_of(block * 4 + ctx, width)
            at.hidden_part[own_rows, pl.ds(block * width, width)] = at.hidden[:, column]

    def attention_inputs():
        lane = lax.broadcasted_iota(jnp.int32, (rows, LANES), 1)
        place = lax.broadcasted_iota(jnp.int32, (rows, LANES), 0) + ctx * rows
        table = place.astype(F32) * at.freqs[...]
        sine = jnp.sin(table)
        at.cosine[...] = jnp.where(lane < ROT, jnp.cos(table), 1.0)
        at.sine_ahead[...] = jnp.where(lane < ROT // 2, -sine, 0.0)
        at.sine_behind[...] = jnp.where((lane >= ROT // 2) & (lane < ROT), sine, 0.0)

        @pl.loop(0, rows // step_rows)
        def _(block):
            some = blocks_of(block, step_rows)
            stats = at.stats[some]
            centered = at.hidden[some].astype(F32) - stats[:, :1]
            normed = centered * stats[:, LANES // 2 : LANES // 2 + 1]
            at.attn_in[some] = (normed * at.attn_gain[...] + at.attn_bias[...]).astype(LOW)

    def low_left():
        for block in range(4):
            column = blocks_of(block * 4 + ctx, width)
            at.low_part[own_rows, pl.ds(block * width, width)] = at.low[:, column]
        part_waits(0)
        for entry, bits in enumerate(ORDER):
            block = at.low_part[:, blocks_of(flip(dp, bits), width)]
            at.left[0, pl.ds(entry * width, width)] = block.T

    def hidden_left():
        for place in (1, 2, 3):
            stats_copy(place).wait_recv()
        part_waits(1)
        for slot in range(1, 4):
            half = lax.broadcasted_iota(jnp.int32, (LANES, rows), 0) < LANES // 2
            line = jnp.where(half, at.stats_line[slot, :1], at.stats_line[slot, 8:9])
            at.stats[pl.ds(slot * rows, rows)] = line.T
        for entry, bits in enumerate(ORDER):
            place = flip(dp, bits)
            block = at.hidden_part[:, blocks_of(place, width)].astype(F32)
            normed = (block - at.stats[:, :1]) * at.stats[:, LANES // 2 : LANES // 2 + 1]
            column = blocks_of(place * 4 + ctx, width)
            to = pl.ds(entry * width, width)
            sides = ((at.mlp_gain, at.mlp_bias), (at.attn_gain, at.attn_bias))
            for number, (gain, bias) in enumerate(sides):
                at.left[1 + number, to] = (normed * gain[:, column] + bias[:, column]).astype(LOW).T

    def start_piece(piece):
        @pl.when(piece >= RING)
        def _():
            pl.semaphore_wait(at.free.at[0], 1)
            pl.semaphore_wait(at.free.at[1], 1)

        @pl.when(piece >= late)
        def _():
            at.rows_all[piece % RING, own_rows] = at.late[piece - late]

        across(piece).start()
        beside(piece, 0).start()

    def pre_act(pair, weights):
        pre = dot(at.mlp_in[...], weights) + at.up_bias[:, blocks_of(pair, span)]
        return pre, 0.5 * (1.0 + lax.erf(pre * math.sqrt(0.5)))

    def activate(pair):
        if pair in (1, 3):
            up_load_aside(pair).wait()
            pre, cumulative = pre_act(pair, at.qkv_held[:, :span])
        else:
            up_load(pair).wait()
            pre, cumulative = pre_act(pair, at.up_held[...])
        at.rows_all[pair % RING, own_rows] = (pre * cumulative).astype(LOW)
        start_piece(pair)
        if pair == 1:
            up_load_aside(3).start()
        elif pair == 3:
            qkv_load(0).start()
        else:
            following = {0: 2, 2: 4}.get(pair, pair + 1)
            up_load(following if following < pairs else 0).start()
        if pair == max(pairs - 2, 3):
            send_hidden()

    def feed_forward(pair):
        up_load(pair).wait()
        down_load(pair).wait()
        pre, cumulative = pre_act(pair, at.up_held[...])
        given = (pre * cumulative).astype(LOW)
        grad_act = dot_rows(at.low[...], at.down_held[...])
        density = jnp.exp(-0.5 * pre * pre) * (1.0 / math.sqrt(2.0 * math.pi))
        grad_pre = (grad_act * (cumulative + pre * density)).astype(LOW)
        at.rows_all[(pairs + pair) % RING, own_rows] = grad_pre
        at.small[pl.ds(4, 1), blocks_of(pair, span)] = jnp.sum(
            grad_pre.astype(F32), 0, keepdims=True
        )
        start_piece(pairs + pair)

        @pl.when(pair == 0)
        def _():
            for held in (at.branch, at.grad_mlp, at.grad_attn):
                held[...] = jnp.zeros_like(held)

        at.branch[...] += dot(given, at.down_held[...])
        at.grad_mlp[...] += dot_rows(grad_pre, at.up_held[...])

        @pl.when(pair + 1 < pairs)
        def _():
            up_load(pair + 1).start()
            down_load(pair + 1).start()

    def project(head):
        qkv_load(head).wait()
        out = dot(at.attn_in[...], at.qkv_held[...]) + at.qkv_bias[:, blocks_of(head, 3 * HS)]
        at.kv[head, own_rows, pl.ds(0, HS)] = turn(out[:, HS : 2 * HS], False).astype(LOW)
        at.kv[head, own_rows, pl.ds(HS, HS)] = out[:, 2 * HS :].astype(LOW)

        @pl.when(ctx < 2)
        def _():
            kv_across(head).start()

        kv_beside(head, 0).start()
        at.query[head] = turn(out[:, :HS], False).astype(LOW)
        gate_load(head).wait()
        at.gate[head] = dot_rows(at.low[...], at.gate_held[...]).astype(LOW)
        qkv_load((head + 1) % heads).start()

        @pl.when(head + 1 < heads)
        def _():
            gate_load(head + 1).start()

    def kv_forward(head):
        @pl.when(ctx >= 2)
        def _():
            kv_across(head).wait_recv()
            kv_beside(head, 1).start()

        @pl.when(ctx < 2)
        def _():
            for slot in (1, 3):
                at.kv[head, pl.ds(slot * rows, rows)] = jnp.zeros((rows, 2 * HS), LOW)

    def attend(head):
        kv_beside(head, 0).wait_recv()

        @pl.when(ctx >= 2)
        def _():
            kv_beside(head, 1).wait_recv()

        query, gate = at.query[head], at.gate[head]
        keys, values = at.kv[head, :, :HS], at.kv[head, :, HS:]
        shape = (rows, 4 * rows)
        key_place = lax.broadcasted_iota(jnp.int32, shape, 1)
        shift = jnp.full(shape, flip(ctx, ORDER[3]) * rows - 3 * rows, jnp.int32)
        for entry in (2, 1, 0):
            here = flip(ctx, ORDER[entry]) * rows - entry * rows
            shift = jnp.where(key_place < (entry + 1) * rows, here, shift)
        query_place = lax.broadcasted_iota(jnp.int32, shape, 0) + ctx * rows
        scores = jnp.where(
            key_place + shift <= query_place, dot_rows(query, keys) * scale, -1e30
        )
        expd = jnp.exp(scores - jnp.max(scores, -1, keepdims=True))
        prob = expd * (1.0 / jnp.sum(expd, -1, keepdims=True))
        prob_low = prob.astype(LOW)
        attended = dot(prob_low, values).astype(LOW)
        at.late[head // per_piece, :, blocks_of(head % per_piece, HS)] = attended
        grad_prob = dot_rows(gate, values)
        delta = jnp.sum(grad_prob * prob, -1, keepdims=True)
        grad_scores = (prob * (grad_prob - delta)).astype(LOW)
        grad_key = dot(grad_scores.T, query) * scale
        grad_value = dot(prob_low.T, gate)
        at.pair_send[:, pl.ds(0, HS)] = grad_key[2 * rows :].astype(LOW)
        at.pair_send[:, pl.ds(HS, HS)] = grad_value[2 * rows :].astype(LOW)
        pair_beside(head).start()
        at.pair[:, pl.ds(0, HS)] = grad_key[: 2 * rows]
        at.pair[:, pl.ds(HS, HS)] = grad_value[: 2 * rows]
        late_block(3 * head)[...] = turn(dot(grad_scores, keys) * scale, True).astype(LOW)
        dense_load(head).wait()
        at.branch[...] += dot(attended, at.dense_held[...])

        @pl.when(head + 1 < heads)
        def _():
            dense_load(head + 1).start()

    def pair_halve(head):
        pair_beside(head).wait()

        @pl.when(ctx >= 2)
        def _():
            other = pl.ds(rows, rows)
            at.pair_send_low[...] = (
                at.pair[other] + at.pair_recv[head, other].astype(F32)
            ).astype(LOW)
            pair_across(head).start()

        at.pair_own[...] = at.pair[own_rows] + at.pair_recv[head, own_rows].astype(F32)

    def pair_finish(head):
        @pl.when(ctx < 2)
        def _():
            pair_across(head).wait_recv()
            at.pair_own[...] += at.pair_recv_low[head].astype(F32)

        @pl.when(ctx >= 2)
        def _():
            pair_across(head).wait_send()

        total = at.pair_own[...]
        late_block(3 * head + 1)[...] = turn(total[:, :HS], True).astype(LOW)
        late_block(3 * head + 2)[...] = total[:, HS:].astype(LOW)
        for number in range(3):
            at.small[pl.ds(3, 1), blocks_of(3 * head + number, HS)] = jnp.sum(
                late_block(3 * head + number)[...].astype(F32), 0, keepdims=True
            )

    def project_back(head):
        qkv_load(head).wait()
        at.grad_attn[...] += (
            dot_rows(late_block(3 * head)[...], at.qkv_held[:, :HS])
            + dot_rows(late_block(3 * head + 1)[...], at.qkv_held[:, HS : 2 * HS])
            + dot_rows(late_block(3 * head + 2)[...], at.qkv_held[:, 2 * HS :])
        )

        @pl.when(head + 1 < heads)
        def _():
            qkv_load(head + 1).start()

    def branch_send():
        at.sum_send[0] = at.branch[...].astype(LOW)
        tensor_copy(0, 0).start()

    def tensor_step(which, level):
        tensor_copy(which, level).wait()
        if level + 1 < len(tensor_bits):
            at.sum_send[level + 1] = (
                at.sum_send[level].astype(F32) + at.sum_recv[which, level].astype(F32)
            ).astype(LOW)
            tensor_copy(which, level + 1).start()
            return

        @pl.loop(0, rows // step_rows)
        def _(block):
            some = blocks_of(block, step_rows)
            total = at.sum_send[level, some].astype(F32) + at.sum_recv[which, level, some].astype(
                F32
            )
            if which == 0:
                total = (
                    at.hidden[some].astype(F32) + total + at.dense_bias[...] + at.down_bias[...]
                )
                at.mlp_in[some] = total.astype(LOW)
            else:
                at.attn_in[some] = (grad_of(some) + total).astype(LOW)

        row_result(which).start()

    def row_result(which):
        source = (at.mlp_in, at.attn_in)[which]
        target = (at.layer_out, at.input_grad)[which]
        return pltpu.make_async_copy(source, target, at.row_sem.at[which])

    def norm_back():
        @pl.loop(0, rows // step_rows)
        def _(block):
            some = blocks_of(block, step_rows)
            stats = at.stats[some]
            inv_std = stats[:, LANES // 2 : LANES // 2 + 1]
            normed = (at.hidden[some].astype(F32) - stats[:, :1]) * inv_std
            grad_attn, grad_mlp = at.grad_attn[some], at.grad_mlp[some]
            at.small[pl.ds(2, 1), pl.ds(0, model)] += jnp.sum(grad_of(some), 0, keepdims=True)
            for row, grad in enumerate((grad_attn, grad_mlp)):
                at.small[pl.ds(row, 1), pl.ds(0, model)] += jnp.sum(
                    grad * normed, 0, keepdims=True
                )
                at.small[pl.ds(row, 1), pl.ds(model, model)] += jnp.sum(grad, 0, keepdims=True)
            grad = grad_attn * at.attn_gain[...] + grad_mlp * at.mlp_gain[...]
            part = inv_std * (
                grad
                - jnp.mean(grad, -1, keepdims=True)
                - normed * jnp.mean(grad * normed, -1, keepdims=True)
            )
            at.sum_send[0, some] = part.astype(LOW)

        tensor_copy(1, 0).start()
        for number in range(2):
            small_half(number).start()

    def small_step(entry):
        if entry == 0:
            for number in range(2):
                small_half(number).wait()
                mine = blocks_of(flip(ctx, 2 * number), quarter)
                at.small_held[number] = at.small[:, mine] + at.small_recv[number]
            small_rest().start()
            return
        if entry == 1:
            small_rest().wait()
            at.line[0] = at.small_held[0] + at.small_recv[2]
        else:
            line_copy(entry - 2).wait()
            added = at.line[entry - 2] + at.line_recv[entry - 2]
            if line_steps[entry - 2][0] == "tensor":
                row = lax.broadcasted_iota(jnp.int32, added.shape, 0)
                added = jnp.where(row < 2, added, at.line[entry - 2])
            at.line[entry - 1] = added
        if entry - 1 < len(line_steps):
            line_copy(entry - 1).start()
            return
        for place in (2, 3, 1):
            small_spread(place).start()
        at.small_full[:, blocks_of(ctx, quarter)] = at.line[len(line_steps)]

    def small_finish():
        for place in (1, 2, 3):
            small_spread(place).wait()
        at.small_out[...] = at.small_full[...]

    lead = 3
    assert pairs in (4, 8)

    def places(base, *lags):
        return [
            [base + 2 * head + sum(lags[:stage]) for stage in range(5)] for head in range(heads)
        ]

    def in_time(jobs):
        for piece in range(attn_pieces):
            if jobs[(piece + 1) * per_piece - 1][2] > late + piece - lead:
                return False
        for block in range(3 * heads):
            if jobs[block // 3][4] > late + attn_pieces + block // per_piece - lead:
                return False
        return True

    jobs = next(pace for pace in (places(1, 5, 2, 2, 2), places(2, 1, 1, 1, 1)) if in_time(pace))
    project_at, forward_at, attend_at, halve_at, finish_at = jobs[0]
    feed_at = max(pairs - 4, 1)
    feed_end = feed_at + pairs - 1
    branch_at = max(attend_at + 2 * (heads - 1), feed_end) + 1
    back_at = max(finish_at + 2 * (heads - 1) + 2, branch_at + 4 * len(tensor_bits) + 1)
    total_steps = max(
        count + 5, back_at + 5 + len(line_steps), back_at + 4 * len(tensor_bits) + 1
    )

    def step(turn_number, carry):
        now = turn_number - 2

        def job(start, stride, times, act):
            index = now - start

            @pl.when((index >= 0) & (index < stride * times) & (index % stride == 0))
            def _():
                act(index // stride)

        multiply = now - 1

        @pl.when((multiply >= 0) & (multiply < count))
        def _():
            beside(multiply, 0).wait_recv()
            beside(multiply, 1).wait_recv()

            @pl.when(multiply >= RING)
            def _():
                pl.semaphore_wait(at.free.at[2], 1)

            @pl.when(multiply >= 3)
            def _():
                first(multiply - 3).wait_send()

            feed = multiply < late
            group = jnp.where(
                feed,
                jnp.where(multiply < pairs, 0, 1),
                jnp.where(multiply < late + attn_pieces, 0, 2),
            )
            at.first_send[multiply % 3] = dot(
                at.left[group, pl.ds(2 * width, 2 * width)], at.rows_all[multiply % RING]
            ).astype(LOW)
            first(multiply).start()
            at.held[multiply % 5] = dot(
                at.left[group, pl.ds(0, 2 * width)], at.rows_all[multiply % RING]
            )

        add = now - 3

        @pl.when((add >= 0) & (add < count))
        def _():
            first(add).wait_recv()

            @pl.when(add >= RING)
            def _():
                pl.semaphore_wait(at.free.at[3], 1)

            @pl.when(add >= 3)
            def _():
                second(add - 3).wait_send()

            lower = pl.ds(width, width)
            at.second_send[add % 3] = (
                at.held[add % 5, lower] + at.first_recv[add % RING, lower].astype(F32)
            ).astype(LOW)
            second(add).start()

        last = now - 5

        @pl.when((last >= 0) & (last < count))
        def _():
            second(last).wait_recv()

            @pl.when(last >= 2)
            def _():
                for_result(last - 2, lambda copy: copy.wait())

            upper = pl.ds(0, width)
            total = (
                at.held[last % 5, upper]
                + at.first_recv[last % RING, upper].astype(F32)
                + at.second_recv[last % RING].astype(F32)
            )
            flat = ((last < late) & (last >= pairs)) | (last >= late + attn_pieces)

            @pl.when(flat)
            def _():
                at.plain[last % 2] = total

            @pl.when(jnp.logical_not(flat))
            def _():
                at.turned[last % 2] = total.T

            for_result(last, lambda copy: copy.start())

            @pl.when(last < count - RING)
            def _():
                for number, bit in ((2, 1), (3, 2)):
                    pl.semaphore_signal(
                        at.free.at[number],
                        1,
                        device_id={"dp": flip(dp, bit)},
                        device_id_type=MESH,
                    )

        @pl.when((now >= 0) & (now < count))
        def _():
            across(now).wait_recv()
            beside(now, 1).start()

        sent = now - 1

        @pl.when((sent >= 0) & (sent < count))
        def _():
            across(sent).wait_send()
            beside(sent, 0).wait_send()
            beside(sent, 1).wait_send()

            @pl.when(sent < count - RING)
            def _():
                for number, bit in ((0, 2), (1, 1)):
                    pl.semaphore_signal(
                        at.free.at[number],
                        1,
                        device_id={"ctx": flip(ctx, bit)},
                        device_id_type=MESH,
                    )

        for pair, place in enumerate((-2, -2, -1, 0, 1, 2, 3, 4)[:pairs]):
            job(place, 1, 1, lambda _: activate(pair))
            if pair == 0:
                job(-2, 1, 1, lambda _: pass_on(0))
            if pair == 3:
                job(0, 1, 1, lambda _: low_left())
                job(min(0, project_at - 1), 1, 1, lambda _: attention_inputs())
        job(pairs - 2, 1, 1, lambda _: pass_on(1))
        job(pairs - 1, 1, 1, lambda _: hidden_left())
        job(feed_at, 1, pairs, feed_forward)
        job(project_at, 2, heads, project)
        job(forward_at, 2, heads, kv_forward)
        job(finish_at, 2, heads, pair_finish)
        job(halve_at, 2, heads, pair_halve)
        job(attend_at, 2, heads, attend)
        job(finish_at + 1, 2, heads, project_back)
        job(branch_at, 1, 1, lambda _: branch_send())
        for level in range(len(tensor_bits)):
            job(branch_at + 4 * (level + 1), 1, 1, lambda _: tensor_step(0, level))
        job(back_at, 1, 1, lambda _: norm_back())
        for level in range(len(tensor_bits)):
            job(back_at + 4 * (level + 1), 1, 1, lambda _: tensor_step(1, level))
        for entry in range(len(line_steps) + 2):
            job(back_at + 1 + entry, 1, 1, lambda _: small_step(entry))
        job(back_at + 3 + len(line_steps), 1, 1, lambda _: small_finish())

        @pl.when((now + lead >= late) & (now + lead < count))
        def _():
            start_piece(now + lead)

        return carry

    lax.fori_loop(0, total_steps + 2, step, 0)

    for place in (1, 2, 3):
        stats_copy(place).wait_send()
        for kind in range(2):
            for number in part_numbers(place):
                part_copy(kind, place, number).wait_send()
            if shared and place > 1:
                part_pass(kind, place).wait_send()

    @pl.loop(0, heads)
    def _(head):
        kv_beside(head, 0).wait_send()

        @pl.when(ctx < 2)
        def _():
            kv_across(head).wait_send()

        @pl.when(ctx >= 2)
        def _():
            kv_beside(head, 1).wait_send()

    @pl.loop(count - 3, count)
    def _(piece):
        first(piece).wait_send()
        second(piece).wait_send()

        @pl.when(piece >= count - 2)
        def _():
            for_result(piece, lambda copy: copy.wait())

    row_result(0).wait()
    row_result(1).wait()


def hand_on(cuts, *refs):
    whole = 6
    sources, small = refs[:whole], refs[whole]
    targets, refs = refs[whole + 1 : 2 * whole + 1], refs[2 * whole + 1 :]
    pieces, refs = refs[: len(cuts)], refs[len(cuts) :]
    held, sem = refs[:whole], refs[whole]

    def halves(ref):
        size = ref.shape[0] // 2
        return [ref.at[pl.ds(half * size, size)] for half in range(2)]

    copies = []
    for number in range(whole):
        parts = zip(halves(sources[number]), halves(held[number]), halves(targets[number]))
        for half, (source, middle, target) in enumerate(parts):
            copies.append(
                (
                    pltpu.make_async_copy(source, middle, sem.at[0, number, half]),
                    pltpu.make_async_copy(middle, target, sem.at[1, number, half]),
                )
            )
    for fetch, _ in copies:
        fetch.start()
    for piece, (row, low, high) in zip(pieces, cuts):
        piece[...] = small[row : row + 1, low:high]
    for fetch, put in copies:
        fetch.wait()
        put.start()
    for _, put in copies:
        put.wait()


def local(
    hidden_in,
    attn_norm_gain,
    attn_norm_bias,
    qkv_weight,
    qkv_bias,
    dense_weight,
    dense_bias,
    mlp_norm_gain,
    mlp_norm_bias,
    up_weight,
    up_bias,
    down_weight,
    down_bias,
    out_cotangent,
    subset_ids,
    subset_weights,
):
    seq_count, rows, model = hidden_in.shape
    heads = qkv_weight.shape[1] // (3 * HS)
    units = up_weight.shape[1]
    width = model // (lax.axis_size("dp") * lax.axis_size("ctx"))
    span = min(512, math.gcd(units, heads * HS, heads * 3 * HS))
    pairs = units // span
    late_count = heads * 4 * HS // span
    plan = types.SimpleNamespace(
        rows=rows, span=span, width=width, pairs=pairs, heads=heads, count=2 * pairs + late_count
    )
    tokens = rows * lax.axis_size("ctx")

    turns = np.arange(LANES) % (ROT // 2)
    freqs = np.float32(10000.0) ** -(turns.astype(np.float32) * np.float32(2.0 / ROT))

    bits = lax.axis_size("tensor").bit_length() - 1
    steps = 2 + bits
    small_width = max(2 * model, units, heads * 3 * HS)
    dma = pltpu.SemaphoreType.DMA
    vmem = pl.BlockSpec(memory_space=pltpu.VMEM)
    hbm = pl.BlockSpec(memory_space=pl.ANY)
    inputs = {
        "hidden": (hidden_in.reshape(rows, model), vmem),
        "cotangent": (out_cotangent.reshape(rows, model), vmem),
        "subset_ids": (subset_ids, vmem),
        "subset_weights": (subset_weights, pl.BlockSpec(memory_space=pltpu.SMEM)),
        "freqs": (jnp.asarray(freqs[None], F32), vmem),
        "attn_gain": (attn_norm_gain[None], vmem),
        "attn_bias": (attn_norm_bias[None], vmem),
        "mlp_gain": (mlp_norm_gain[None], vmem),
        "mlp_bias": (mlp_norm_bias[None], vmem),
        "dense_bias": (dense_bias[None], vmem),
        "down_bias": (down_bias[None], vmem),
        "qkv_bias": (qkv_bias[None], vmem),
        "up_bias": (up_bias[None], vmem),
        "qkv_weight": (qkv_weight, hbm),
        "dense_weight": (dense_weight, hbm),
        "up_weight": (up_weight, hbm),
        "down_weight": (down_weight, hbm),
    }
    outputs = {
        "layer_out": ((rows, model), LOW, hbm),
        "input_grad": ((rows, model), LOW, hbm),
        "small_out": ((8, small_width), F32, vmem),
        "down_out": ((units, width), F32, hbm),
        "up_out": ((width, units), F32, hbm),
        "dense_out": ((heads * HS, width), F32, hbm),
        "qkv_out": ((width, heads * 3 * HS), F32, hbm),
    }
    scratch = {
        "rows_all": pltpu.VMEM((RING, tokens, span), LOW),
        "first_send": pltpu.VMEM((3, 2 * width, span), LOW),
        "first_recv": pltpu.VMEM((RING, 2 * width, span), LOW),
        "second_send": pltpu.VMEM((3, width, span), LOW),
        "second_recv": pltpu.VMEM((RING, width, span), LOW),
        "held": pltpu.VMEM((5, 2 * width, span), F32),
        "plain": pltpu.VMEM((2, width, span), F32),
        "turned": pltpu.VMEM((2, span, width), F32),
        "left": pltpu.VMEM((3, 4 * width, tokens), LOW),
        "low_part": pltpu.VMEM((tokens, 4 * width), LOW),
        "hidden_part": pltpu.VMEM((tokens, 4 * width), LOW),
        "stats": pltpu.VMEM((tokens, LANES), F32),
        "stats_line": pltpu.VMEM((4, 16, rows), F32),
        "row_weight": pltpu.VMEM((rows, LANES), F32),
        "cosine": pltpu.VMEM((rows, LANES), F32),
        "sine_ahead": pltpu.VMEM((rows, LANES), F32),
        "sine_behind": pltpu.VMEM((rows, LANES), F32),
        "attn_in": pltpu.VMEM((rows, model), LOW),
        "mlp_in": pltpu.VMEM((rows, model), LOW),
        "low": pltpu.VMEM((rows, model), LOW),
        "up_held": pltpu.VMEM((model, span), LOW),
        "down_held": pltpu.VMEM((span, model), LOW),
        "qkv_held": pltpu.VMEM((model, 3 * HS), LOW),
        "gate_held": pltpu.VMEM((HS, model), LOW),
        "dense_held": pltpu.VMEM((HS, model), LOW),
        "query": pltpu.VMEM((heads, rows, HS), LOW),
        "gate": pltpu.VMEM((heads, rows, HS), LOW),
        "kv": pltpu.VMEM((heads, tokens, 2 * HS), LOW),
        "pair": pltpu.VMEM((2 * rows, 2 * HS), F32),
        "pair_own": pltpu.VMEM((rows, 2 * HS), F32),
        "pair_send": pltpu.VMEM((2 * rows, 2 * HS), LOW),
        "pair_recv": pltpu.VMEM((heads, 2 * rows, 2 * HS), LOW),
        "pair_send_low": pltpu.VMEM((rows, 2 * HS), LOW),
        "pair_recv_low": pltpu.VMEM((heads, rows, 2 * HS), LOW),
        "late": pltpu.VMEM((late_count, rows, span), LOW),
        "branch": pltpu.VMEM((rows, model), F32),
        "grad_mlp": pltpu.VMEM((rows, model), F32),
        "grad_attn": pltpu.VMEM((rows, model), F32),
        "sum_send": pltpu.VMEM((bits, rows, model), LOW),
        "sum_recv": pltpu.VMEM((2, bits, rows, model), LOW),
        "small": pltpu.VMEM((8, small_width), F32),
        "small_full": pltpu.VMEM((8, small_width), F32),
        "small_held": pltpu.VMEM((2, 8, small_width // 4), F32),
        "small_recv": pltpu.VMEM((3, 8, small_width // 4), F32),
        "line": pltpu.VMEM((steps + 1, 8, small_width // 4), F32),
        "line_recv": pltpu.VMEM((steps, 8, small_width // 4), F32),
        "load_sem": dma((5,)),
        "part_send": dma((2, 3, 4)),
        "part_recv": dma((2, 3, 4)),
        "pass_sems": dma((2, 2, 2)),
        "stats_send": dma((3,)),
        "stats_recv": dma((3,)),
        "ctx_send": dma((RING, 3)),
        "ctx_recv": dma((RING, 3)),
        "dp_send": dma((RING, 2)),
        "dp_recv": dma((RING, 2)),
        "out_sem": dma((2,)),
        "row_sem": dma((2,)),
        "kv_send": dma((heads, 5)),
        "kv_recv": dma((heads, 5)),
        "sum_sems": dma((2, 2, bits)),
        "small_sems": dma((2, 3 + steps)),
        "spread_sems": dma((2, 3)),
        "free": pltpu.SemaphoreType.REGULAR((4,)),
    }
    names = [*inputs, *outputs, *scratch]
    results = pl.pallas_call(
        functools.partial(layer_kernel, plan, names),
        out_shape=[jax.ShapeDtypeStruct(shape, kind) for shape, kind, _ in outputs.values()],
        in_specs=[spec for _, spec in inputs.values()],
        out_specs=[spec for _, _, spec in outputs.values()],
        scratch_shapes=list(scratch.values()),
        compiler_params=pltpu.CompilerParams(
            collective_id=0, has_side_effects=True, vmem_limit_bytes=63 << 20
        ),
        name="layer",
    )(*[array for array, _ in inputs.values()])
    cuts = [
        (0, 0, model),
        (0, model, 2 * model),
        (1, 0, model),
        (1, model, 2 * model),
        (2, 0, model),
        (2, 0, model),
        (3, 0, heads * 3 * HS),
        (4, 0, units),
    ]
    layer_out, input_grad, small, down_grad, up_grad, dense_grad, qkv_grad = results
    large = [layer_out, input_grad, down_grad, up_grad, dense_grad, qkv_grad]
    shapes = [jax.ShapeDtypeStruct(array.shape, array.dtype) for array in large]
    shapes += [jax.ShapeDtypeStruct((1, high - low), F32) for _, low, high in cuts]
    done = pl.pallas_call(
        functools.partial(hand_on, cuts),
        out_shape=shapes,
        in_specs=[hbm] * len(large) + [vmem],
        out_specs=[hbm] * len(large) + [vmem] * len(cuts),
        scratch_shapes=[pltpu.VMEM(array.shape, array.dtype) for array in large]
        + [dma((2, len(large), 2))],
        compiler_params=pltpu.CompilerParams(vmem_limit_bytes=60 << 20),
        name="hand_on",
    )(*large, small)
    layer_out, input_grad, down_grad, up_grad, dense_grad, qkv_grad = done[:6]
    vectors = [vector.reshape(-1) for vector in done[6:]]
    attn_gain, attn_bias, mlp_gain, mlp_bias, dense_sum, down_sum, qkv_sum, up_sum = vectors
    shape = (seq_count, rows, model)
    return (
        layer_out.reshape(shape),
        input_grad.reshape(shape),
        attn_gain,
        attn_bias,
        qkv_grad,
        qkv_sum,
        dense_grad,
        dense_sum,
        mlp_gain,
        mlp_bias,
        up_grad,
        up_sum,
        down_grad,
        down_sum,
    )


def solution(mesh):
    return jax.shard_map(
        local,
        mesh=mesh,
        in_specs=(
            P("dp", "ctx", None),
            P(),
            P(),
            P(None, "tensor"),
            P("tensor"),
            P("tensor", None),
            P(),
            P(),
            P(),
            P(None, "tensor"),
            P("tensor"),
            P("tensor", None),
            P(),
            P("dp", "ctx", None),
            P("dp", "ctx"),
            P(),
        ),
        out_specs=(
            P("dp", "ctx", None),
            P("dp", "ctx", None),
            P(),
            P(),
            P(("dp", "ctx"), "tensor"),
            P("tensor"),
            P("tensor", ("dp", "ctx")),
            P(),
            P(),
            P(),
            P(("dp", "ctx"), "tensor"),
            P("tensor"),
            P("tensor", ("dp", "ctx")),
            P(),
        ),
        check_vma=False,
    )
```
